256 devices in a mesh: seg: 4 (over x_lo, core), tile: 32 (over y, z), kind: 2 (over x_hi).
Axes of the slice: x: 4 (x_hi: 2, x_lo: 2; x = x_hi * 2 + x_lo), y: 4, z: 8, core: 2. Of those that a mesh axis runs over, the one named last changes fastest.
Arguments:
- displacement: float32 [3, 32, 256, 512], P(None, 'seg', 'tile'), may hold values from -0.15 to 0.15
- velocity: float32 [3, 32, 256, 512], P(None, 'seg', 'tile'), may hold values from -0.3 to 0.3
- load: float32 [3, 32, 256, 512], P(None, 'seg', 'tile'), may hold values from -0.3 to 0.3
- blend: float32 [32, 256, 512], P('seg', 'tile'), may hold values from 0 to 1, as said below
- classes: int32 [32, 256, 512], P('seg', 'tile'), may hold values from 0 to 3
- pd_table: float32 [4], replicated, may hold values from 0.1 to 1
- fem_table: float32 [4], replicated, may hold values from 0.3 to 3
Outputs:
- new_displacement: float32 [3, 32, 256, 512], P(None, 'seg', 'tile')
- new_velocity: float32 [3, 32, 256, 512], P(None, 'seg', 'tile')
The draws below stay inside these ranges and needn't reach their ends.
Inputs may be any that keep to these rules, and one draw needn't show every extreme that they name: `blend`: exactly 1 in a region around the impact point that spans the whole thickness, exactly 0 at cells more than 4 cells from that region in the plane, between 0 and 1 in the band between.
All inputs are finite; a program needn't handle non-finite values.
Results may differ from the reference program's by a relative error of at most 0.00002.
Values sent between devices are 32-bit elements; how exact they have to be, the bound alone decides.
No kernel may reach another device: no remote copies, remote signals or barrier semaphores. Data moves between devices by JAX's collectives and lax.ppermute only.
A program may use at most 64 MiB of HBM per device.

```python
import math
import jax
import jax.numpy as jnp
from jax import lax

NX = 512
HORIZON = 3
STEPS = 2
NCLASS = 4
RAMP = 4
NZ = 32
NY = 256


def draw_blend(key, part):
    base_key = jax.random.fold_in(key, 7)
    key_row, key_column, key_jitter = jax.random.split(base_key, 3)
    centre_row = jax.random.uniform(key_row, (), jnp.float32, 0.25 * NY, 0.75 * NY)
    centre_column = jax.random.uniform(key_column, (), jnp.float32, 0.25 * NX, 0.75 * NX)
    half_rows = NY / 8.0
    half_columns = NX / 8.0
    row_index = jnp.arange(NY, dtype=jnp.float32)[:, None]
    column_index = jnp.arange(NX, dtype=jnp.float32)[None, :]
    gap_rows = jnp.maximum(jnp.abs(row_index - centre_row) - half_rows, 0.0)
    gap_columns = jnp.maximum(jnp.abs(column_index - centre_column) - half_columns, 0.0)
    blend_ramp = jnp.clip(1.0 - jnp.maximum(gap_rows, gap_columns) / float(RAMP), 0.0, 1.0)
    blend_ramp = jnp.broadcast_to(blend_ramp[None, :, :], (NZ, NY, NX))
    jitter = jax.random.uniform(key_jitter, (NZ, NY, NX), jnp.float32, -0.5, 0.5)
    return blend_ramp + jitter * blend_ramp * (1.0 - blend_ramp)


def touch_ends(array, stream_key, low, largest):
    dims = array.shape
    spot = [jax.random.randint(jax.random.fold_in(stream_key, axis), (), 0, dims[axis]) for axis in range(len(dims))]
    array = array.at[tuple(spot)].set(low)
    longest = dims.index(max(dims))
    spot[longest] = (spot[longest] + 1) % dims[longest]
    return array.at[tuple(spot)].set(largest)


def levels(rng, shape, cuts, low, top_value):
    def one(position, blocks):
        draws = jax.random.uniform(jax.random.fold_in(jax.random.fold_in(rng, 6), position), (blocks,), jnp.float32, low / len(cuts), top_value / len(cuts))
        return jnp.repeat(jnp.exp(draws), shape[position] // blocks).reshape((-1,) + (1,) * (len(shape) - position - 1))

    factor_of = one(*cuts[0])
    for cut in cuts[1:]:
        factor_of = factor_of * one(*cut)
    return factor_of


def bell_draw(stream_key, dims, deviation, reach, cuts=(), kind=jnp.bfloat16):
    factor_of = levels(stream_key, dims, cuts, -0.22, 0.18) if cuts else 1.0
    drawn = jax.random.normal(stream_key, dims, jnp.float32) * deviation * factor_of
    return jnp.minimum(jnp.maximum(drawn, -reach), reach).astype(kind)


def setup_inputs(seed: int = 0) -> dict:
    key_list = jax.random.split(jax.random.key(seed), 8)
    return {
        "displacement": bell_draw(key_list[0], (3, NZ, NY, NX), 0.06, 0.15, ((1, 4), (2, 32)), jnp.float32),
        "velocity": bell_draw(key_list[1], (3, NZ, NY, NX), 0.05, 0.3, ((1, 4), (2, 32)), jnp.float32),
        "load": bell_draw(key_list[2], (3, NZ, NY, NX), 0.05, 0.3, ((1, 4), (2, 32)), jnp.float32),
        "blend": draw_blend(jax.random.fold_in(key_list[7], 71), 0),
        "classes": touch_ends(jax.random.randint(key_list[4], (NZ, NY, NX), 0, NCLASS), jax.random.fold_in(key_list[4], 1), 0, NCLASS - 1).astype(jnp.int32),
        "pd_table": jnp.clip(jnp.exp(jax.random.uniform(key_list[5], (NCLASS,), jnp.float32, math.log(0.1), math.log(1.0))), 0.1, 1.0),
        "fem_table": jnp.clip(jnp.exp(jax.random.uniform(key_list[6], (NCLASS,), jnp.float32, math.log(0.3), math.log(3.0))), 0.3, 3.0),
    }


def bond_offsets():
    result = []
    for first in range(-HORIZON, HORIZON + 1):
        for second in range(-HORIZON, HORIZON + 1):
            for third in range(-HORIZON, HORIZON + 1):
                norm_sq = first * first + second * second + third * third
                if 0 < norm_sq <= HORIZON * HORIZON:
                    result.append((first, second, third))
    return result

def lookup(table, classes):
    total = jnp.zeros(classes.shape, jnp.float32)
    for index in range(NCLASS):
        total = total + jnp.where(classes == index, table[index], 0.0)
    return total

def peri_force(padded, modulus, depth, depth_z, depth_y, width):
    center = padded[:, depth:depth + depth_z, depth:depth + depth_y, depth:depth + width]
    mod_center = modulus[depth:depth + depth_z, depth:depth + depth_y, depth:depth + width]
    totals = [jnp.zeros(center.shape[1:], jnp.float32) for comp in range(3)]
    for offset in bond_offsets():
        first, second, third = offset
        moved = padded[:, depth + first:depth + first + depth_z, depth + second:depth + second + depth_y, depth + third:depth + third + width]
        mod_moved = modulus[depth + first:depth + first + depth_z, depth + second:depth + second + depth_y, depth + third:depth + third + width]
        length_ref = math.sqrt(first * first + second * second + third * third)
        parts = [moved[comp] - center[comp] + float(offset[comp]) for comp in range(3)]
        square = parts[0] * parts[0] + parts[1] * parts[1] + parts[2] * parts[2]
        inverse = lax.rsqrt(square)
        factor = 0.5 * (mod_center + mod_moved) * ((square * inverse - length_ref) / length_ref) * inverse
        totals = [totals[comp] + factor * parts[comp] for comp in range(3)]
    return jnp.stack(totals)

def fem_force(padded, modulus, depth, depth_z, depth_y, width):
    low = depth - 1
    corners = [(p_bit, q_bit, r_bit) for p_bit in range(2) for q_bit in range(2) for r_bit in range(2)]
    values = {}
    for corner in corners:
        p_bit, q_bit, r_bit = corner
        values[corner] = padded[:, low + p_bit:low + p_bit + depth_z + 1, low + q_bit:low + q_bit + depth_y + 1, low + r_bit:low + r_bit + width + 1]
    elem_mod = modulus[low:low + depth_z + 1, low:low + depth_y + 1, low:low + width + 1]
    total_sum = values[corners[0]]
    for corner in corners[1:]:
        total_sum = total_sum + values[corner]
    force = jnp.zeros((3, depth_z, depth_y, width), jnp.float32)
    for corner in corners:
        p_bit, q_bit, r_bit = corner
        face_sum = values[1 - p_bit, q_bit, r_bit] + values[p_bit, 1 - q_bit, r_bit] + values[p_bit, q_bit, 1 - r_bit]
        far_sum = total_sum - values[corner] - face_sum
        element_force = elem_mod * (values[corner] / 3.0 - far_sum / 12.0)
        force = force - element_force[:, 1 - p_bit:1 - p_bit + depth_z, 1 - q_bit:1 - q_bit + depth_y, 1 - r_bit:1 - r_bit + width]
    return force

def reference(displacement, velocity, load, blend, classes, pd_table, fem_table):
    pd_mod = lookup(pd_table, classes) * blend
    fem_mod = lookup(fem_table, classes) * (1.0 - blend)
    depth = HORIZON
    pd_pad = jnp.pad(pd_mod, depth)
    fem_pad = jnp.pad(fem_mod, depth)
    depth_z, depth_y, width = (displacement.shape[1], displacement.shape[2], displacement.shape[3])
    for step in range(STEPS):
        padded = jnp.pad(displacement, ((0, 0), (depth, depth), (depth, depth), (depth, depth)))
        force = peri_force(padded, pd_pad, depth, depth_z, depth_y, width) + fem_force(padded, fem_pad, depth, depth_z, depth_y, width)
        velocity = velocity + 0.25 * (force + load)
        displacement = displacement + 0.01 * velocity
    return (displacement, velocity)
```

```python
import functools
import math

import jax
import jax.numpy as jnp
from jax import lax
from jax.experimental import pallas as pl
from jax.experimental.pallas import tpu as pltpu
from jax.sharding import PartitionSpec as P

H = 3
STEPS = 2
NCLASS = 4
NZ = 8
NY = 8
NT = 4
LANES = 128
F32 = jnp.float32

YRUN = NZ * H
ZRUN = 32
FRUN = 9


def offsets():
    out = []
    for dz in range(-H, H + 1):
        for dy in range(-H, H + 1):
            for dx in range(-H, H + 1):
                n = dz * dz + dy * dy + dx * dx
                if 0 < n <= H * H:
                    out.append((dz, dy, dx, n))
    return out


OFFSETS = offsets()


def vmem():
    return pl.BlockSpec(memory_space=pltpu.VMEM)


def smem():
    return pl.BlockSpec(memory_space=pltpu.SMEM)


def params():
    return pltpu.CompilerParams(vmem_limit_bytes=24 * 1024 * 1024)


def lanes(tile):
    return pl.ds(tile * LANES, LANES)


def pack_y(fields, up_ref, dn_ref):
    for index, load in enumerate(fields):
        for tile in range(NT):
            base = (index * NT + tile) * YRUN
            for z in range(NZ):
                rows = load(z, tile)
                up_ref[pl.ds(base + z * H, 8), :] = pltpu.roll(rows, H, 0)
                dn_ref[pl.ds(base + z * H, 8), :] = rows


def first_kernel(u_ref, blend_ref, cls_ref, pdt_ref, femt_ref, hm_ref, fem_ref, up_ref, dn_ref):
    for z in range(NZ):
        for tile in range(NT):
            blend = blend_ref[z, :, lanes(tile)]
            cls = cls_ref[z, :, lanes(tile)]
            pd = jnp.zeros_like(blend)
            fem = jnp.zeros_like(blend)
            for index in range(NCLASS):
                hit = cls == index
                pd = jnp.where(hit, pdt_ref[index], pd)
                fem = jnp.where(hit, femt_ref[index], fem)
            hm_ref[z, tile] = 0.5 * (pd * blend)
            fem_ref[z, tile] = fem * (1.0 - blend)
    loaders = [lambda z, t, c=c: u_ref[c, z, :, lanes(t)] for c in range(3)]
    loaders.append(lambda z, t: hm_ref[z, t])
    pack_y(loaders, up_ref, dn_ref)
    for tile in range(NT):
        base = 4 * NT * YRUN + tile * NZ
        for z in range(NZ):
            up_ref[pl.ds(base + z, 8), :] = pltpu.roll(fem_ref[z, tile], 1, 0)


def spread_kernel(nfields, *refs):
    if nfields == 5:
        u_ref, hm_ref, fem_ref, lo_ref, hi_ref, ext_ref, extm_ref, up_ref, dn_ref = refs
    else:
        u_ref, lo_ref, hi_ref, ext_ref, up_ref, dn_ref = refs
    sub = lax.broadcasted_iota(jnp.int32, (8, LANES), 0)
    nrun = min(nfields, 4)
    for index in range(nrun):
        for tile in range(NT):
            base = (index * NT + tile) * YRUN
            for z in range(NZ):
                rows = u_ref[index, z, :, lanes(tile)] if index < 3 else hm_ref[z, tile]
                turned = pltpu.roll(rows, H, 0)
                lo = lo_ref[pl.ds(base + z * H, 8), :]
                hi = pltpu.roll(hi_ref[pl.ds(base + z * H, 8), :], H, 0)
                dst = ext_ref.at[index, z, tile] if index < 3 else extm_ref.at[0, z, tile]
                dst[pl.ds(0, 8), :] = jnp.where(sub < H, lo, turned)
                dst[pl.ds(8, 8), :] = jnp.where(sub < H, turned, hi)
    if nfields == 5:
        for tile in range(NT):
            base = 4 * NT * YRUN + tile * NZ
            for z in range(NZ):
                turned = pltpu.roll(fem_ref[z, tile], H, 0)
                lo = pltpu.roll(lo_ref[pl.ds(base + z, 8), :], H - 1, 0)
                extm_ref[1, z, tile, pl.ds(0, 8), :] = jnp.where(sub < H, lo, turned)
                extm_ref[1, z, tile, pl.ds(8, 8), :] = turned
    for index in range(nrun):
        for tile in range(NT):
            base = (index * NT + tile) * ZRUN
            src = (lambda z: ext_ref.at[index, z, tile]) if index < 3 else (lambda z: extm_ref.at[0, z, tile])
            for ref, order in ((up_ref, (5, 6, 7)), (dn_ref, (2, 1, 0))):
                ref[pl.ds(base, 8), :] = src(order[0])[pl.ds(3, 8), :]
                for place, z in ((8, order[1]), (20, order[2])):
                    ref[pl.ds(base + place, 8), :] = src(z)[pl.ds(1, 8), :]
                    ref[pl.ds(base + place + 4, 8), :] = src(z)[pl.ds(5, 8), :]
    if nfields == 5:
        for tile in range(NT):
            base = 4 * NT * ZRUN + tile * FRUN
            up_ref[pl.ds(base, 8), :] = extm_ref[1, NZ - 1, tile, pl.ds(2, 8), :]
            up_ref[pl.ds(base + 1, 8), :] = extm_ref[1, NZ - 1, tile, pl.ds(3, 8), :]


def unpack_z(dst, index, tile, lo_ref, hi_ref, run):
    base = run * ZRUN
    for ref, order in ((lo_ref, (0, 1, 2)), (hi_ref, (13, 12, 11))):
        dst(order[0])[pl.ds(3, 8), :] = ref[pl.ds(base, 8), :]
        for place, z in ((8, order[1]), (20, order[2])):
            dst(z)[pl.ds(1, 8), :] = ref[pl.ds(base + place, 8), :]
            dst(z)[pl.ds(5, 8), :] = ref[pl.ds(base + place + 4, 8), :]


def fem_tile(sz, fe, p_ref, q_ref, tile, lane):
    edge = lane < 1

    def spread(c, z, row):
        here = sz[c, z, tile + 1, pl.ds(row, 8), :]
        after = sz[c, z, tile + 2, pl.ds(row, 8), :]
        nxt = pltpu.roll(jnp.where(edge, after, here), LANES - 1, 1)
        return here + nxt, nxt - here

    def modes(low, high):
        return (low[0] + high[0], low[1] + high[1], high[0] - low[0], high[1] - low[1])

    for c in range(3):
        before = None
        carried = None
        for n in range(-1, NZ + 1):
            level = [spread(c, n + H, row) for row in (2, 3, 4)]
            now = (modes(level[1], level[2]), modes(level[0], level[1]))
            if before is not None:
                sets = []
                for which, row in ((0, 3), (1, 2)):
                    e = fe[n, tile, pl.ds(row, 8), :]
                    e1, e2, e3 = e * (1.0 / 16.0), e * (1.0 / 24.0), e * (1.0 / 48.0)
                    lo, hi = before[which], now[which]
                    d_ss = e1 * (hi[0] - lo[0])
                    s_dx, d_dx = e1 * (lo[1] + hi[1]), e2 * (hi[1] - lo[1])
                    s_dy, d_dy = e1 * (lo[2] + hi[2]), e2 * (hi[2] - lo[2])
                    s_dd, d_dd = e2 * (lo[3] + hi[3]), e3 * (hi[3] - lo[3])
                    first = (-d_ss, s_dx - d_dx, s_dy - d_dy, s_dd - d_dd)
                    second = (d_ss, s_dx + d_dx, s_dy + d_dy, s_dd + d_dd)
                    sets.append((first, second))
                if carried is not None:
                    z = n - 1
                    a = [sets[0][0][m] + carried[0][m] for m in range(4)]
                    b = [sets[1][0][m] + carried[1][m] for m in range(4)]
                    x_s = (a[0] - a[2]) + (b[0] + b[2])
                    x_d = (a[1] - a[3]) + (b[1] + b[3])
                    p_ref[c, z, tile + 1] = x_s - x_d
                    q_ref[c, z, tile + 1] = x_s + x_d
                carried = (sets[0][1], sets[1][1])
            before = now


def bonds_of(sr, z):
    center = [sr[c, H, z + H, pl.ds(H, 8), :] for c in range(3)]
    hm = sr[3, H, z + H, pl.ds(H, 8), :]
    moved_center = {}
    for c in range(3):
        for d in range(-H, H + 1):
            moved_center[c, d] = center[c] - float(d) if d else center[c]
    acc = [[None] * 3 for _ in range(2)]
    for index, (dz, dy, dx, norm) in enumerate(OFFSETS):
        rows = pl.ds(H + dy, 8)
        off = (dz, dy, dx)
        rel = [sr[c, dx + H, z + (dz + H), rows, :] - moved_center[c, off[c]] for c in range(3)]
        m = hm + sr[3, dx + H, z + (dz + H), rows, :]
        square = rel[0] * rel[0] + rel[1] * rel[1] + rel[2] * rel[2]
        factor = m * (1.0 / math.sqrt(norm) - lax.rsqrt(square))
        way = index % 2
        for c in range(3):
            term = factor * rel[c]
            acc[way][c] = term if acc[way][c] is None else acc[way][c] + term
    return [acc[0][c] + acc[1][c] for c in range(3)]


def step_kernel(last, u_ref, v_ref, load_ref, ext_ref, extm_ref, ulo_ref, uhi_ref, mlo_ref, mhi_ref, *refs):
    if last:
        nu_ref, nv_ref, sz, fe, sr, p_ref, q_ref, f_ref = refs
    else:
        nu_ref, nv_ref, up_ref, dn_ref, sz, fe, sr, p_ref, q_ref, f_ref = refs
    lane = lax.broadcasted_iota(jnp.int32, (8, LANES), 1)
    sub = lax.broadcasted_iota(jnp.int32, (8, LANES), 0)
    zero = jnp.zeros((8, LANES), F32)

    for f in range(4):
        for z in range(NZ + 2 * H):
            for half in (0, 8):
                sz[f, z, 0, pl.ds(half, 8), :] = zero
                sz[f, z, NT + 1, pl.ds(half, 8), :] = zero
                if f == 3 and (z < H or z >= H + NZ):
                    for tile in range(NT):
                        sz[f, z, tile + 1, pl.ds(half, 8), :] = zero
        for tile in range(NT):
            for z in range(NZ):
                for half in (0, 8):
                    src = ext_ref.at[f] if f < 3 else extm_ref.at[0]
                    sz[f, z + H, tile + 1, pl.ds(half, 8), :] = src[z, tile, pl.ds(half, 8), :]
            run = f * NT + tile if f < 3 else tile
            unpack_z(lambda z: sz.at[f, z, tile + 1], f, tile, ulo_ref if f < 3 else mlo_ref, uhi_ref if f < 3 else mhi_ref, run)
    for tile in range(NT):
        base = NT * ZRUN + tile * FRUN
        fe[0, tile, pl.ds(2, 8), :] = mlo_ref[pl.ds(base, 8), :]
        fe[0, tile, pl.ds(3, 8), :] = mlo_ref[pl.ds(base + 1, 8), :]
        for z in range(NZ):
            for half in (0, 8):
                fe[z + 1, tile, pl.ds(half, 8), :] = extm_ref[1, z, tile, pl.ds(half, 8), :]

    def fem_loop(tile, carry):
        fem_tile(sz, fe, p_ref, q_ref, tile, lane)
        return carry

    for c in range(3):
        for z in range(NZ):
            q_ref[c, z, 0] = zero
    lax.fori_loop(0, NT, fem_loop, 0)

    def pd_loop(tile, carry):
        most = zero
        for z in range(NZ + 2 * H):
            for row, keep in ((0, None), (6, None)):
                mine = sz[3, z, tile + 1, pl.ds(row, 8), :]
                left = jnp.where(lane >= LANES - H, sz[3, z, tile, pl.ds(row, 8), :], 0.0)
                right = jnp.where(lane < H, sz[3, z, tile + 2, pl.ds(row, 8), :], 0.0)
                most = jnp.maximum(most, jnp.maximum(mine, jnp.maximum(left, right)))
        active = jnp.max(most) > 0.0

        @pl.when(active)
        def _():
            def build(z, c2):
                for f in range(4):
                    for half in (0, 8):
                        left = sz[f, z, tile, pl.ds(half, 8), :]
                        here = sz[f, z, tile + 1, pl.ds(half, 8), :]
                        right = sz[f, z, tile + 2, pl.ds(half, 8), :]
                        sr[f, H, z, pl.ds(half, 8), :] = here
                        for d in range(1, H + 1):
                            sr[f, H + d, z, pl.ds(half, 8), :] = pltpu.roll(jnp.where(lane < d, right, here), LANES - d, 1)
                            sr[f, H - d, z, pl.ds(half, 8), :] = pltpu.roll(jnp.where(lane >= LANES - d, left, here), d, 1)
                return c2

            lax.fori_loop(0, NZ + 2 * H, build, 0)

            def pd_z(z, c2):
                total = bonds_of(sr, z)
                for c in range(3):
                    f_ref[c, z, tile] = total[c]
                return c2

            lax.fori_loop(0, NZ, pd_z, 0)

        @pl.when(jnp.logical_not(active))
        def _():
            for c in range(3):
                for z in range(NZ):
                    f_ref[c, z, tile] = zero

        return carry

    lax.fori_loop(0, NT, pd_loop, 0)

    for c in range(3):
        for z in range(NZ):
            for tile in range(NT):
                here = q_ref[c, z, tile + 1]
                left = q_ref[c, z, tile]
                moved = pltpu.roll(jnp.where(lane == LANES - 1, left, here), 1, 1)
                force = f_ref[c, z, tile] - (p_ref[c, z, tile + 1] + moved)
                where = (c, z, slice(None), lanes(tile))
                v = v_ref[where] + 0.25 * (force + load_ref[where])
                u = u_ref[where] + 0.01 * v
                nv_ref[where] = v
                nu_ref[where] = u
    if not last:
        pack_y([lambda z, t, c=c: nu_ref[c, z, :, lanes(t)] for c in range(3)], up_ref, dn_ref)


def shape(*dims):
    return jax.ShapeDtypeStruct(dims, F32)


def send(axis, up, down):
    count = lax.axis_size(axis)
    pairs = [(i, i + 1) for i in range(count - 1)]
    low = lax.ppermute(up, axis, pairs)
    high = lax.ppermute(down, axis, [(b, a) for a, b in pairs])
    return low, high


UROWS = 3 * NT * ZRUN


def body(displacement, velocity, load, blend, classes, pd_table, fem_table):
    whole = shape(3, NZ, NY, NT * LANES)
    hm, fem, up, dn = pl.pallas_call(
        first_kernel,
        out_shape=(shape(NZ, NT, 8, LANES), shape(NZ, NT, 8, LANES), shape(4 * NT * YRUN + NT * NZ + 8, LANES), shape(4 * NT * YRUN + 8, LANES)),
        in_specs=[vmem()] * 3 + [smem()] * 2,
        out_specs=(vmem(),) * 4,
        compiler_params=params(),
        name="moduli",
    )(displacement, blend, classes, pd_table, fem_table)
    lo, hi = send("tile", up, dn)
    ext, extm, up, dn = pl.pallas_call(
        functools.partial(spread_kernel, 5),
        out_shape=(
            shape(3, NZ, NT, 16, LANES),
            shape(2, NZ, NT, 16, LANES),
            shape(4 * NT * ZRUN + 40, LANES),
            shape(4 * NT * ZRUN, LANES),
        ),
        in_specs=[vmem()] * 5,
        out_specs=(vmem(),) * 4,
        compiler_params=params(),
        name="spread_first",
    )(displacement, hm, fem, lo, hi)
    lo, hi = send("seg", up, dn)
    mlo, mhi = lo[UROWS:], hi[UROWS:]

    def step(last, u, v, ext, ulo, uhi):
        outs = [whole, whole]
        if not last:
            outs += [shape(3 * NT * YRUN + 8, LANES)] * 2
        return pl.pallas_call(
            functools.partial(step_kernel, last),
            out_shape=tuple(outs),
            in_specs=[vmem()] * 9,
            out_specs=(vmem(),) * len(outs),
            scratch_shapes=[
                pltpu.VMEM((4, NZ + 2 * H, NT + 2, 16, LANES), F32),
                pltpu.VMEM((NZ + 1, NT, 16, LANES), F32),
                pltpu.VMEM((4, 2 * H + 1, NZ + 2 * H, 16, LANES), F32),
                pltpu.VMEM((3, NZ, NT + 1, 8, LANES), F32),
                pltpu.VMEM((3, NZ, NT + 1, 8, LANES), F32),
                pltpu.VMEM((3, NZ, NT, 8, LANES), F32),
            ],
            compiler_params=params(),
            name="step_last" if last else "step_first",
        )(u, v, load, ext, extm, ulo, uhi, mlo, mhi)

    u, v, up, dn = step(False, displacement, velocity, ext, lo, hi)
    lo, hi = send("tile", up, dn)
    ext, up, dn = pl.pallas_call(
        functools.partial(spread_kernel, 3),
        out_shape=(shape(3, NZ, NT, 16, LANES), shape(UROWS, LANES), shape(UROWS, LANES)),
        in_specs=[vmem()] * 3,
        out_specs=(vmem(),) * 3,
        compiler_params=params(),
        name="spread_second",
    )(u, lo, hi)
    lo, hi = send("seg", up, dn)
    u, v = step(True, u, v, ext, lo, hi)
    return u, v


def solution(mesh):
    cells = P(None, "seg", "tile", None)
    plane = P("seg", "tile", None)
    return jax.shard_map(
        body,
        mesh=mesh,
        in_specs=(cells, cells, cells, plane, plane, P(), P()),
        out_specs=(cells, cells),
        check_vma=False,
    )
```

```python
import functools
import math

import jax
import jax.numpy as jnp
from jax import lax
from jax.experimental import pallas as pl
from jax.experimental.pallas import tpu as pltpu
from jax.sharding import PartitionSpec as P

H = 3
STEPS = 2
NCLASS = 4
NZ = 8
NY = 8
NT = 4
LANES = 128
F32 = jnp.float32

YRUN = NZ * H
ZRUN = 32
FRUN = 9


def offsets():
    out = []
    for dz in range(-H, H + 1):
        for dy in range(-H, H + 1):
            for dx in range(-H, H + 1):
                n = dz * dz + dy * dy + dx * dx
                if 0 < n <= H * H:
                    out.append((dz, dy, dx, n))
    return out


OFFSETS = offsets()


def vmem():
    return pl.BlockSpec(memory_space=pltpu.VMEM)


def hbm():
    return pl.BlockSpec(memory_space=pltpu.MemorySpace.HBM)


def smem():
    return pl.BlockSpec(memory_space=pltpu.SMEM)


def params():
    return pltpu.CompilerParams(vmem_limit_bytes=24 * 1024 * 1024)


def lanes(tile):
    return pl.ds(tile * LANES, LANES)


def even_mask(par_ref, index):
    return jnp.full((8, LANES), par_ref[index], jnp.int32) == 0


def pack_y(fields, even, a_ref, b_ref):
    for index, load in enumerate(fields):
        for tile in range(NT):
            base = (index * NT + tile) * YRUN
            for z in range(NZ):
                rows = load(z, tile)
                up = pltpu.roll(rows, H, 0)
                a_ref[pl.ds(base + z * H, 8), :] = jnp.where(even, up, rows)
                b_ref[pl.ds(base + z * H, 8), :] = jnp.where(even, rows, up)


def first_kernel(par_ref, u_hbm, blend_hbm, cls_hbm, pdt_ref, femt_ref, hm_ref, fem_ref, a_ref, b_ref, u_ref, blend_ref, cls_ref, sem):
    copies = [pltpu.make_async_copy(blend_hbm, blend_ref, sem.at[3]), pltpu.make_async_copy(cls_hbm, cls_ref, sem.at[4])]
    moves = [pltpu.make_async_copy(u_hbm.at[c], u_ref.at[c], sem.at[c]) for c in range(3)]
    for copy in copies + moves:
        copy.start()
    for copy in copies:
        copy.wait()
    even = even_mask(par_ref, 0)
    for z in range(NZ):
        for tile in range(NT):
            blend = blend_ref[z, :, lanes(tile)]
            cls = cls_ref[z, :, lanes(tile)]
            pd = jnp.zeros_like(blend)
            fem = jnp.zeros_like(blend)
            for index in range(NCLASS):
                hit = cls == index
                pd = jnp.where(hit, pdt_ref[index], pd)
                fem = jnp.where(hit, femt_ref[index], fem)
            hm_ref[z, tile] = 0.5 * (pd * blend)
            fem_ref[z, tile] = fem * (1.0 - blend)
    for copy in moves:
        copy.wait()
    loaders = [lambda z, t, c=c: u_ref[c, z, :, lanes(t)] for c in range(3)]
    loaders.append(lambda z, t: hm_ref[z, t])
    pack_y(loaders, even, a_ref, b_ref)
    for tile in range(NT):
        base = 4 * NT * YRUN + tile * NZ
        for z in range(NZ):
            up = pltpu.roll(fem_ref[z, tile], 1, 0)
            a_ref[pl.ds(base + z, 8), :] = up
            b_ref[pl.ds(base + z, 8), :] = up


def spread_kernel(nfields, par_ref, *refs):
    if nfields == 5:
        u_ref, hm_ref, fem_ref, ra_ref, rb_ref, ext_ref, extm_ref, a_ref, b_ref = refs
    else:
        u_ref, ra_ref, rb_ref, ext_ref, a_ref, b_ref = refs
    sub = lax.broadcasted_iota(jnp.int32, (8, LANES), 0)
    even = even_mask(par_ref, 0)
    even_z = even_mask(par_ref, 1)
    nrun = min(nfields, 4)
    for index in range(nrun):
        for tile in range(NT):
            base = (index * NT + tile) * YRUN
            for z in range(NZ):
                rows = u_ref[index, z, :, lanes(tile)] if index < 3 else hm_ref[z, tile]
                turned = pltpu.roll(rows, H, 0)
                got_a = ra_ref[pl.ds(base + z * H, 8), :]
                got_b = rb_ref[pl.ds(base + z * H, 8), :]
                lo = jnp.where(even, got_b, got_a)
                hi = pltpu.roll(jnp.where(even, got_a, got_b), H, 0)
                dst = ext_ref.at[index, z, tile] if index < 3 else extm_ref.at[0, z, tile]
                dst[pl.ds(0, 8), :] = jnp.where(sub < H, lo, turned)
                dst[pl.ds(8, 8), :] = jnp.where(sub < H, turned, hi)
    if nfields == 5:
        for tile in range(NT):
            base = 4 * NT * YRUN + tile * NZ
            for z in range(NZ):
                turned = pltpu.roll(fem_ref[z, tile], H, 0)
                lo = jnp.where(even, rb_ref[pl.ds(base + z, 8), :], ra_ref[pl.ds(base + z, 8), :])
                lo = pltpu.roll(lo, H - 1, 0)
                extm_ref[1, z, tile, pl.ds(0, 8), :] = jnp.where(sub < H, lo, turned)
                extm_ref[1, z, tile, pl.ds(8, 8), :] = turned

    def put(row, up, down):
        a_ref[pl.ds(row, 8), :] = jnp.where(even_z, up, down)
        b_ref[pl.ds(row, 8), :] = jnp.where(even_z, down, up)

    for index in range(nrun):
        for tile in range(NT):
            base = (index * NT + tile) * ZRUN
            src = (lambda z: ext_ref.at[index, z, tile]) if index < 3 else (lambda z: extm_ref.at[0, z, tile])
            put(base, src(5)[pl.ds(3, 8), :], src(2)[pl.ds(3, 8), :])
            for place, zu, zd in ((8, 6, 1), (20, 7, 0)):
                put(base + place, src(zu)[pl.ds(1, 8), :], src(zd)[pl.ds(1, 8), :])
                put(base + place + 4, src(zu)[pl.ds(5, 8), :], src(zd)[pl.ds(5, 8), :])
    if nfields == 5:
        for tile in range(NT):
            base = 4 * NT * ZRUN + tile * FRUN
            for row in (0, 1):
                up = extm_ref[1, NZ - 1, tile, pl.ds(2 + row, 8), :]
                put(base + row, up, up)


def unpack_z(dst, even_z, ra_ref, rb_ref, run):
    base = run * ZRUN

    def get(z_lo, z_hi, row, place):
        got_a = ra_ref[pl.ds(base + place, 8), :]
        got_b = rb_ref[pl.ds(base + place, 8), :]
        dst(z_lo)[pl.ds(row, 8), :] = jnp.where(even_z, got_b, got_a)
        dst(z_hi)[pl.ds(row, 8), :] = jnp.where(even_z, got_a, got_b)

    get(0, 13, 3, 0)
    for place, z_lo, z_hi in ((8, 1, 12), (20, 2, 11)):
        get(z_lo, z_hi, 1, place)
        get(z_lo, z_hi, 5, place + 4)


def fem_tile(sz, fe, p_ref, q_ref, tile, lane):
    edge = lane < 1

    def spread(c, z, row):
        here = sz[c, z, tile + 1, pl.ds(row, 8), :]
        after = sz[c, z, tile + 2, pl.ds(row, 8), :]
        nxt = pltpu.roll(jnp.where(edge, after, here), LANES - 1, 1)
        return here + nxt, nxt - here

    def modes(low, high):
        return (low[0] + high[0], low[1] + high[1], high[0] - low[0], high[1] - low[1])

    for c in range(3):
        before = None
        carried = None
        for n in range(-1, NZ + 1):
            level = [spread(c, n + H, row) for row in (2, 3, 4)]
            now = (modes(level[1], level[2]), modes(level[0], level[1]))
            if before is not None:
                sets = []
                for which, row in ((0, 3), (1, 2)):
                    e = fe[n, tile, pl.ds(row, 8), :]
                    e1, e2, e3 = e * (1.0 / 16.0), e * (1.0 / 24.0), e * (1.0 / 48.0)
                    lo, hi = before[which], now[which]
                    d_ss = e1 * (hi[0] - lo[0])
                    s_dx, d_dx = e1 * (lo[1] + hi[1]), e2 * (hi[1] - lo[1])
                    s_dy, d_dy = e1 * (lo[2] + hi[2]), e2 * (hi[2] - lo[2])
                    s_dd, d_dd = e2 * (lo[3] + hi[3]), e3 * (hi[3] - lo[3])
                    first = (-d_ss, s_dx - d_dx, s_dy - d_dy, s_dd - d_dd)
                    second = (d_ss, s_dx + d_dx, s_dy + d_dy, s_dd + d_dd)
                    sets.append((first, second))
                if carried is not None:
                    z = n - 1
                    a = [sets[0][0][m] + carried[0][m] for m in range(4)]
                    b = [sets[1][0][m] + carried[1][m] for m in range(4)]
                    x_s = (a[0] - a[2]) + (b[0] + b[2])
                    x_d = (a[1] - a[3]) + (b[1] + b[3])
                    p_ref[c, z, tile + 1] = x_s - x_d
                    q_ref[c, z, tile + 1] = x_s + x_d
                carried = (sets[0][1], sets[1][1])
            before = now


def bonds_of(sr, z):
    center = [sr[c, H, z + H, pl.ds(H, 8), :] for c in range(3)]
    hm = sr[3, H, z + H, pl.ds(H, 8), :]
    moved_center = {}
    for c in range(3):
        for d in range(-H, H + 1):
            moved_center[c, d] = center[c] - float(d) if d else center[c]
    acc = [[None] * 3 for _ in range(2)]
    for index, (dz, dy, dx, norm) in enumerate(OFFSETS):
        rows = pl.ds(H + dy, 8)
        off = (dz, dy, dx)
        rel = [sr[c, dx + H, z + (dz + H), rows, :] - moved_center[c, off[c]] for c in range(3)]
        m = hm + sr[3, dx + H, z + (dz + H), rows, :]
        square = rel[0] * rel[0] + rel[1] * rel[1] + rel[2] * rel[2]
        factor = m * (1.0 / math.sqrt(norm) - lax.rsqrt(square))
        way = index % 2
        for c in range(3):
            term = factor * rel[c]
            acc[way][c] = term if acc[way][c] is None else acc[way][c] + term
    return [acc[0][c] + acc[1][c] for c in range(3)]


def step_kernel(last, par_ref, u_ref, v_hbm, load_hbm, ext_ref, extm_ref, ura_ref, urb_ref, mra_ref, mrb_ref, *refs):
    if last:
        nu_ref, nv_ref, sz, fe, sr, p_ref, q_ref, f_ref, v_ref, load_ref, sem = refs
    else:
        nu_ref, nv_ref, a_ref, b_ref, sz, fe, sr, p_ref, q_ref, f_ref, v_ref, load_ref, sem = refs
    copies = [pltpu.make_async_copy(v_hbm, v_ref, sem.at[0]), pltpu.make_async_copy(load_hbm, load_ref, sem.at[1])]
    for copy in copies:
        copy.start()
    even = even_mask(par_ref, 0)
    even_z = even_mask(par_ref, 1)
    lane = lax.broadcasted_iota(jnp.int32, (8, LANES), 1)
    zero = jnp.zeros((8, LANES), F32)

    for f in range(4):
        for z in range(NZ + 2 * H):
            for half in (0, 8):
                sz[f, z, 0, pl.ds(half, 8), :] = zero
                sz[f, z, NT + 1, pl.ds(half, 8), :] = zero
                if f == 3 and (z < H or z >= H + NZ):
                    for tile in range(NT):
                        sz[f, z, tile + 1, pl.ds(half, 8), :] = zero
        for tile in range(NT):
            for z in range(NZ):
                for half in (0, 8):
                    src = ext_ref.at[f] if f < 3 else extm_ref.at[0]
                    sz[f, z + H, tile + 1, pl.ds(half, 8), :] = src[z, tile, pl.ds(half, 8), :]
            ra, rb = (ura_ref, urb_ref) if f < 3 else (mra_ref, mrb_ref)
            unpack_z(lambda z: sz.at[f, z, tile + 1], even_z, ra, rb, f * NT + tile)
    for tile in range(NT):
        base = 4 * NT * ZRUN + tile * FRUN
        for row in (0, 1):
            fe[0, tile, pl.ds(2 + row, 8), :] = jnp.where(
                even_z, mrb_ref[pl.ds(base + row, 8), :], mra_ref[pl.ds(base + row, 8), :]
            )
        for z in range(NZ):
            for half in (0, 8):
                fe[z + 1, tile, pl.ds(half, 8), :] = extm_ref[1, z, tile, pl.ds(half, 8), :]

    def fem_loop(tile, carry):
        fem_tile(sz, fe, p_ref, q_ref, tile, lane)
        return carry

    for c in range(3):
        for z in range(NZ):
            q_ref[c, z, 0] = zero
    lax.fori_loop(0, NT, fem_loop, 0)

    def pd_loop(tile, carry):
        most = zero
        for z in range(NZ + 2 * H):
            for row, keep in ((0, None), (6, None)):
                mine = sz[3, z, tile + 1, pl.ds(row, 8), :]
                left = jnp.where(lane >= LANES - H, sz[3, z, tile, pl.ds(row, 8), :], 0.0)
                right = jnp.where(lane < H, sz[3, z, tile + 2, pl.ds(row, 8), :], 0.0)
                most = jnp.maximum(most, jnp.maximum(mine, jnp.maximum(left, right)))
        active = jnp.max(most) > 0.0

        @pl.when(active)
        def _():
            def build(z, c2):
                for f in range(4):
                    for half in (0, 8):
                        left = sz[f, z, tile, pl.ds(half, 8), :]
                        here = sz[f, z, tile + 1, pl.ds(half, 8), :]
                        right = sz[f, z, tile + 2, pl.ds(half, 8), :]
                        sr[f, H, z, pl.ds(half, 8), :] = here
                        for d in range(1, H + 1):
                            sr[f, H + d, z, pl.ds(half, 8), :] = pltpu.roll(jnp.where(lane < d, right, here), LANES - d, 1)
                            sr[f, H - d, z, pl.ds(half, 8), :] = pltpu.roll(jnp.where(lane >= LANES - d, left, here), d, 1)
                return c2

            lax.fori_loop(0, NZ + 2 * H, build, 0)

            def pd_z(z, c2):
                total = bonds_of(sr, z)
                for c in range(3):
                    f_ref[c, z, tile] = total[c]
                return c2

            lax.fori_loop(0, NZ, pd_z, 0)

        @pl.when(jnp.logical_not(active))
        def _():
            for c in range(3):
                for z in range(NZ):
                    f_ref[c, z, tile] = zero

        return carry

    lax.fori_loop(0, NT, pd_loop, 0)

    for copy in copies:
        copy.wait()
    for c in range(3):
        for z in range(NZ):
            for tile in range(NT):
                here = q_ref[c, z, tile + 1]
                left = q_ref[c, z, tile]
                moved = pltpu.roll(jnp.where(lane == LANES - 1, left, here), 1, 1)
                force = f_ref[c, z, tile] - (p_ref[c, z, tile + 1] + moved)
                where = (c, z, slice(None), lanes(tile))
                v = v_ref[where] + 0.25 * (force + load_ref[where])
                u = u_ref[where] + 0.01 * v
                nv_ref[where] = v
                nu_ref[where] = u
    if not last:
        pack_y([lambda z, t, c=c: nu_ref[c, z, :, lanes(t)] for c in range(3)], even, a_ref, b_ref)


def shape(*dims):
    return jax.ShapeDtypeStruct(dims, F32)


def swap(axis, a, b):
    count = lax.axis_size(axis)

    def pairs(first):
        out = []
        for i in range(first, count - 1, 2):
            out += [(i, i + 1), (i + 1, i)]
        return out

    return lax.ppermute(a, axis, pairs(0)), lax.ppermute(b, axis, pairs(1))


YROWS = 3 * NT * YRUN + 8
ZROWS = 3 * NT * ZRUN
YROWS5 = 4 * NT * YRUN + NT * NZ + 8
ZROWS5 = 4 * NT * ZRUN + 40


def body(displacement, velocity, load, blend, classes, pd_table, fem_table):
    whole = shape(3, NZ, NY, NT * LANES)
    block = (3, NZ, NY, NT * LANES)
    par = jnp.stack([lax.axis_index("tile") % 2, lax.axis_index("seg") % 2]).astype(jnp.int32)
    hm, fem, a, b = pl.pallas_call(
        first_kernel,
        out_shape=(shape(NZ, NT, 8, LANES), shape(NZ, NT, 8, LANES), shape(YROWS5, LANES), shape(YROWS5, LANES)),
        in_specs=[smem()] + [hbm()] * 3 + [smem()] * 2,
        out_specs=(vmem(),) * 4,
        scratch_shapes=[
            pltpu.VMEM(block, F32),
            pltpu.VMEM(block[1:], F32),
            pltpu.VMEM(block[1:], jnp.int32),
            pltpu.SemaphoreType.DMA((5,)),
        ],
        compiler_params=params(),
        name="moduli",
    )(par, displacement, blend, classes, pd_table, fem_table)
    ra, rb = swap("tile", a, b)
    ext, extm, a, b = pl.pallas_call(
        functools.partial(spread_kernel, 5),
        out_shape=(
            shape(3, NZ, NT, 16, LANES),
            shape(2, NZ, NT, 16, LANES),
            shape(ZROWS5, LANES),
            shape(ZROWS5, LANES),
        ),
        in_specs=[smem()] + [vmem()] * 5,
        out_specs=(vmem(),) * 4,
        compiler_params=params(),
        name="spread_first",
    )(par, displacement, hm, fem, ra, rb)
    mra, mrb = swap("seg", a, b)

    def step(last, u, v, ext, ra, rb):
        outs = [whole, whole]
        if not last:
            outs += [shape(YROWS, LANES)] * 2
        return pl.pallas_call(
            functools.partial(step_kernel, last),
            out_shape=tuple(outs),
            in_specs=[smem(), vmem()] + [hbm()] * 2 + [vmem()] * 6,
            out_specs=(vmem(),) * len(outs),
            scratch_shapes=[
                pltpu.VMEM((4, NZ + 2 * H, NT + 2, 16, LANES), F32),
                pltpu.VMEM((NZ + 1, NT, 16, LANES), F32),
                pltpu.VMEM((4, 2 * H + 1, NZ + 2 * H, 16, LANES), F32),
                pltpu.VMEM((3, NZ, NT + 1, 8, LANES), F32),
                pltpu.VMEM((3, NZ, NT + 1, 8, LANES), F32),
                pltpu.VMEM((3, NZ, NT, 8, LANES), F32),
                pltpu.VMEM(block, F32),
                pltpu.VMEM(block, F32),
                pltpu.SemaphoreType.DMA((2,)),
            ],
            compiler_params=params(),
            name="step_last" if last else "step_first",
        )(par, u, v, load, ext, extm, ra, rb, mra, mrb)

    u, v, a, b = step(False, displacement, velocity, ext, mra, mrb)
    ra, rb = swap("tile", a, b)
    ext, a, b = pl.pallas_call(
        functools.partial(spread_kernel, 3),
        out_shape=(shape(3, NZ, NT, 16, LANES), shape(ZROWS, LANES), shape(ZROWS, LANES)),
        in_specs=[smem()] + [vmem()] * 3,
        out_specs=(vmem(),) * 3,
        compiler_params=params(),
        name="spread_second",
    )(par, u, ra, rb)
    ra, rb = swap("seg", a, b)
    u, v = step(True, u, v, ext, ra, rb)
    return u, v


def solution(mesh):
    cells = P(None, "seg", "tile", None)
    plane = P("seg", "tile", None)
    return jax.shard_map(
        body,
        mesh=mesh,
        in_specs=(cells, cells, cells, plane, plane, P(), P()),
        out_specs=(cells, cells),
        check_vma=False,
    )
```

```python
import functools
import math

import jax
import jax.numpy as jnp
from jax import lax
from jax.experimental import pallas as pl
from jax.experimental.pallas import tpu as pltpu
from jax.sharding import PartitionSpec as P

H = 3
STEPS = 2
NCLASS = 4
NZ = 8
NY = 8
NT = 4
LANES = 128
F32 = jnp.float32

YRUN = NZ * H
ZRUN = 32
FRUN = 9


def offsets():
    out = []
    for dz in range(-H, H + 1):
        for dy in range(-H, H + 1):
            for dx in range(-H, H + 1):
                n = dz * dz + dy * dy + dx * dx
                if 0 < n <= H * H:
                    out.append((dz, dy, dx, n))
    return out


OFFSETS = offsets()
FLAT = {dz: [o for o in OFFSETS if o[0] == dz and o[1] == 0] for dz in range(-H, H + 1)}
TILTED = {dz: [o for o in OFFSETS if o[0] == dz and o[1] != 0] for dz in range(-H, H + 1)}


def vmem():
    return pl.BlockSpec(memory_space=pltpu.VMEM)


def anywhere():
    return pl.BlockSpec(memory_space=pl.ANY)


def smem():
    return pl.BlockSpec(memory_space=pltpu.SMEM)


def params():
    return pltpu.CompilerParams(vmem_limit_bytes=24 * 1024 * 1024)


def lanes(tile):
    return pl.ds(tile * LANES, LANES)


def even_mask(par_ref, index):
    return jnp.full((8, LANES), par_ref[index], jnp.int32) == 0


def pack_y(fields, even, a_ref, b_ref):
    for index, load in enumerate(fields):
        for tile in range(NT):
            base = (index * NT + tile) * YRUN
            for z in range(NZ):
                rows = load(z, tile)
                up = pltpu.roll(rows, H, 0)
                a_ref[pl.ds(base + z * H, 8), :] = jnp.where(even, up, rows)
                b_ref[pl.ds(base + z * H, 8), :] = jnp.where(even, rows, up)


def first_kernel(par_ref, u_ref, blend_ref, cls_ref, pdt_ref, femt_ref, hm_ref, fem_ref, a_ref, b_ref):
    even = even_mask(par_ref, 0)
    for z in range(NZ):
        for tile in range(NT):
            blend = blend_ref[z, :, lanes(tile)]
            cls = cls_ref[z, :, lanes(tile)]
            pd = jnp.zeros_like(blend)
            fem = jnp.zeros_like(blend)
            for index in range(NCLASS):
                hit = cls == index
                pd = jnp.where(hit, pdt_ref[index], pd)
                fem = jnp.where(hit, femt_ref[index], fem)
            hm_ref[z, tile] = 0.5 * (pd * blend)
            fem_ref[z, tile] = fem * (1.0 - blend)
    loaders = [lambda z, t, c=c: u_ref[c, z, :, lanes(t)] for c in range(3)]
    loaders.append(lambda z, t: hm_ref[z, t])
    pack_y(loaders, even, a_ref, b_ref)
    for tile in range(NT):
        base = 4 * NT * YRUN + tile * NZ
        for z in range(NZ):
            up = pltpu.roll(fem_ref[z, tile], 1, 0)
            a_ref[pl.ds(base + z, 8), :] = up
            b_ref[pl.ds(base + z, 8), :] = up


def spread_kernel(nfields, par_ref, after_ref, *refs):
    if nfields == 5:
        u_ref, hm_ref, fem_ref, ra_ref, rb_ref, ext_ref, extm_ref, a_ref, b_ref = refs
    else:
        u_ref, ra_ref, rb_ref, ext_ref, a_ref, b_ref = refs
    sub = lax.broadcasted_iota(jnp.int32, (8, LANES), 0)
    even = even_mask(par_ref, 0)
    even_z = even_mask(par_ref, 1)
    nrun = min(nfields, 4)
    for index in range(nrun):
        for tile in range(NT):
            base = (index * NT + tile) * YRUN
            for z in range(NZ):
                rows = u_ref[index, z, :, lanes(tile)] if index < 3 else hm_ref[z, tile]
                turned = pltpu.roll(rows, H, 0)
                got_a = ra_ref[pl.ds(base + z * H, 8), :]
                got_b = rb_ref[pl.ds(base + z * H, 8), :]
                lo = jnp.where(even, got_b, got_a)
                hi = pltpu.roll(jnp.where(even, got_a, got_b), H, 0)
                dst = ext_ref.at[index, z, tile] if index < 3 else extm_ref.at[0, z, tile]
                dst[pl.ds(0, 8), :] = jnp.where(sub < H, lo, turned)
                dst[pl.ds(8, 8), :] = jnp.where(sub < H, turned, hi)
    if nfields == 5:
        for tile in range(NT):
            base = 4 * NT * YRUN + tile * NZ
            for z in range(NZ):
                turned = pltpu.roll(fem_ref[z, tile], H, 0)
                lo = jnp.where(even, rb_ref[pl.ds(base + z, 8), :], ra_ref[pl.ds(base + z, 8), :])
                lo = pltpu.roll(lo, H - 1, 0)
                extm_ref[1, z, tile, pl.ds(0, 8), :] = jnp.where(sub < H, lo, turned)
                extm_ref[1, z, tile, pl.ds(8, 8), :] = turned

    def put(row, up, down):
        a_ref[pl.ds(row, 8), :] = jnp.where(even_z, up, down)
        b_ref[pl.ds(row, 8), :] = jnp.where(even_z, down, up)

    for index in range(nrun):
        for tile in range(NT):
            base = (index * NT + tile) * ZRUN
            src = (lambda z: ext_ref.at[index, z, tile]) if index < 3 else (lambda z: extm_ref.at[0, z, tile])
            put(base, src(5)[pl.ds(3, 8), :], src(2)[pl.ds(3, 8), :])
            for place, zu, zd in ((8, 6, 1), (20, 7, 0)):
                put(base + place, src(zu)[pl.ds(1, 8), :], src(zd)[pl.ds(1, 8), :])
                put(base + place + 4, src(zu)[pl.ds(5, 8), :], src(zd)[pl.ds(5, 8), :])
    if nfields == 5:
        for tile in range(NT):
            base = 4 * NT * ZRUN + tile * FRUN
            for row in (0, 1):
                up = extm_ref[1, NZ - 1, tile, pl.ds(2 + row, 8), :]
                put(base + row, up, up)


def unpack_z(dst, even_z, ra_ref, rb_ref, run):
    base = run * ZRUN

    def get(z_lo, z_hi, row, place):
        got_a = ra_ref[pl.ds(base + place, 8), :]
        got_b = rb_ref[pl.ds(base + place, 8), :]
        dst(z_lo)[pl.ds(row, 8), :] = jnp.where(even_z, got_b, got_a)
        dst(z_hi)[pl.ds(row, 8), :] = jnp.where(even_z, got_a, got_b)

    get(0, 13, 3, 0)
    for place, z_lo, z_hi in ((8, 1, 12), (20, 2, 11)):
        get(z_lo, z_hi, 1, place)
        get(z_lo, z_hi, 5, place + 4)


def fem_force(load, fe, tile, edge, first_layer, layers, emit):
    def spread(c, z, row):
        here = load(c, z, row, 0)
        after = load(c, z, row, 1)
        nxt = pltpu.roll(jnp.where(edge, after, here), LANES - 1, 1)
        return here + nxt, nxt - here

    def modes(low, high):
        return (low[0] + high[0], low[1] + high[1], high[0] - low[0], high[1] - low[1])

    def finish(c, z, low, high):
        parts = []
        for which in range(2):
            if low is None:
                parts.append(high[which])
            elif high is None:
                parts.append(low[which])
            else:
                parts.append([low[which][m] + high[which][m] for m in range(4)])
        a, b = parts
        x_s = (a[0] - a[2]) + (b[0] + b[2])
        x_d = (a[1] - a[3]) + (b[1] + b[3])
        emit(c, z, x_s - x_d, x_s + x_d)

    for c in range(3):
        before = None
        carried = None
        for z in range(first_layer, first_layer + layers + 1):
            level = [spread(c, z, row) for row in (2, 3, 4)]
            now = (modes(level[1], level[2]), modes(level[0], level[1]))
            if before is not None:
                lower, upper = [], []
                for which, row in ((0, 3), (1, 2)):
                    e = fe(z - 1, row)
                    e1, e2, e3 = e * (1.0 / 16.0), e * (1.0 / 24.0), e * (1.0 / 48.0)
                    lo, hi = before[which], now[which]
                    d_ss = e1 * (hi[0] - lo[0])
                    s_dx, d_dx = e1 * (lo[1] + hi[1]), e2 * (hi[1] - lo[1])
                    s_dy, d_dy = e1 * (lo[2] + hi[2]), e2 * (hi[2] - lo[2])
                    s_dd, d_dd = e2 * (lo[3] + hi[3]), e3 * (hi[3] - lo[3])
                    lower.append((-d_ss, s_dx - d_dx, s_dy - d_dy, s_dd - d_dd))
                    upper.append((d_ss, s_dx + d_dx, s_dy + d_dy, s_dd + d_dd))
                if z - 1 >= 0:
                    finish(c, z - 1, carried, lower)
                carried = upper
            before = now
        last = first_layer + layers
        if last < NZ:
            finish(c, last, carried, None)


def roll_out(dst, field, lane, left, here, right):
    bake = field == 2
    dst(0)[...] = here
    for d in range(1, H + 1):
        up = pltpu.roll(jnp.where(lane < d, right, here), LANES - d, 1)
        down = pltpu.roll(jnp.where(lane >= LANES - d, left, here), d, 1)
        dst(d)[...] = up + float(d) if bake else up
        dst(-d)[...] = down - float(d) if bake else down


def reach(lane, left, here, right):
    edge = jnp.maximum(jnp.where(lane >= LANES - H, left, 0.0), jnp.where(lane < H, right, 0.0))
    return jnp.maximum(here, edge)


def bond_sum(moved, center, hm, dz, bonds, acc):
    base = {0: center[0] - dz, 2: center[2]}
    mids = {}
    for _, dy, dx, norm in bonds:
        if dy not in mids:
            mids[dy] = center[1] - float(dy) if dy else center[1]
        rel = [moved(0, dy, dx) - base[0], moved(1, dy, dx) - mids[dy], moved(2, dy, dx) - base[2]]
        m = hm + moved(3, dy, dx)
        square = rel[0] * rel[0] + rel[1] * rel[1] + rel[2] * rel[2]
        factor = m * (1.0 / math.sqrt(norm) - lax.rsqrt(square))
        for c in range(3):
            acc[c] = acc[c] + factor * rel[c]
    return acc


def inside(center_of, moved_of, f_ref, tile, bonds):
    def run(step, size, first, dz, span):
        for k in range(span):
            z = first + k
            center, hm = center_of(z)
            acc = [f_ref[c, z, tile] for c in range(3)]
            acc = bond_sum(lambda f, dy, dx: moved_of(f, dy, dx, z + step), center, hm, dz, bonds[size], acc)
            for c in range(3):
                f_ref[c, z, tile] = acc[c]

    run(0, 0, 0, 0.0, NZ)
    for size in range(1, H + 1):
        if not bonds[size]:
            continue

        def both(side, carry, size=size):
            step = size - 2 * size * side
            run(step, size, size * side, step.astype(F32), NZ - size)
            return carry

        lax.fori_loop(0, 2, both, 0)


def neighbours(load, tile):
    here = load(tile)
    left = jnp.where(tile > 0, load(jnp.maximum(tile - 1, 0)), 0.0)
    right = jnp.where(tile < NT - 1, load(jnp.minimum(tile + 1, NT - 1)), 0.0)
    return left, here, right


def flat_kernel(u_ref, hm_ref, f_ref, sr):
    lane = lax.broadcasted_iota(jnp.int32, (8, LANES), 1)
    zero = jnp.zeros((8, LANES), F32)

    def field(f, z):
        if f < 3:
            return lambda t: u_ref[f, z, :, pl.ds(pl.multiple_of(t * LANES, LANES), LANES)]
        return lambda t: hm_ref[z, t]

    def per_tile(tile, carry):
        most = zero
        for z in range(NZ):
            most = jnp.maximum(most, reach(lane, *neighbours(field(3, z), tile)))
            for c in range(3):
                f_ref[c, z, tile] = zero

        @pl.when(jnp.max(most) > 0.0)
        def _():
            def build(z, c2):
                for f in range(4):
                    roll_out(lambda d: sr.at[f, H + d, z], f, lane, *neighbours(field(f, z), tile))
                return c2

            lax.fori_loop(0, NZ, build, 0)
            inside(
                lambda z: ([sr[c, H, z] for c in range(3)], sr[3, H, z]),
                lambda f, dy, dx, z: sr[f, H + dx, z],
                f_ref,
                tile,
                FLAT,
            )

        return carry

    lax.fori_loop(0, NT, per_tile, 0)


def tilted_kernel(ext_ref, extm_ref, fin_ref, f_ref, p_ref, q_ref, sr):
    lane = lax.broadcasted_iota(jnp.int32, (8, LANES), 1)
    zero = jnp.zeros((8, LANES), F32)

    def field(f, z, row):
        if f < 3:
            return lambda t: ext_ref[f, z, t, pl.ds(row, 8), :]
        return lambda t: extm_ref[0, z, t, pl.ds(row, 8), :]

    def per_tile(tile, carry):
        after = jnp.minimum(tile + 1, NT - 1)
        more = tile < NT - 1

        def load(c, z, row, side):
            if side == 0:
                return ext_ref[c, z, tile, pl.ds(row, 8), :]
            return jnp.where(more, ext_ref[c, z, after, pl.ds(row, 8), :], 0.0)

        def emit(c, z, p, q):
            p_ref[c, z, tile] = p
            q_ref[c, z, tile] = q

        fem_force(load, lambda z, row: extm_ref[1, z, tile, pl.ds(row, 8), :], tile, lane < 1, 0, NZ - 1, emit)
        most = zero
        for z in range(NZ):
            for c in range(3):
                f_ref[c, z, tile] = fin_ref[c, z, tile]
            for row in (0, 6):
                most = jnp.maximum(most, reach(lane, *neighbours(field(3, z, row), tile)))

        @pl.when(jnp.max(most) > 0.0)
        def _():
            def build(z, c2):
                for f in range(4):
                    for half in (0, 8):
                        roll_out(lambda d: sr.at[f, H + d, z, pl.ds(half, 8)], f, lane, *neighbours(field(f, z, half), tile))
                return c2

            lax.fori_loop(0, NZ, build, 0)
            inside(
                lambda z: ([sr[c, H, z, pl.ds(H, 8), :] for c in range(3)], sr[3, H, z, pl.ds(H, 8), :]),
                lambda f, dy, dx, z: sr[f, H + dx, z, pl.ds(H + dy, 8), :],
                f_ref,
                tile,
                TILTED,
            )

        return carry

    lax.fori_loop(0, NT, per_tile, 0)


def last_kernel(last, par_ref, u_ref, v_ref, load_ref, ext_ref, extm_ref, ura_ref, urb_ref, mra_ref, mrb_ref, f_ref, p_ref, q_ref, *refs):
    if last:
        nu_ref, nv_ref, sz, fe, sr, fx, px, qx = refs
    else:
        nu_ref, nv_ref, a_ref, b_ref, sz, fe, sr, fx, px, qx = refs
    even = even_mask(par_ref, 0)
    even_z = even_mask(par_ref, 1)
    lane = lax.broadcasted_iota(jnp.int32, (8, LANES), 1)
    zero = jnp.zeros((8, LANES), F32)
    spot = {0: 0, 1: 1, 2: 2, 11: 3, 12: 4, 13: 5}
    for tile in range(NT):
        for z in range(2 * H):
            for half in (0, 8):
                sz[3, z, tile, pl.ds(half, 8), :] = zero
        for f in range(4):
            ra, rb = (ura_ref, urb_ref) if f < 3 else (mra_ref, mrb_ref)
            unpack_z(lambda z: sz.at[f, spot[z], tile], even_z, ra, rb, f * NT + tile)
        base = 4 * NT * ZRUN + tile * FRUN
        for row in (0, 1):
            fe[tile, pl.ds(2 + row, 8), :] = jnp.where(
                even_z, mrb_ref[pl.ds(base + row, 8), :], mra_ref[pl.ds(base + row, 8), :]
            )

    def per_tile(tile, carry):
        after = jnp.minimum(tile + 1, NT - 1)
        more = tile < NT - 1

        def load(c, z, row, side):
            t = tile if side == 0 else after
            if z < 0:
                got = sz[c, H + z, t, pl.ds(row, 8), :]
            elif z >= NZ:
                got = sz[c, z - NZ + H, t, pl.ds(row, 8), :]
            else:
                got = ext_ref[c, z, t, pl.ds(row, 8), :]
            return got if side == 0 else jnp.where(more, got, 0.0)

        def emit(c, z, p, q):
            px[c, 0 if z == 0 else 1, tile] = p
            qx[c, 0 if z == 0 else 1, tile] = q

        fem_force(load, lambda z, row: fe[tile, pl.ds(row, 8), :], tile, lane < 1, -1, 1, emit)
        fem_force(load, lambda z, row: extm_ref[1, NZ - 1, tile, pl.ds(row, 8), :], tile, lane < 1, NZ - 1, 1, emit)

        def center_hm(z):
            return lambda t: extm_ref[0, z, t, pl.ds(H, 8), :]

        most = zero
        for z in range(2 * H):
            for row in (0, 6):
                got = neighbours(lambda t: sz[3, z, t, pl.ds(row, 8), :], tile)
                most = jnp.maximum(most, reach(lane, *got))
        for z in (0, 1, 2, 5, 6, 7):
            most = jnp.maximum(most, extm_ref[0, z, tile, pl.ds(H, 8), :])
            for c in range(3):
                fx[c, z if z < H else z - 2, tile] = zero

        @pl.when(jnp.max(most) > 0.0)
        def _():
            def build(z, c2):
                for f in range(4):
                    for half in (0, 8):
                        got = neighbours(lambda t: sz[f, z, t, pl.ds(half, 8), :], tile)
                        roll_out(lambda d: sr.at[f, H + d, z, pl.ds(half, 8)], f, lane, *got)
                return c2

            lax.fori_loop(0, 2 * H, build, 0)

            def side_loop(side, c2):
                sign = 2 * side - 1
                for k in range(H):
                    z = k + side * (NZ - 1 - 2 * k)
                    center = [ext_ref[c, z, tile, pl.ds(H, 8), :] for c in range(3)]
                    hm = extm_ref[0, z, tile, pl.ds(H, 8), :]
                    acc = [zero] * 3
                    for size in range(k + 1, H + 1):
                        place = (H - (size - k)) + side * (2 * (size - k) - 1)
                        acc = bond_sum(
                            lambda f, dy, dx: sr[f, H + dx, place, pl.ds(H + dy, 8), :],
                            center,
                            hm,
                            (sign * size).astype(F32),
                            FLAT[size] + TILTED[size],
                            acc,
                        )
                    for c in range(3):
                        fx[c, k + side * (2 * H - 1 - 2 * k), tile] = acc[c]
                return c2

            lax.fori_loop(0, 2, side_loop, 0)

        return carry

    lax.fori_loop(0, NT, per_tile, 0)

    for c in range(3):
        for z in range(NZ):
            shifted = zero
            for tile in range(NT):
                p, q, f = p_ref[c, z, tile], q_ref[c, z, tile], f_ref[c, z, tile]
                if z in (0, NZ - 1):
                    p = p + px[c, 0 if z == 0 else 1, tile]
                    q = q + qx[c, 0 if z == 0 else 1, tile]
                if z < H or z >= NZ - H:
                    f = f + fx[c, z if z < H else z - 2, tile]
                moved = pltpu.roll(jnp.where(lane == LANES - 1, shifted, q), 1, 1)
                shifted = q
                force = f - (p + moved)
                where = (c, z, slice(None), lanes(tile))
                v = v_ref[where] + 0.25 * (force + load_ref[where])
                u = u_ref[where] + 0.01 * v
                nv_ref[where] = v
                nu_ref[where] = u
    if not last:
        pack_y([lambda z, t, c=c: nu_ref[c, z, :, lanes(t)] for c in range(3)], even, a_ref, b_ref)


def shape(*dims):
    return jax.ShapeDtypeStruct(dims, F32)


def swap(axis, a, b):
    count = lax.axis_size(axis)

    def pairs(first):
        out = []
        for i in range(first, count - 1, 2):
            out += [(i, i + 1), (i + 1, i)]
        return out

    got_b = lax.ppermute(b, axis, pairs(1))
    return lax.ppermute(a, axis, pairs(0)), got_b


YROWS = 3 * NT * YRUN + 8
ZROWS = 3 * NT * ZRUN
YROWS5 = 4 * NT * YRUN + NT * NZ + 8
ZROWS5 = 4 * NT * ZRUN + 40


def call(kernel, name, outs, ins, scratch=(), work=1):
    return pl.pallas_call(
        kernel,
        out_shape=tuple(outs),
        in_specs=[{"s": smem, "v": vmem, "a": anywhere}[kind]() for kind in ins],
        out_specs=(vmem(),) * len(outs),
        scratch_shapes=[pltpu.VMEM(dims, F32) for dims in scratch],
        compiler_params=params(),
        cost_estimate=pl.CostEstimate(flops=work * 1000000, bytes_accessed=work * 1000000, transcendentals=0),
        name=name,
    )


def body(displacement, velocity, load, blend, classes, pd_table, fem_table):
    whole = shape(3, NZ, NY, NT * LANES)
    tiles = shape(3, NZ, NT, 8, LANES)
    ext_shape = shape(3, NZ, NT, 16, LANES)
    par = jnp.stack([lax.axis_index("tile") % 2, lax.axis_index("seg") % 2]).astype(jnp.int32)
    one = shape(NZ, NT, 8, LANES)
    hm, fem, a, b = call(first_kernel, "moduli", (one, one, shape(YROWS5, LANES), shape(YROWS5, LANES)), "svvvss")(
        par, displacement, blend, classes, pd_table, fem_table
    )
    u, v = displacement, velocity
    extm = mra = mrb = None
    for step in range(STEPS):
        last = step == STEPS - 1
        ra, rb = swap("tile", a, b)
        (f,) = call(flat_kernel, f"flat_{step}", (tiles,), "vv", [(4, 2 * H + 1, NZ, 8, LANES)], 4)(u, hm)
        if step == 0:
            outs = (ext_shape, shape(2, NZ, NT, 16, LANES), shape(ZROWS5, LANES), shape(ZROWS5, LANES))
            ext, extm, a, b = call(functools.partial(spread_kernel, 5), "spread_0", outs, "savvvvv")(par, f, u, hm, fem, ra, rb)
        else:
            outs = (ext_shape, shape(ZROWS, LANES), shape(ZROWS, LANES))
            ext, a, b = call(functools.partial(spread_kernel, 3), f"spread_{step}", outs, "savvv")(par, f, u, ra, rb)
        ra, rb = swap("seg", a, b)
        if step == 0:
            mra, mrb = ra, rb
        f, p, q = call(
            tilted_kernel, f"tilted_{step}", (tiles, tiles, tiles), "vvv", [(4, 2 * H + 1, NZ, 16, LANES)], 16
        )(ext, extm, f)
        outs = [whole, whole]
        if not last:
            outs += [shape(YROWS, LANES)] * 2
        scratch = [
            (4, 2 * H, NT, 16, LANES),
            (NT, 16, LANES),
            (4, 2 * H + 1, 2 * H, 16, LANES),
            (3, 2 * H, NT, 8, LANES),
            (3, 2, NT, 8, LANES),
            (3, 2, NT, 8, LANES),
        ]
        got = call(functools.partial(last_kernel, last), f"finish_{step}", outs, "s" + "v" * 12, scratch, 4)(
            par, u, v, load, ext, extm, ra, rb, mra, mrb, f, p, q
        )
        u, v = got[:2]
        if not last:
            a, b = got[2:]
    return u, v


def solution(mesh):
    cells = P(None, "seg", "tile", None)
    plane = P("seg", "tile", None)
    return jax.shard_map(
        body,
        mesh=mesh,
        in_specs=(cells, cells, cells, plane, plane, P(), P()),
        out_specs=(cells, cells),
        check_vma=False,
    )
```

```python
import functools
import math

import jax
import jax.numpy as jnp
from jax import lax
from jax.experimental import pallas as pl
from jax.experimental.pallas import tpu as pltpu
from jax.sharding import PartitionSpec as P

H = 3
STEPS = 2
NCLASS = 4
NZ = 8
NY = 8
NT = 4
LANES = 128
F32 = jnp.float32

YRUN = NZ * H
ZRUN = 32
FRUN = 9
UNROLL = 2
FIRST_LIMIT = 67000000
UNROLL3 = 2


def offsets():
    out = []
    for dz in range(-H, H + 1):
        for dy in range(-H, H + 1):
            for dx in range(-H, H + 1):
                n = dz * dz + dy * dy + dx * dx
                if 0 < n <= H * H:
                    out.append((dz, dy, dx, n))
    return out


OFFSETS = offsets()
FLAT = {dz: [o for o in OFFSETS if o[0] == dz and o[1] == 0] for dz in range(-H, H + 1)}
TILTED = {dz: [o for o in OFFSETS if o[0] == dz and o[1] != 0] for dz in range(-H, H + 1)}


def vmem():
    return pl.BlockSpec(memory_space=pltpu.VMEM)


def anywhere():
    return pl.BlockSpec(memory_space=pl.ANY)


def params():
    return pltpu.CompilerParams(vmem_limit_bytes=24 * 1024 * 1024)


def lanes(tile):
    return pl.ds(tile * LANES, LANES)


def even_mask(axis):
    return jnp.full((8, LANES), lax.axis_index(axis) % 2, jnp.int32) == 0


def pack_y(fields, even, a_ref, b_ref):
    for index, load in enumerate(fields):
        for tile in range(NT):
            base = (index * NT + tile) * YRUN
            for z in range(NZ):
                rows = load(z, tile)
                up = pltpu.roll(rows, H, 0)
                a_ref[pl.ds(base + z * H, 8), :] = jnp.where(even, up, rows)
                b_ref[pl.ds(base + z * H, 8), :] = jnp.where(even, rows, up)


def first_kernel(u_hbm, blend_hbm, cls_hbm, pdt_hbm, femt_hbm, hm_ref, fem_ref, a_ref, b_ref, u_ref, blend_ref, cls_ref, pdt_ref, femt_ref, sem):
    copies = [pltpu.make_async_copy(blend_hbm, blend_ref, sem.at[3]), pltpu.make_async_copy(cls_hbm, cls_ref, sem.at[4])]
    copies += [pltpu.make_async_copy(pdt_hbm, pdt_ref, sem.at[5]), pltpu.make_async_copy(femt_hbm, femt_ref, sem.at[6])]
    moves = [pltpu.make_async_copy(u_hbm.at[c], u_ref.at[c], sem.at[c]) for c in range(3)]
    for copy in copies + moves:
        copy.start()
    for copy in copies:
        copy.wait()
    even = even_mask("tile")
    for z in range(NZ):
        for tile in range(NT):
            blend = blend_ref[z, :, lanes(tile)]
            cls = cls_ref[z, :, lanes(tile)]
            pd = jnp.zeros_like(blend)
            fem = jnp.zeros_like(blend)
            for index in range(NCLASS):
                hit = cls == index
                pd = jnp.where(hit, pdt_ref[index], pd)
                fem = jnp.where(hit, femt_ref[index], fem)
            hm_ref[z, tile] = 0.5 * (pd * blend)
            fem_ref[z, tile] = fem * (1.0 - blend)
    for copy in moves:
        copy.wait()
    loaders = [lambda z, t, c=c: u_ref[c, z, :, lanes(t)] for c in range(3)]
    loaders.append(lambda z, t: hm_ref[z, t])
    pack_y(loaders, even, a_ref, b_ref)
    for tile in range(NT):
        base = 4 * NT * YRUN + tile * NZ
        for z in range(NZ):
            up = pltpu.roll(fem_ref[z, tile], 1, 0)
            a_ref[pl.ds(base + z, 8), :] = up
            b_ref[pl.ds(base + z, 8), :] = up


def spread_kernel(nfields, after_ref, *refs):
    if nfields == 5:
        u_ref, hm_ref, fem_ref, ra_ref, rb_ref, ext_ref, extm_ref, a_ref, b_ref = refs
    else:
        u_ref, ra_ref, rb_ref, ext_ref, a_ref, b_ref = refs
    sub = lax.broadcasted_iota(jnp.int32, (8, LANES), 0)
    even = even_mask("tile")
    even_z = even_mask("seg")
    nrun = min(nfields, 4)
    for index in range(nrun):
        for tile in range(NT):
            base = (index * NT + tile) * YRUN
            for z in range(NZ):
                rows = u_ref[index, z, :, lanes(tile)] if index < 3 else hm_ref[z, tile]
                turned = pltpu.roll(rows, H, 0)
                got_a = ra_ref[pl.ds(base + z * H, 8), :]
                got_b = rb_ref[pl.ds(base + z * H, 8), :]
                lo = jnp.where(even, got_b, got_a)
                hi = pltpu.roll(jnp.where(even, got_a, got_b), H, 0)
                dst = ext_ref.at[index, z, tile] if index < 3 else extm_ref.at[0, z, tile]
                dst[pl.ds(0, 8), :] = jnp.where(sub < H, lo, turned)
                dst[pl.ds(8, 8), :] = jnp.where(sub < H, turned, hi)
    if nfields == 5:
        for tile in range(NT):
            base = 4 * NT * YRUN + tile * NZ
            for z in range(NZ):
                turned = pltpu.roll(fem_ref[z, tile], H, 0)
                lo = jnp.where(even, rb_ref[pl.ds(base + z, 8), :], ra_ref[pl.ds(base + z, 8), :])
                lo = pltpu.roll(lo, H - 1, 0)
                extm_ref[1, z, tile, pl.ds(0, 8), :] = jnp.where(sub < H, lo, turned)
                extm_ref[1, z, tile, pl.ds(8, 8), :] = turned

    def put(row, up, down):
        a_ref[pl.ds(row, 8), :] = jnp.where(even_z, up, down)
        b_ref[pl.ds(row, 8), :] = jnp.where(even_z, down, up)

    for index in range(nrun):
        for tile in range(NT):
            base = (index * NT + tile) * ZRUN
            src = (lambda z: ext_ref.at[index, z, tile]) if index < 3 else (lambda z: extm_ref.at[0, z, tile])
            put(base, src(5)[pl.ds(3, 8), :], src(2)[pl.ds(3, 8), :])
            for place, zu, zd in ((8, 6, 1), (20, 7, 0)):
                put(base + place, src(zu)[pl.ds(1, 8), :], src(zd)[pl.ds(1, 8), :])
                put(base + place + 4, src(zu)[pl.ds(5, 8), :], src(zd)[pl.ds(5, 8), :])
    if nfields == 5:
        for tile in range(NT):
            base = 4 * NT * ZRUN + tile * FRUN
            for row in (0, 1):
                up = extm_ref[1, NZ - 1, tile, pl.ds(2 + row, 8), :]
                put(base + row, up, up)


def unpack_z(dst, even_z, ra_ref, rb_ref, run):
    base = run * ZRUN

    def get(z_lo, z_hi, row, place):
        got_a = ra_ref[pl.ds(base + place, 8), :]
        got_b = rb_ref[pl.ds(base + place, 8), :]
        dst(z_lo)[pl.ds(row, 8), :] = jnp.where(even_z, got_b, got_a)
        dst(z_hi)[pl.ds(row, 8), :] = jnp.where(even_z, got_a, got_b)

    get(0, 13, 3, 0)
    for place, z_lo, z_hi in ((8, 1, 12), (20, 2, 11)):
        get(z_lo, z_hi, 1, place)
        get(z_lo, z_hi, 5, place + 4)


def fem_force(load, fe, tile, edge, first_layer, layers, emit):
    def spread(c, z, row):
        here = load(c, z, row, 0)
        after = load(c, z, row, 1)
        nxt = pltpu.roll(jnp.where(edge, after, here), LANES - 1, 1)
        return here + nxt, nxt - here

    def modes(low, high):
        return (low[0] + high[0], low[1] + high[1], high[0] - low[0], high[1] - low[1])

    def finish(c, z, low, high):
        parts = []
        for which in range(2):
            if low is None:
                parts.append(high[which])
            elif high is None:
                parts.append(low[which])
            else:
                parts.append([low[which][m] + high[which][m] for m in range(4)])
        a, b = parts
        x_s = (a[0] - a[2]) + (b[0] + b[2])
        x_d = (a[1] - a[3]) + (b[1] + b[3])
        emit(c, z, x_s - x_d, x_s + x_d)

    for c in range(3):
        before = None
        carried = None
        for z in range(first_layer, first_layer + layers + 1):
            level = [spread(c, z, row) for row in (2, 3, 4)]
            now = (modes(level[1], level[2]), modes(level[0], level[1]))
            if before is not None:
                lower, upper = [], []
                for which, row in ((0, 3), (1, 2)):
                    e = fe(z - 1, row)
                    e1, e2, e3 = e * (1.0 / 16.0), e * (1.0 / 24.0), e * (1.0 / 48.0)
                    lo, hi = before[which], now[which]
                    d_ss = e1 * (hi[0] - lo[0])
                    s_dx, d_dx = e1 * (lo[1] + hi[1]), e2 * (hi[1] - lo[1])
                    s_dy, d_dy = e1 * (lo[2] + hi[2]), e2 * (hi[2] - lo[2])
                    s_dd, d_dd = e2 * (lo[3] + hi[3]), e3 * (hi[3] - lo[3])
                    lower.append((-d_ss, s_dx - d_dx, s_dy - d_dy, s_dd - d_dd))
                    upper.append((d_ss, s_dx + d_dx, s_dy + d_dy, s_dd + d_dd))
                if z - 1 >= 0:
                    finish(c, z - 1, carried, lower)
                carried = upper
            before = now
        last = first_layer + layers
        if last < NZ:
            finish(c, last, carried, None)


def roll_out(dst, field, lane, left, here, right):
    bake = field == 2
    dst(0)[...] = here
    for d in range(1, H + 1):
        up = pltpu.roll(jnp.where(lane < d, right, here), LANES - d, 1)
        down = pltpu.roll(jnp.where(lane >= LANES - d, left, here), d, 1)
        dst(d)[...] = up + float(d) if bake else up
        dst(-d)[...] = down - float(d) if bake else down


def reach(lane, left, here, right):
    edge = jnp.maximum(jnp.where(lane >= LANES - H, left, 0.0), jnp.where(lane < H, right, 0.0))
    return jnp.maximum(here, edge)


def bond_sum(moved, center, hm, dz, bonds, acc):
    base = {0: center[0] - dz, 2: center[2]}
    mids = {}
    for _, dy, dx, norm in bonds:
        if dy not in mids:
            mids[dy] = center[1] - float(dy) if dy else center[1]
        rel = [moved(0, dy, dx) - base[0], moved(1, dy, dx) - mids[dy], moved(2, dy, dx) - base[2]]
        m = hm + moved(3, dy, dx)
        square = rel[0] * rel[0] + rel[1] * rel[1] + rel[2] * rel[2]
        factor = m * (1.0 / math.sqrt(norm) - lax.rsqrt(square))
        for c in range(3):
            acc[c] = acc[c] + factor * rel[c]
    return acc


def inside(center_of, moved_of, f_ref, tile, bonds):
    def run(step, size, first, dz, span):
        for k in range(span):
            z = first + k
            center, hm = center_of(z)
            acc = [f_ref[c, z, tile] for c in range(3)]
            acc = bond_sum(lambda f, dy, dx: moved_of(f, dy, dx, z + step), center, hm, dz, bonds[size], acc)
            for c in range(3):
                f_ref[c, z, tile] = acc[c]

    run(0, 0, 0, 0.0, NZ)
    for size in range(1, H + 1):
        if not bonds[size]:
            continue

        def both(side, carry, size=size):
            step = size - 2 * size * side
            run(step, size, size * side, step.astype(F32), NZ - size)
            return carry

        lax.fori_loop(0, 2, both, 0)


def neighbours(load, tile):
    here = load(tile)
    left = jnp.where(tile > 0, load(jnp.maximum(tile - 1, 0)), 0.0)
    right = jnp.where(tile < NT - 1, load(jnp.minimum(tile + 1, NT - 1)), 0.0)
    return left, here, right


def flat_kernel(u_ref, hm_ref, f_ref, sr):
    lane = lax.broadcasted_iota(jnp.int32, (8, LANES), 1)
    zero = jnp.zeros((8, LANES), F32)

    def field(f, z):
        if f < 3:
            return lambda t: u_ref[f, z, :, pl.ds(pl.multiple_of(t * LANES, LANES), LANES)]
        return lambda t: hm_ref[z, t]

    def per_tile(tile, carry):
        most = zero
        for z in range(NZ):
            most = jnp.maximum(most, reach(lane, *neighbours(field(3, z), tile)))
            for c in range(3):
                f_ref[c, z, tile] = zero

        @pl.when(jnp.max(most) > 0.0)
        def _():
            def build(z, c2):
                for f in range(4):
                    roll_out(lambda d: sr.at[f, H + d, z], f, lane, *neighbours(field(f, z), tile))
                return c2

            lax.fori_loop(0, NZ, build, 0, unroll=UNROLL)
            inside(
                lambda z: ([sr[c, H, z] for c in range(3)], sr[3, H, z]),
                lambda f, dy, dx, z: sr[f, H + dx, z],
                f_ref,
                tile,
                FLAT,
            )

        return carry

    lax.fori_loop(0, NT, per_tile, 0)


def tilted_kernel(ext_ref, extm_ref, fin_ref, f_ref, p_ref, q_ref, sr):
    lane = lax.broadcasted_iota(jnp.int32, (8, LANES), 1)
    zero = jnp.zeros((8, LANES), F32)

    def field(f, z, row):
        if f < 3:
            return lambda t: ext_ref[f, z, t, pl.ds(row, 8), :]
        return lambda t: extm_ref[0, z, t, pl.ds(row, 8), :]

    def per_tile(tile, carry):
        after = jnp.minimum(tile + 1, NT - 1)
        more = tile < NT - 1

        def load(c, z, row, side):
            if side == 0:
                return ext_ref[c, z, tile, pl.ds(row, 8), :]
            return jnp.where(more, ext_ref[c, z, after, pl.ds(row, 8), :], 0.0)

        def emit(c, z, p, q):
            p_ref[c, z, tile] = p
            q_ref[c, z, tile] = q

        fem_force(load, lambda z, row: extm_ref[1, z, tile, pl.ds(row, 8), :], tile, lane < 1, 0, NZ - 1, emit)
        most = zero
        for z in range(NZ):
            for c in range(3):
                f_ref[c, z, tile] = fin_ref[c, z, tile]
            for row in (0, 6):
                most = jnp.maximum(most, reach(lane, *neighbours(field(3, z, row), tile)))

        @pl.when(jnp.max(most) > 0.0)
        def _():
            def build(z, c2):
                for f in range(4):
                    for half in (0, 8):
                        roll_out(lambda d: sr.at[f, H + d, z, pl.ds(half, 8)], f, lane, *neighbours(field(f, z, half), tile))
                return c2

            lax.fori_loop(0, NZ, build, 0, unroll=UNROLL)
            inside(
                lambda z: ([sr[c, H, z, pl.ds(H, 8), :] for c in range(3)], sr[3, H, z, pl.ds(H, 8), :]),
                lambda f, dy, dx, z: sr[f, H + dx, z, pl.ds(H + dy, 8), :],
                f_ref,
                tile,
                TILTED,
            )

        return carry

    lax.fori_loop(0, NT, per_tile, 0)


def last_kernel(last, u_ref, v_ref, load_ref, ext_ref, extm_ref, ura_ref, urb_ref, mra_ref, mrb_ref, f_ref, p_ref, q_ref, *refs):
    if last:
        nu_ref, nv_ref, sz, fe, sr, fx, px, qx = refs
    else:
        nu_ref, nv_ref, a_ref, b_ref, sz, fe, sr, fx, px, qx = refs
    even = even_mask("tile")
    even_z = even_mask("seg")
    lane = lax.broadcasted_iota(jnp.int32, (8, LANES), 1)
    zero = jnp.zeros((8, LANES), F32)
    spot = {0: 0, 1: 1, 2: 2, 11: 3, 12: 4, 13: 5}
    for tile in range(NT):
        for z in range(2 * H):
            for half in (0, 8):
                sz[3, z, tile, pl.ds(half, 8), :] = zero
        for f in range(4):
            ra, rb = (ura_ref, urb_ref) if f < 3 else (mra_ref, mrb_ref)
            unpack_z(lambda z: sz.at[f, spot[z], tile], even_z, ra, rb, f * NT + tile)
        base = 4 * NT * ZRUN + tile * FRUN
        for row in (0, 1):
            fe[tile, pl.ds(2 + row, 8), :] = jnp.where(
                even_z, mrb_ref[pl.ds(base + row, 8), :], mra_ref[pl.ds(base + row, 8), :]
            )

    def per_tile(tile, carry):
        after = jnp.minimum(tile + 1, NT - 1)
        more = tile < NT - 1

        def load(c, z, row, side):
            t = tile if side == 0 else after
            if z < 0:
                got = sz[c, H + z, t, pl.ds(row, 8), :]
            elif z >= NZ:
                got = sz[c, z - NZ + H, t, pl.ds(row, 8), :]
            else:
                got = ext_ref[c, z, t, pl.ds(row, 8), :]
            return got if side == 0 else jnp.where(more, got, 0.0)

        def emit(c, z, p, q):
            px[c, 0 if z == 0 else 1, tile] = p
            qx[c, 0 if z == 0 else 1, tile] = q

        fem_force(load, lambda z, row: fe[tile, pl.ds(row, 8), :], tile, lane < 1, -1, 1, emit)
        fem_force(load, lambda z, row: extm_ref[1, NZ - 1, tile, pl.ds(row, 8), :], tile, lane < 1, NZ - 1, 1, emit)

        def center_hm(z):
            return lambda t: extm_ref[0, z, t, pl.ds(H, 8), :]

        most = zero
        for z in range(2 * H):
            for row in (0, 6):
                got = neighbours(lambda t: sz[3, z, t, pl.ds(row, 8), :], tile)
                most = jnp.maximum(most, reach(lane, *got))
        for z in (0, 1, 2, 5, 6, 7):
            most = jnp.maximum(most, extm_ref[0, z, tile, pl.ds(H, 8), :])
            for c in range(3):
                fx[c, z if z < H else z - 2, tile] = zero

        @pl.when(jnp.max(most) > 0.0)
        def _():
            def build(z, c2):
                for f in range(4):
                    for half in (0, 8):
                        got = neighbours(lambda t: sz[f, z, t, pl.ds(half, 8), :], tile)
                        roll_out(lambda d: sr.at[f, H + d, z, pl.ds(half, 8)], f, lane, *got)
                return c2

            lax.fori_loop(0, 2 * H, build, 0, unroll=UNROLL3)

            def side_loop(side, c2):
                sign = 2 * side - 1
                for k in range(H):
                    z = k + side * (NZ - 1 - 2 * k)
                    center = [ext_ref[c, z, tile, pl.ds(H, 8), :] for c in range(3)]
                    hm = extm_ref[0, z, tile, pl.ds(H, 8), :]
                    acc = [zero] * 3
                    for size in range(k + 1, H + 1):
                        place = (H - (size - k)) + side * (2 * (size - k) - 1)
                        acc = bond_sum(
                            lambda f, dy, dx: sr[f, H + dx, place, pl.ds(H + dy, 8), :],
                            center,
                            hm,
                            (sign * size).astype(F32),
                            FLAT[size] + TILTED[size],
                            acc,
                        )
                    for c in range(3):
                        fx[c, k + side * (2 * H - 1 - 2 * k), tile] = acc[c]
                return c2

            lax.fori_loop(0, 2, side_loop, 0)

        return carry

    lax.fori_loop(0, NT, per_tile, 0)

    for c in range(3):
        for z in range(NZ):
            shifted = zero
            for tile in range(NT):
                p, q, f = p_ref[c, z, tile], q_ref[c, z, tile], f_ref[c, z, tile]
                if z in (0, NZ - 1):
                    p = p + px[c, 0 if z == 0 else 1, tile]
                    q = q + qx[c, 0 if z == 0 else 1, tile]
                if z < H or z >= NZ - H:
                    f = f + fx[c, z if z < H else z - 2, tile]
                moved = pltpu.roll(jnp.where(lane == LANES - 1, shifted, q), 1, 1)
                shifted = q
                force = f - (p + moved)
                where = (c, z, slice(None), lanes(tile))
                v = v_ref[where] + 0.25 * (force + load_ref[where])
                u = u_ref[where] + 0.01 * v
                nv_ref[where] = v
                nu_ref[where] = u
    if not last:
        pack_y([lambda z, t, c=c: nu_ref[c, z, :, lanes(t)] for c in range(3)], even, a_ref, b_ref)


def shape(*dims):
    return jax.ShapeDtypeStruct(dims, F32)


def swap(axis, a, b):
    count = lax.axis_size(axis)

    def pairs(first):
        out = []
        for i in range(first, count - 1, 2):
            out += [(i, i + 1), (i + 1, i)]
        return out

    got_b = lax.ppermute(b, axis, pairs(1))
    return lax.ppermute(a, axis, pairs(0)), got_b


YROWS = 3 * NT * YRUN + 8
ZROWS = 3 * NT * ZRUN
YROWS5 = 4 * NT * YRUN + NT * NZ + 8
ZROWS5 = 4 * NT * ZRUN + 40


def call(kernel, name, outs, ins, scratch=(), work=1):
    return pl.pallas_call(
        kernel,
        out_shape=tuple(outs),
        in_specs=[anywhere() if kind == "a" else vmem() for kind in ins],
        out_specs=(vmem(),) * len(outs),
        scratch_shapes=[pltpu.VMEM(dims, F32) for dims in scratch],
        compiler_params=params(),
        cost_estimate=pl.CostEstimate(flops=work * 1000000, bytes_accessed=work * 1000000, transcendentals=0),
        name=name,
    )


def body(displacement, velocity, load, blend, classes, pd_table, fem_table):
    whole = shape(3, NZ, NY, NT * LANES)
    tiles = shape(3, NZ, NT, 8, LANES)
    ext_shape = shape(3, NZ, NT, 16, LANES)
    one = shape(NZ, NT, 8, LANES)
    block = (3, NZ, NY, NT * LANES)
    hm, fem, a, b = pl.pallas_call(
        first_kernel,
        out_shape=(one, one, shape(YROWS5, LANES), shape(YROWS5, LANES)),
        in_specs=[anywhere()] * 5,
        out_specs=(vmem(),) * 4,
        scratch_shapes=[
            pltpu.VMEM(block, F32),
            pltpu.VMEM(block[1:], F32),
            pltpu.VMEM(block[1:], jnp.int32),
            pltpu.SMEM((NCLASS,), F32),
            pltpu.SMEM((NCLASS,), F32),
            pltpu.SemaphoreType.DMA((7,)),
        ],
        compiler_params=pltpu.CompilerParams(vmem_limit_bytes=FIRST_LIMIT),
        name="moduli",
    )(displacement, blend, classes, pd_table, fem_table)
    u, v = displacement, velocity
    extm = mra = mrb = None
    for step in range(STEPS):
        last = step == STEPS - 1
        ra, rb = swap("tile", a, b)
        (f,) = call(flat_kernel, f"flat_{step}", (tiles,), "vv", [(4, 2 * H + 1, NZ, 8, LANES)], 4)(u, hm)
        if step == 0:
            outs = (ext_shape, shape(2, NZ, NT, 16, LANES), shape(ZROWS5, LANES), shape(ZROWS5, LANES))
            ext, extm, a, b = call(functools.partial(spread_kernel, 5), "spread_0", outs, "avvvvv")(f, u, hm, fem, ra, rb)
        else:
            outs = (ext_shape, shape(ZROWS, LANES), shape(ZROWS, LANES))
            ext, a, b = call(functools.partial(spread_kernel, 3), f"spread_{step}", outs, "avvv")(f, u, ra, rb)
        ra, rb = swap("seg", a, b)
        if step == 0:
            mra, mrb = ra, rb
        f, p, q = call(
            tilted_kernel, f"tilted_{step}", (tiles, tiles, tiles), "vvv", [(4, 2 * H + 1, NZ, 16, LANES)], 16
        )(ext, extm, f)
        outs = [whole, whole]
        if not last:
            outs += [shape(YROWS, LANES)] * 2
        scratch = [
            (4, 2 * H, NT, 16, LANES),
            (NT, 16, LANES),
            (4, 2 * H + 1, 2 * H, 16, LANES),
            (3, 2 * H, NT, 8, LANES),
            (3, 2, NT, 8, LANES),
            (3, 2, NT, 8, LANES),
        ]
        got = call(functools.partial(last_kernel, last), f"finish_{step}", outs, "v" * 12, scratch, 4)(
            u, v, load, ext, extm, ra, rb, mra, mrb, f, p, q
        )
        u, v = got[:2]
        if not last:
            a, b = got[2:]
    return u, v


def solution(mesh):
    cells = P(None, "seg", "tile", None)
    plane = P("seg", "tile", None)
    return jax.shard_map(
        body,
        mesh=mesh,
        in_specs=(cells, cells, cells, plane, plane, P(), P()),
        out_specs=(cells, cells),
        check_vma=False,
    )
```

```python
import functools
import math

import jax
import jax.numpy as jnp
from jax import lax
from jax.experimental import pallas as pl
from jax.experimental.pallas import tpu as pltpu
from jax.sharding import PartitionSpec as P

H = 3
STEPS = 2
NCLASS = 4
NZ = 8
NY = 8
NT = 4
LANES = 128
F32 = jnp.float32

YRUN = NZ * H
ZRUN = 32
FRUN = 9
UNROLL = 2
FIRST_LIMIT = 67000000
FLAT_CHUNK = 8
TILTED_CHUNK = 4
UNROLL3 = 2


def offsets():
    out = []
    for dz in range(-H, H + 1):
        for dy in range(-H, H + 1):
            for dx in range(-H, H + 1):
                n = dz * dz + dy * dy + dx * dx
                if 0 < n <= H * H:
                    out.append((dz, dy, dx, n))
    return out


OFFSETS = offsets()
FLAT = {dz: [o for o in OFFSETS if o[0] == dz and o[1] == 0] for dz in range(-H, H + 1)}
TILTED = {dz: [o for o in OFFSETS if o[0] == dz and o[1] != 0] for dz in range(-H, H + 1)}


def vmem():
    return pl.BlockSpec(memory_space=pltpu.VMEM)


def anywhere():
    return pl.BlockSpec(memory_space=pl.ANY)


def params():
    return pltpu.CompilerParams(vmem_limit_bytes=24 * 1024 * 1024)


def lanes(tile):
    return pl.ds(tile * LANES, LANES)


def even_mask(axis):
    return jnp.full((8, LANES), lax.axis_index(axis) % 2, jnp.int32) == 0


def pack_y(fields, even, a_ref, b_ref):
    for tile in range(NT):
        for index, load in enumerate(fields):
            base = (tile * len(fields) + index) * YRUN
            for z in range(NZ):
                rows = load(z, tile)
                up = pltpu.roll(rows, H, 0)
                a_ref[pl.ds(base + z * H, 8), :] = jnp.where(even, up, rows)
                b_ref[pl.ds(base + z * H, 8), :] = jnp.where(even, rows, up)


def first_kernel(u_hbm, blend_hbm, cls_hbm, pdt_hbm, femt_hbm, hm_ref, fem_ref, a_ref, b_ref, u_ref, blend_ref, cls_ref, pdt_ref, femt_ref, sem):
    copies = [pltpu.make_async_copy(blend_hbm, blend_ref, sem.at[3]), pltpu.make_async_copy(cls_hbm, cls_ref, sem.at[4])]
    copies += [pltpu.make_async_copy(pdt_hbm, pdt_ref, sem.at[5]), pltpu.make_async_copy(femt_hbm, femt_ref, sem.at[6])]
    moves = [pltpu.make_async_copy(u_hbm.at[c], u_ref.at[c], sem.at[c]) for c in range(3)]
    for copy in copies + moves:
        copy.start()
    for copy in copies:
        copy.wait()
    even = even_mask("tile")
    for z in range(NZ):
        for tile in range(NT):
            blend = blend_ref[z, :, lanes(tile)]
            cls = cls_ref[z, :, lanes(tile)]
            pd = jnp.zeros_like(blend)
            fem = jnp.zeros_like(blend)
            for index in range(NCLASS):
                hit = cls == index
                pd = jnp.where(hit, pdt_ref[index], pd)
                fem = jnp.where(hit, femt_ref[index], fem)
            hm_ref[z, tile] = 0.5 * (pd * blend)
            fem_ref[z, tile] = fem * (1.0 - blend)
    for copy in moves:
        copy.wait()
    loaders = [lambda z, t, c=c: u_ref[c, z, :, lanes(t)] for c in range(3)]
    loaders.append(lambda z, t: hm_ref[z, t])
    pack_y(loaders, even, a_ref, b_ref)
    for tile in range(NT):
        base = 4 * NT * YRUN + tile * NZ
        for z in range(NZ):
            up = pltpu.roll(fem_ref[z, tile], 1, 0)
            a_ref[pl.ds(base + z, 8), :] = up
            b_ref[pl.ds(base + z, 8), :] = up


def spread_kernel(nfields, after_ref, *refs):
    if nfields == 5:
        u_ref, hm_ref, fem_ref, ra_ref, rb_ref, ext_ref, extm_ref, a_ref, b_ref = refs
    else:
        u_ref, ra_ref, rb_ref, ext_ref, a_ref, b_ref = refs
    sub = lax.broadcasted_iota(jnp.int32, (8, LANES), 0)
    even = even_mask("tile")
    even_z = even_mask("seg")
    nrun = min(nfields, 4)
    for index in range(nrun):
        for tile in range(NT):
            base = (tile * nrun + index) * YRUN
            for z in range(NZ):
                rows = u_ref[index, z, :, lanes(tile)] if index < 3 else hm_ref[z, tile]
                turned = pltpu.roll(rows, H, 0)
                got_a = ra_ref[pl.ds(base + z * H, 8), :]
                got_b = rb_ref[pl.ds(base + z * H, 8), :]
                lo = jnp.where(even, got_b, got_a)
                hi = pltpu.roll(jnp.where(even, got_a, got_b), H, 0)
                dst = ext_ref.at[index, z, tile] if index < 3 else extm_ref.at[0, z, tile]
                dst[pl.ds(0, 8), :] = jnp.where(sub < H, lo, turned)
                dst[pl.ds(8, 8), :] = jnp.where(sub < H, turned, hi)
    if nfields == 5:
        for tile in range(NT):
            base = 4 * NT * YRUN + tile * NZ
            for z in range(NZ):
                turned = pltpu.roll(fem_ref[z, tile], H, 0)
                lo = jnp.where(even, rb_ref[pl.ds(base + z, 8), :], ra_ref[pl.ds(base + z, 8), :])
                lo = pltpu.roll(lo, H - 1, 0)
                extm_ref[1, z, tile, pl.ds(0, 8), :] = jnp.where(sub < H, lo, turned)
                extm_ref[1, z, tile, pl.ds(8, 8), :] = turned

    def put(row, up, down):
        a_ref[pl.ds(row, 8), :] = jnp.where(even_z, up, down)
        b_ref[pl.ds(row, 8), :] = jnp.where(even_z, down, up)

    for index in range(nrun):
        for tile in range(NT):
            base = (index * NT + tile) * ZRUN
            src = (lambda z: ext_ref.at[index, z, tile]) if index < 3 else (lambda z: extm_ref.at[0, z, tile])
            put(base, src(5)[pl.ds(3, 8), :], src(2)[pl.ds(3, 8), :])
            for place, zu, zd in ((8, 6, 1), (20, 7, 0)):
                put(base + place, src(zu)[pl.ds(1, 8), :], src(zd)[pl.ds(1, 8), :])
                put(base + place + 4, src(zu)[pl.ds(5, 8), :], src(zd)[pl.ds(5, 8), :])
    if nfields == 5:
        for tile in range(NT):
            base = 4 * NT * ZRUN + tile * FRUN
            for row in (0, 1):
                up = extm_ref[1, NZ - 1, tile, pl.ds(2 + row, 8), :]
                put(base + row, up, up)


def unpack_z(dst, even_z, ra_ref, rb_ref, run):
    base = run * ZRUN

    def get(z_lo, z_hi, row, place):
        got_a = ra_ref[pl.ds(base + place, 8), :]
        got_b = rb_ref[pl.ds(base + place, 8), :]
        dst(z_lo)[pl.ds(row, 8), :] = jnp.where(even_z, got_b, got_a)
        dst(z_hi)[pl.ds(row, 8), :] = jnp.where(even_z, got_a, got_b)

    get(0, 13, 3, 0)
    for place, z_lo, z_hi in ((8, 1, 12), (20, 2, 11)):
        get(z_lo, z_hi, 1, place)
        get(z_lo, z_hi, 5, place + 4)


def x_modes(here, after, edge):
    nxt = pltpu.roll(jnp.where(edge, after, here), LANES - 1, 1)
    return here + nxt, nxt - here


def y_modes(low, high):
    return (low[0] + high[0], low[1] + high[1], high[0] - low[0], high[1] - low[1])


def fem_layers(modes_of, e_of, close, first_layer, layers, emit):
    def finish(c, z, low, high):
        parts = []
        for which in range(len(low or high)):
            if low is None:
                parts.append(high[which])
            elif high is None:
                parts.append(low[which])
            else:
                parts.append([low[which][m] + high[which][m] for m in range(4)])
        x_s, x_d = close(parts)
        emit(c, z, x_s - x_d, x_s + x_d)

    for c in range(3):
        before = None
        carried = None
        for z in range(first_layer, first_layer + layers + 1):
            now = modes_of(c, z)
            if before is not None:
                lower, upper = [], []
                for which in range(len(now)):
                    e = e_of(z - 1, which)
                    e1, e2, e3 = e * (1.0 / 16.0), e * (1.0 / 24.0), e * (1.0 / 48.0)
                    lo, hi = before[which], now[which]
                    d_ss = e1 * (hi[0] - lo[0])
                    s_dx, d_dx = e1 * (lo[1] + hi[1]), e2 * (hi[1] - lo[1])
                    s_dy, d_dy = e1 * (lo[2] + hi[2]), e2 * (hi[2] - lo[2])
                    s_dd, d_dd = e2 * (lo[3] + hi[3]), e3 * (hi[3] - lo[3])
                    lower.append((-d_ss, s_dx - d_dx, s_dy - d_dy, s_dd - d_dd))
                    upper.append((d_ss, s_dx + d_dx, s_dy + d_dy, s_dd + d_dd))
                if z - 1 >= 0:
                    finish(c, z - 1, carried, lower)
                carried = upper
            before = now
        last = first_layer + layers
        if last < NZ:
            finish(c, last, carried, None)


def roll_out(dst, field, lane, left, here, right, reach_x=H):
    bake = field == 2
    dst(0)[...] = here
    for d in range(1, reach_x + 1):
        up = pltpu.roll(jnp.where(lane < d, right, here), LANES - d, 1)
        down = pltpu.roll(jnp.where(lane >= LANES - d, left, here), d, 1)
        dst(d)[...] = up + float(d) if bake else up
        dst(-d)[...] = down - float(d) if bake else down


def reach(lane, left, here, right):
    edge = jnp.maximum(jnp.where(lane >= LANES - H, left, 0.0), jnp.where(lane < H, right, 0.0))
    return jnp.maximum(here, edge)


def bond_sum(moved, center, hm, dz, bonds, acc):
    base = {0: center[0] - dz, 2: center[2]}
    mids = {}
    for _, dy, dx, norm in bonds:
        if dy not in mids:
            mids[dy] = center[1] - float(dy) if dy else center[1]
        rel = [moved(0, dy, dx) - base[0], moved(1, dy, dx) - mids[dy], moved(2, dy, dx) - base[2]]
        m = hm + moved(3, dy, dx)
        square = rel[0] * rel[0] + rel[1] * rel[1] + rel[2] * rel[2]
        factor = m * (1.0 / math.sqrt(norm) - lax.rsqrt(square))
        for c in range(3):
            acc[c] = acc[c] + factor * rel[c]
    return acc


def inside(center_of, moved_of, f_ref, tile, bonds, chunk):
    def run(step, size, first, dz, span):
        for k in range(span):
            z = first + k
            center, hm = center_of(z)
            acc = [f_ref[c, z, tile] for c in range(3)]
            acc = bond_sum(lambda f, dy, dx: moved_of(f, dy, dx, z + step), center, hm, dz, bonds[size], acc)
            for c in range(3):
                f_ref[c, z, tile] = acc[c]

    def level(part, carry):
        run(0, 0, part * chunk, 0.0, chunk)
        return carry

    lax.fori_loop(0, NZ // chunk, level, 0)
    for size in range(1, H + 1):
        if not bonds[size]:
            continue

        def both(side, carry, size=size):
            step = size - 2 * size * side
            run(step, size, size * side, step.astype(F32), NZ - size)
            return carry

        lax.fori_loop(0, 2, both, 0)


def neighbours(load, tile):
    here = load(tile)
    left = jnp.where(tile > 0, load(jnp.maximum(tile - 1, 0)), 0.0)
    right = jnp.where(tile < NT - 1, load(jnp.minimum(tile + 1, NT - 1)), 0.0)
    return left, here, right


def columns(tile):
    return pl.ds(pl.multiple_of(tile * LANES, LANES), LANES)


def flat_kernel(u_ref, hm_ref, fem_ref, f_ref, p_ref, q_ref, sr):
    lane = lax.broadcasted_iota(jnp.int32, (8, LANES), 1)
    sub = lax.broadcasted_iota(jnp.int32, (8, LANES), 0)
    zero = jnp.zeros((8, LANES), F32)

    def field(f, z):
        if f < 3:
            return lambda t: u_ref[f, z, :, columns(t)]
        return lambda t: hm_ref[z, t]

    def per_tile(tile, carry):
        after = jnp.minimum(tile + 1, NT - 1)
        more = tile < NT - 1

        def modes_of(c, z):
            low = x_modes(u_ref[c, z, :, columns(tile)], jnp.where(more, u_ref[c, z, :, columns(after)], 0.0), lane < 1)
            high = [pltpu.roll(part, 7, 0) for part in low]
            return [y_modes(low, high)]

        def e_of(z, which):
            return jnp.where(sub < 7, fem_ref[z, tile], 0.0)

        def close(parts):
            (a,) = parts
            return (a[0] - a[2]) + pltpu.roll(a[0] + a[2], 1, 0), (a[1] - a[3]) + pltpu.roll(a[1] + a[3], 1, 0)

        def emit(c, z, p, q):
            p_ref[c, z, tile] = p
            q_ref[c, z, tile] = q

        fem_layers(modes_of, e_of, close, 0, NZ - 1, emit)

        most = zero
        for z in range(NZ):
            most = jnp.maximum(most, reach(lane, *neighbours(field(3, z), tile)))
            for c in range(3):
                f_ref[c, z, tile] = zero

        @pl.when(jnp.max(most) > 0.0)
        def _():
            def build(z, c2):
                for f in range(4):
                    roll_out(lambda d: sr.at[f, H + d, z], f, lane, *neighbours(field(f, z), tile))
                return c2

            lax.fori_loop(0, NZ, build, 0, unroll=UNROLL)
            inside(
                lambda z: ([sr[c, H, z] for c in range(3)], sr[3, H, z]),
                lambda f, dy, dx, z: sr[f, H + dx, z],
                f_ref,
                tile,
                FLAT,
                FLAT_CHUNK,
            )

        return carry

    lax.fori_loop(0, NT, per_tile, 0)


def tilted_kernel(ext_ref, extm_ref, fin_ref, pin_ref, qin_ref, f_ref, p_ref, q_ref, sr):
    lane = lax.broadcasted_iota(jnp.int32, (8, LANES), 1)
    sub = lax.broadcasted_iota(jnp.int32, (8, LANES), 0)
    zero = jnp.zeros((8, LANES), F32)

    def field(f, z, row):
        if f < 3:
            return lambda t: ext_ref[f, z, t, pl.ds(row, 8), :]
        return lambda t: extm_ref[0, z, t, pl.ds(row, 8), :]

    def per_tile(tile, carry):
        after = jnp.minimum(tile + 1, NT - 1)
        more = tile < NT - 1

        def far(c, z, t):
            return jnp.where(sub < 4, ext_ref[c, z, t, pl.ds(2, 8), :], ext_ref[c, z, t, pl.ds(4, 8), :])

        def modes_of(c, z):
            near_after = jnp.where(more, ext_ref[c, z, after, pl.ds(H, 8), :], 0.0)
            far_after = jnp.where(more, far(c, z, after), 0.0)
            near = x_modes(ext_ref[c, z, tile, pl.ds(H, 8), :], near_after, lane < 1)
            return [y_modes(x_modes(far(c, z, tile), far_after, lane < 1), near)]

        def e_of(z, which):
            top = jnp.where(sub == 7, extm_ref[1, z, tile, pl.ds(H, 8), :], 0.0)
            return jnp.where(sub == 0, extm_ref[1, z, tile, pl.ds(2, 8), :], top)

        def emit(c, z, p, q):
            p_ref[c, z, tile] = pin_ref[c, z, tile] + p
            q_ref[c, z, tile] = qin_ref[c, z, tile] + q

        fem_layers(modes_of, e_of, lambda parts: (parts[0][0] + parts[0][2], parts[0][1] + parts[0][3]), 0, NZ - 1, emit)
        most = zero
        for z in range(NZ):
            for c in range(3):
                f_ref[c, z, tile] = fin_ref[c, z, tile]
            for row in (0, 6):
                most = jnp.maximum(most, reach(lane, *neighbours(field(3, z, row), tile)))

        @pl.when(jnp.max(most) > 0.0)
        def _():
            def build(z, c2):
                for f in range(4):
                    for half in (0, 8):
                        got = neighbours(field(f, z, half), tile)
                        roll_out(lambda d: sr.at[f, 2 + d, z, pl.ds(half, 8)], f, lane, *got, reach_x=2)
                return c2

            lax.fori_loop(0, NZ, build, 0, unroll=UNROLL)
            inside(
                lambda z: ([sr[c, 2, z, pl.ds(H, 8), :] for c in range(3)], sr[3, 2, z, pl.ds(H, 8), :]),
                lambda f, dy, dx, z: sr[f, 2 + dx, z, pl.ds(H + dy, 8), :],
                f_ref,
                tile,
                TILTED,
                TILTED_CHUNK,
            )

        return carry

    lax.fori_loop(0, NT, per_tile, 0)


def last_kernel(last, u_ref, v_ref, load_ref, ext_ref, extm_ref, ura_ref, urb_ref, mra_ref, mrb_ref, f_ref, p_ref, q_ref, *refs):
    if last:
        u_hbm, v_hbm, sz, fe, sr, fx, px, qx, nu_ref, nv_ref, sem = refs
    else:
        nu_ref, nv_ref, a_ref, b_ref, sz, fe, sr, fx, px, qx = refs
    even = even_mask("tile")
    even_z = even_mask("seg")
    lane = lax.broadcasted_iota(jnp.int32, (8, LANES), 1)
    zero = jnp.zeros((8, LANES), F32)
    spot = {0: 0, 1: 1, 2: 2, 11: 3, 12: 4, 13: 5}
    for tile in range(NT):
        for z in range(2 * H):
            for half in (0, 8):
                sz[3, z, tile, pl.ds(half, 8), :] = zero
        for f in range(4):
            ra, rb = (ura_ref, urb_ref) if f < 3 else (mra_ref, mrb_ref)
            unpack_z(lambda z: sz.at[f, spot[z], tile], even_z, ra, rb, f * NT + tile)
        base = 4 * NT * ZRUN + tile * FRUN
        for row in (0, 1):
            fe[tile, pl.ds(2 + row, 8), :] = jnp.where(
                even_z, mrb_ref[pl.ds(base + row, 8), :], mra_ref[pl.ds(base + row, 8), :]
            )

    def out_copies(tile):
        out = []
        for index, (src, dst) in enumerate(((nu_ref, u_hbm), (nv_ref, v_hbm))):
            view = (slice(None), slice(None), slice(None), columns(tile))
            out.append(pltpu.make_async_copy(src.at[view], dst.at[view], sem.at[index, tile]))
        return out

    def per_tile(tile, carry):
        after = jnp.minimum(tile + 1, NT - 1)
        more = tile < NT - 1

        def load(c, z, row, side):
            t = tile if side == 0 else after
            if z < 0:
                got = sz[c, H + z, t, pl.ds(row, 8), :]
            elif z >= NZ:
                got = sz[c, z - NZ + H, t, pl.ds(row, 8), :]
            else:
                got = ext_ref[c, z, t, pl.ds(row, 8), :]
            return got if side == 0 else jnp.where(more, got, 0.0)

        def modes_of(c, z):
            level = [x_modes(load(c, z, row, 0), load(c, z, row, 1), lane < 1) for row in (2, 3, 4)]
            return [y_modes(level[1], level[2]), y_modes(level[0], level[1])]

        def close(parts):
            a, b = parts
            return (a[0] - a[2]) + (b[0] + b[2]), (a[1] - a[3]) + (b[1] + b[3])

        def emit(c, z, p, q):
            px[c, 0 if z == 0 else 1, tile] = p
            qx[c, 0 if z == 0 else 1, tile] = q

        def e_low(z, which):
            return fe[tile, pl.ds(H - which, 8), :]

        def e_high(z, which):
            return extm_ref[1, NZ - 1, tile, pl.ds(H - which, 8), :]

        fem_layers(modes_of, e_low, close, -1, 1, emit)
        fem_layers(modes_of, e_high, close, NZ - 1, 1, emit)

        most = zero
        for z in range(2 * H):
            for row in (0, 6):
                got = neighbours(lambda t: sz[3, z, t, pl.ds(row, 8), :], tile)
                most = jnp.maximum(most, reach(lane, *got))
        for z in (0, 1, 2, 5, 6, 7):
            most = jnp.maximum(most, extm_ref[0, z, tile, pl.ds(H, 8), :])
            for c in range(3):
                fx[c, z if z < H else z - 2, tile] = zero

        @pl.when(jnp.max(most) > 0.0)
        def _():
            def build(z, c2):
                for f in range(4):
                    for half in (0, 8):
                        got = neighbours(lambda t: sz[f, z, t, pl.ds(half, 8), :], tile)
                        roll_out(lambda d: sr.at[f, 2 + d, z, pl.ds(half, 8)], f, lane, *got, reach_x=2)
                return c2

            for f in range(4):
                for z in (0, 2 * H - 1):
                    sr[f, 2, z, pl.ds(H, 8), :] = sz[f, z, tile, pl.ds(H, 8), :]
            lax.fori_loop(1, 2 * H - 1, build, 0, unroll=UNROLL)

            def side_loop(side, c2):
                sign = 2 * side - 1
                for k in range(H):
                    z = k + side * (NZ - 1 - 2 * k)
                    center = [ext_ref[c, z, tile, pl.ds(H, 8), :] for c in range(3)]
                    hm = extm_ref[0, z, tile, pl.ds(H, 8), :]
                    acc = [zero] * 3
                    for size in range(k + 1, H + 1):
                        place = (H - (size - k)) + side * (2 * (size - k) - 1)
                        acc = bond_sum(
                            lambda f, dy, dx: sr[f, 2 + dx, place, pl.ds(H + dy, 8), :],
                            center,
                            hm,
                            (sign * size).astype(F32),
                            FLAT[size] + TILTED[size],
                            acc,
                        )
                    for c in range(3):
                        fx[c, k + side * (2 * H - 1 - 2 * k), tile] = acc[c]
                return c2

            lax.fori_loop(0, 2, side_loop, 0)

        before = jnp.maximum(tile - 1, 0)
        for c in range(3):
            for z in range(NZ):
                p, q, f = p_ref[c, z, tile], q_ref[c, z, tile], f_ref[c, z, tile]
                shifted = q_ref[c, z, before]
                if z in (0, NZ - 1):
                    p = p + px[c, 0 if z == 0 else 1, tile]
                    q = q + qx[c, 0 if z == 0 else 1, tile]
                    shifted = shifted + qx[c, 0 if z == 0 else 1, before]
                if z < H or z >= NZ - H:
                    f = f + fx[c, z if z < H else z - 2, tile]
                shifted = jnp.where(tile > 0, shifted, 0.0)
                moved = pltpu.roll(jnp.where(lane == LANES - 1, shifted, q), 1, 1)
                force = f - (p + moved)
                where = (c, z, slice(None), columns(tile))
                v = v_ref[where] + 0.25 * (force + load_ref[where])
                u = u_ref[where] + 0.01 * v
                nv_ref[where] = v
                nu_ref[where] = u
                if not last:
                    row = (tile * 3 + c) * YRUN + z * H
                    up = pltpu.roll(u, H, 0)
                    a_ref[pl.ds(row, 8), :] = jnp.where(even, up, u)
                    b_ref[pl.ds(row, 8), :] = jnp.where(even, u, up)
        if last:
            for copy in out_copies(tile):
                copy.start()
        return carry

    lax.fori_loop(0, NT, per_tile, 0)
    if last:
        for tile in range(NT):
            for copy in out_copies(tile):
                copy.wait()


def shape(*dims):
    return jax.ShapeDtypeStruct(dims, F32)


def swap(axis, a, b):
    count = lax.axis_size(axis)

    def pairs(first):
        out = []
        for i in range(first, count - 1, 2):
            out += [(i, i + 1), (i + 1, i)]
        return out

    got_b = lax.ppermute(b, axis, pairs(1))
    return lax.ppermute(a, axis, pairs(0)), got_b


YROWS = 3 * NT * YRUN + 8
ZROWS = 3 * NT * ZRUN
YROWS5 = 4 * NT * YRUN + NT * NZ + 8
ZROWS5 = 4 * NT * ZRUN + 40


def call(kernel, name, outs, ins, scratch=(), work=1, out_space=vmem, more=()):
    return pl.pallas_call(
        kernel,
        out_shape=tuple(outs),
        in_specs=[anywhere() if kind == "a" else vmem() for kind in ins],
        out_specs=tuple(out_space() for _ in outs),
        scratch_shapes=[pltpu.VMEM(dims, F32) for dims in scratch] + list(more),
        compiler_params=params(),
        cost_estimate=pl.CostEstimate(flops=work * 1000000, bytes_accessed=work * 1000000, transcendentals=0),
        name=name,
    )


def body(displacement, velocity, load, blend, classes, pd_table, fem_table):
    whole = shape(3, NZ, NY, NT * LANES)
    tiles = shape(3, NZ, NT, 8, LANES)
    ext_shape = shape(3, NZ, NT, 16, LANES)
    one = shape(NZ, NT, 8, LANES)
    block = (3, NZ, NY, NT * LANES)
    hm, fem, a, b = pl.pallas_call(
        first_kernel,
        out_shape=(one, one, shape(YROWS5, LANES), shape(YROWS5, LANES)),
        in_specs=[anywhere()] * 5,
        out_specs=(vmem(),) * 4,
        scratch_shapes=[
            pltpu.VMEM(block, F32),
            pltpu.VMEM(block[1:], F32),
            pltpu.VMEM(block[1:], jnp.int32),
            pltpu.SMEM((NCLASS,), F32),
            pltpu.SMEM((NCLASS,), F32),
            pltpu.SemaphoreType.DMA((7,)),
        ],
        compiler_params=pltpu.CompilerParams(vmem_limit_bytes=FIRST_LIMIT),
        name="moduli",
    )(displacement, blend, classes, pd_table, fem_table)
    u, v = displacement, velocity
    extm = mra = mrb = None
    for step in range(STEPS):
        last = step == STEPS - 1
        ra, rb = swap("tile", a, b)
        f, p, q = call(
            flat_kernel, f"flat_{step}", (tiles, tiles, tiles), "vvv", [(4, 2 * H + 1, NZ, 8, LANES)], 4
        )(u, hm, fem)
        if step == 0:
            outs = (ext_shape, shape(2, NZ, NT, 16, LANES), shape(ZROWS5, LANES), shape(ZROWS5, LANES))
            ext, extm, a, b = call(functools.partial(spread_kernel, 5), "spread_0", outs, "avvvvv")(f, u, hm, fem, ra, rb)
        else:
            outs = (ext_shape, shape(ZROWS, LANES), shape(ZROWS, LANES))
            ext, a, b = call(functools.partial(spread_kernel, 3), f"spread_{step}", outs, "avvv")(f, u, ra, rb)
        ra, rb = swap("seg", a, b)
        if step == 0:
            mra, mrb = ra, rb
        f, p, q = call(
            tilted_kernel, f"tilted_{step}", (tiles, tiles, tiles), "vvvvv", [(4, 5, NZ, 16, LANES)], 16
        )(ext, extm, f, p, q)
        outs = [whole, whole]
        if not last:
            outs += [shape(YROWS, LANES)] * 2
        scratch = [
            (4, 2 * H, NT, 16, LANES),
            (NT, 16, LANES),
            (4, 5, 2 * H, 16, LANES),
            (3, 2 * H, NT, 8, LANES),
            (3, 2, NT, 8, LANES),
            (3, 2, NT, 8, LANES),
        ]
        more = ()
        if last:
            scratch += [block, block]
            more = (pltpu.SemaphoreType.DMA((2, NT)),)
        space = anywhere if last else vmem
        got = call(functools.partial(last_kernel, last), f"finish_{step}", outs, "v" * 12, scratch, 4, space, more)(
            u, v, load, ext, extm, ra, rb, mra, mrb, f, p, q
        )
        u, v = got[:2]
        if not last:
            a, b = got[2:]
    return u, v


def solution(mesh):
    cells = P(None, "seg", "tile", None)
    plane = P("seg", "tile", None)
    return jax.shard_map(
        body,
        mesh=mesh,
        in_specs=(cells, cells, cells, plane, plane, P(), P()),
        out_specs=(cells, cells),
        check_vma=False,
    )
```

```python
import functools
import math

import jax
import jax.numpy as jnp
from jax import lax
from jax.experimental import pallas as pl
from jax.experimental.pallas import tpu as pltpu
from jax.sharding import PartitionSpec as P

H = 3
STEPS = 2
NCLASS = 4
NZ = 8
NY = 8
NT = 4
LANES = 128
F32 = jnp.float32

YRUN = NZ * H
ZRUN = 32
FRUN = 9
UNROLL = 2
FLAT_CHUNK = 8
TILTED_CHUNK = 4
UNROLL3 = 2


def offsets():
    out = []
    for dz in range(-H, H + 1):
        for dy in range(-H, H + 1):
            for dx in range(-H, H + 1):
                n = dz * dz + dy * dy + dx * dx
                if 0 < n <= H * H:
                    out.append((dz, dy, dx, n))
    return out


OFFSETS = offsets()
FLAT = {dz: [o for o in OFFSETS if o[0] == dz and o[1] == 0] for dz in range(-H, H + 1)}
TILTED = {dz: [o for o in OFFSETS if o[0] == dz and o[1] != 0] for dz in range(-H, H + 1)}


def vmem():
    return pl.BlockSpec(memory_space=pltpu.VMEM)


def anywhere():
    return pl.BlockSpec(memory_space=pl.ANY)


def params():
    return pltpu.CompilerParams(
        vmem_limit_bytes=24 * 1024 * 1024,
    )


def lanes(tile):
    return pl.ds(tile * LANES, LANES)


def even_mask(axis):
    return jnp.full((8, LANES), lax.axis_index(axis) % 2, jnp.int32) == 0


def pack_y(fields, even, a_ref, b_ref):
    for tile in range(NT):
        for index, load in enumerate(fields):
            base = (tile * len(fields) + index) * YRUN
            for z in range(NZ):
                rows = load(z, tile)
                up = pltpu.roll(rows, H, 0)
                a_ref[pl.ds(base + z * H, 8), :] = jnp.where(even, up, rows)
                b_ref[pl.ds(base + z * H, 8), :] = jnp.where(even, rows, up)


def first_kernel(u_hbm, blend_hbm, cls_hbm, pdt_hbm, femt_hbm, u_ref, hm_ref, fem_ref, a_ref, b_ref, blend_ref, cls_ref, pdt_ref, femt_ref, sem):
    copies = [pltpu.make_async_copy(blend_hbm, blend_ref, sem.at[3]), pltpu.make_async_copy(cls_hbm, cls_ref, sem.at[4])]
    copies += [pltpu.make_async_copy(pdt_hbm, pdt_ref, sem.at[5]), pltpu.make_async_copy(femt_hbm, femt_ref, sem.at[6])]
    moves = [pltpu.make_async_copy(u_hbm.at[c], u_ref.at[c], sem.at[c]) for c in range(3)]
    for copy in copies + moves:
        copy.start()
    for copy in copies:
        copy.wait()
    even = even_mask("tile")
    for z in range(NZ):
        for tile in range(NT):
            blend = blend_ref[z, :, lanes(tile)]
            cls = cls_ref[z, :, lanes(tile)]
            pd = jnp.zeros_like(blend)
            fem = jnp.zeros_like(blend)
            for index in range(NCLASS):
                hit = cls == index
                pd = jnp.where(hit, pdt_ref[index], pd)
                fem = jnp.where(hit, femt_ref[index], fem)
            hm_ref[z, tile] = 0.5 * (pd * blend)
            fem_ref[z, tile] = fem * (1.0 - blend)
    for copy in moves:
        copy.wait()
    loaders = [lambda z, t, c=c: u_ref[c, z, :, lanes(t)] for c in range(3)]
    loaders.append(lambda z, t: hm_ref[z, t])
    pack_y(loaders, even, a_ref, b_ref)
    for tile in range(NT):
        base = 4 * NT * YRUN + tile * NZ
        for z in range(NZ):
            up = pltpu.roll(fem_ref[z, tile], 1, 0)
            a_ref[pl.ds(base + z, 8), :] = up
            b_ref[pl.ds(base + z, 8), :] = up


def spread_kernel(nfields, after_ref, *refs):
    if nfields == 5:
        u_ref, hm_ref, fem_ref, ra_ref, rb_ref, ext_ref, extm_ref, a_ref, b_ref = refs
    else:
        u_ref, ra_ref, rb_ref, ext_ref, a_ref, b_ref = refs
    sub = lax.broadcasted_iota(jnp.int32, (8, LANES), 0)
    even = even_mask("tile")
    even_z = even_mask("seg")
    nrun = min(nfields, 4)
    for index in range(nrun):
        for tile in range(NT):
            base = (tile * nrun + index) * YRUN
            for z in range(NZ):
                rows = u_ref[index, z, :, lanes(tile)] if index < 3 else hm_ref[z, tile]
                turned = pltpu.roll(rows, H, 0)
                got_a = ra_ref[pl.ds(base + z * H, 8), :]
                got_b = rb_ref[pl.ds(base + z * H, 8), :]
                lo = jnp.where(even, got_b, got_a)
                hi = pltpu.roll(jnp.where(even, got_a, got_b), H, 0)
                dst = ext_ref.at[index, z, tile] if index < 3 else extm_ref.at[0, z, tile]
                dst[pl.ds(0, 8), :] = jnp.where(sub < H, lo, turned)
                dst[pl.ds(8, 8), :] = jnp.where(sub < H, turned, hi)
    if nfields == 5:
        for tile in range(NT):
            base = 4 * NT * YRUN + tile * NZ
            for z in range(NZ):
                turned = pltpu.roll(fem_ref[z, tile], H, 0)
                lo = jnp.where(even, rb_ref[pl.ds(base + z, 8), :], ra_ref[pl.ds(base + z, 8), :])
                lo = pltpu.roll(lo, H - 1, 0)
                extm_ref[1, z, tile, pl.ds(0, 8), :] = jnp.where(sub < H, lo, turned)
                extm_ref[1, z, tile, pl.ds(8, 8), :] = turned

    def put(row, up, down):
        a_ref[pl.ds(row, 8), :] = jnp.where(even_z, up, down)
        b_ref[pl.ds(row, 8), :] = jnp.where(even_z, down, up)

    for index in range(nrun):
        for tile in range(NT):
            base = (index * NT + tile) * ZRUN
            src = (lambda z: ext_ref.at[index, z, tile]) if index < 3 else (lambda z: extm_ref.at[0, z, tile])
            put(base, src(5)[pl.ds(3, 8), :], src(2)[pl.ds(3, 8), :])
            for place, zu, zd in ((8, 6, 1), (20, 7, 0)):
                put(base + place, src(zu)[pl.ds(1, 8), :], src(zd)[pl.ds(1, 8), :])
                put(base + place + 4, src(zu)[pl.ds(5, 8), :], src(zd)[pl.ds(5, 8), :])
    if nfields == 5:
        for tile in range(NT):
            base = 4 * NT * ZRUN + tile * FRUN
            for row in (0, 1):
                up = extm_ref[1, NZ - 1, tile, pl.ds(2 + row, 8), :]
                put(base + row, up, up)


def unpack_z(dst, even_z, ra_ref, rb_ref, run):
    base = run * ZRUN

    def get(z_lo, z_hi, row, place):
        got_a = ra_ref[pl.ds(base + place, 8), :]
        got_b = rb_ref[pl.ds(base + place, 8), :]
        dst(z_lo)[pl.ds(row, 8), :] = jnp.where(even_z, got_b, got_a)
        dst(z_hi)[pl.ds(row, 8), :] = jnp.where(even_z, got_a, got_b)

    get(0, 13, 3, 0)
    for place, z_lo, z_hi in ((8, 1, 12), (20, 2, 11)):
        get(z_lo, z_hi, 1, place)
        get(z_lo, z_hi, 5, place + 4)


def x_modes(here, after, edge):
    nxt = pltpu.roll(jnp.where(edge, after, here), LANES - 1, 1)
    return here + nxt, nxt - here


def y_modes(low, high):
    return (low[0] + high[0], low[1] + high[1], high[0] - low[0], high[1] - low[1])


def fem_layers(modes_of, e_of, close, first_layer, layers, emit):
    def finish(c, z, low, high):
        parts = []
        for which in range(len(low or high)):
            if low is None:
                parts.append(high[which])
            elif high is None:
                parts.append(low[which])
            else:
                parts.append([low[which][m] + high[which][m] for m in range(4)])
        x_s, x_d = close(parts)
        emit(c, z, x_s - x_d, x_s + x_d)

    for c in range(3):
        before = None
        carried = None
        for z in range(first_layer, first_layer + layers + 1):
            now = modes_of(c, z)
            if before is not None:
                lower, upper = [], []
                for which in range(len(now)):
                    e = e_of(z - 1, which)
                    e1, e2, e3 = e * (1.0 / 16.0), e * (1.0 / 24.0), e * (1.0 / 48.0)
                    lo, hi = before[which], now[which]
                    d_ss = e1 * (hi[0] - lo[0])
                    s_dx, d_dx = e1 * (lo[1] + hi[1]), e2 * (hi[1] - lo[1])
                    s_dy, d_dy = e1 * (lo[2] + hi[2]), e2 * (hi[2] - lo[2])
                    s_dd, d_dd = e2 * (lo[3] + hi[3]), e3 * (hi[3] - lo[3])
                    lower.append((-d_ss, s_dx - d_dx, s_dy - d_dy, s_dd - d_dd))
                    upper.append((d_ss, s_dx + d_dx, s_dy + d_dy, s_dd + d_dd))
                if z - 1 >= 0:
                    finish(c, z - 1, carried, lower)
                carried = upper
            before = now
        last = first_layer + layers
        if last < NZ:
            finish(c, last, carried, None)


def roll_out(dst, field, lane, left, here, right, reach_x=H):
    bake = field == 2
    dst(0)[...] = here
    for d in range(1, reach_x + 1):
        up = pltpu.roll(jnp.where(lane < d, right, here), LANES - d, 1)
        down = pltpu.roll(jnp.where(lane >= LANES - d, left, here), d, 1)
        dst(d)[...] = up + float(d) if bake else up
        dst(-d)[...] = down - float(d) if bake else down


def reach(lane, left, here, right):
    edge = jnp.maximum(jnp.where(lane >= LANES - H, left, 0.0), jnp.where(lane < H, right, 0.0))
    return jnp.maximum(here, edge)


def bond_sum(moved, center, hm, dz, bonds, acc):
    base = {0: center[0] - dz, 2: center[2]}
    mids = {}
    for _, dy, dx, norm in bonds:
        if dy not in mids:
            mids[dy] = center[1] - float(dy) if dy else center[1]
        rel = [moved(0, dy, dx) - base[0], moved(1, dy, dx) - mids[dy], moved(2, dy, dx) - base[2]]
        m = hm + moved(3, dy, dx)
        square = rel[0] * rel[0] + rel[1] * rel[1] + rel[2] * rel[2]
        factor = m * (1.0 / math.sqrt(norm) - lax.rsqrt(square))
        for c in range(3):
            acc[c] = acc[c] + factor * rel[c]
    return acc


def inside(center_of, moved_of, f_ref, tile, bonds, chunk):
    def run(step, size, first, dz, span):
        for k in range(span):
            z = first + k
            center, hm = center_of(z)
            acc = [f_ref[c, z, tile] for c in range(3)]
            acc = bond_sum(lambda f, dy, dx: moved_of(f, dy, dx, z + step), center, hm, dz, bonds[size], acc)
            for c in range(3):
                f_ref[c, z, tile] = acc[c]

    def level(part, carry):
        run(0, 0, part * chunk, 0.0, chunk)
        return carry

    lax.fori_loop(0, NZ // chunk, level, 0)
    for size in range(1, H + 1):
        if not bonds[size]:
            continue

        def both(side, carry, size=size):
            step = size - 2 * size * side
            run(step, size, size * side, step.astype(F32), NZ - size)
            return carry

        lax.fori_loop(0, 2, both, 0)


def neighbours(load, tile):
    here = load(tile)
    left = jnp.where(tile > 0, load(jnp.maximum(tile - 1, 0)), 0.0)
    right = jnp.where(tile < NT - 1, load(jnp.minimum(tile + 1, NT - 1)), 0.0)
    return left, here, right


def columns(tile):
    return pl.ds(pl.multiple_of(tile * LANES, LANES), LANES)


def flat_kernel(u_ref, hm_ref, fem_ref, f_ref, p_ref, q_ref, sr):
    lane = lax.broadcasted_iota(jnp.int32, (8, LANES), 1)
    sub = lax.broadcasted_iota(jnp.int32, (8, LANES), 0)
    zero = jnp.zeros((8, LANES), F32)

    def field(f, z):
        if f < 3:
            return lambda t: u_ref[f, z, :, columns(t)]
        return lambda t: hm_ref[z, t]

    def per_tile(tile, carry):
        after = jnp.minimum(tile + 1, NT - 1)
        more = tile < NT - 1

        def modes_of(c, z):
            low = x_modes(u_ref[c, z, :, columns(tile)], jnp.where(more, u_ref[c, z, :, columns(after)], 0.0), lane < 1)
            high = [pltpu.roll(part, 7, 0) for part in low]
            return [y_modes(low, high)]

        def e_of(z, which):
            return jnp.where(sub < 7, fem_ref[z, tile], 0.0)

        def close(parts):
            (a,) = parts
            return (a[0] - a[2]) + pltpu.roll(a[0] + a[2], 1, 0), (a[1] - a[3]) + pltpu.roll(a[1] + a[3], 1, 0)

        def emit(c, z, p, q):
            p_ref[c, z, tile] = p
            q_ref[c, z, tile] = q

        fem_layers(modes_of, e_of, close, 0, NZ - 1, emit)

        most = zero
        for z in range(NZ):
            most = jnp.maximum(most, reach(lane, *neighbours(field(3, z), tile)))
            for c in range(3):
                f_ref[c, z, tile] = zero

        @pl.when(jnp.max(most) > 0.0)
        def _():
            def build(z, c2):
                for f in range(4):
                    roll_out(lambda d: sr.at[f, H + d, z], f, lane, *neighbours(field(f, z), tile))
                return c2

            lax.fori_loop(0, NZ, build, 0, unroll=UNROLL)
            inside(
                lambda z: ([sr[c, H, z] for c in range(3)], sr[3, H, z]),
                lambda f, dy, dx, z: sr[f, H + dx, z],
                f_ref,
                tile,
                FLAT,
                FLAT_CHUNK,
            )

        return carry

    lax.fori_loop(0, NT, per_tile, 0)


def tilted_kernel(ext_ref, extm_ref, fin_ref, pin_ref, qin_ref, f_ref, p_ref, q_ref, sr):
    lane = lax.broadcasted_iota(jnp.int32, (8, LANES), 1)
    sub = lax.broadcasted_iota(jnp.int32, (8, LANES), 0)
    zero = jnp.zeros((8, LANES), F32)

    def field(f, z, row):
        if f < 3:
            return lambda t: ext_ref[f, z, t, pl.ds(row, 8), :]
        return lambda t: extm_ref[0, z, t, pl.ds(row, 8), :]

    def per_tile(tile, carry):
        after = jnp.minimum(tile + 1, NT - 1)
        more = tile < NT - 1

        def far(c, z, t):
            return jnp.where(sub < 4, ext_ref[c, z, t, pl.ds(2, 8), :], ext_ref[c, z, t, pl.ds(4, 8), :])

        def modes_of(c, z):
            near_after = jnp.where(more, ext_ref[c, z, after, pl.ds(H, 8), :], 0.0)
            far_after = jnp.where(more, far(c, z, after), 0.0)
            near = x_modes(ext_ref[c, z, tile, pl.ds(H, 8), :], near_after, lane < 1)
            return [y_modes(x_modes(far(c, z, tile), far_after, lane < 1), near)]

        def e_of(z, which):
            top = jnp.where(sub == 7, extm_ref[1, z, tile, pl.ds(H, 8), :], 0.0)
            return jnp.where(sub == 0, extm_ref[1, z, tile, pl.ds(2, 8), :], top)

        def emit(c, z, p, q):
            p_ref[c, z, tile] = pin_ref[c, z, tile] + p
            q_ref[c, z, tile] = qin_ref[c, z, tile] + q

        fem_layers(modes_of, e_of, lambda parts: (parts[0][0] + parts[0][2], parts[0][1] + parts[0][3]), 0, NZ - 1, emit)
        most = zero
        for z in range(NZ):
            for c in range(3):
                f_ref[c, z, tile] = fin_ref[c, z, tile]
            for row in (0, 6):
                most = jnp.maximum(most, reach(lane, *neighbours(field(3, z, row), tile)))

        @pl.when(jnp.max(most) > 0.0)
        def _():
            def build(z, c2):
                for f in range(4):
                    for half in (0, 8):
                        got = neighbours(field(f, z, half), tile)
                        roll_out(lambda d: sr.at[f, 2 + d, z, pl.ds(half, 8)], f, lane, *got, reach_x=2)
                return c2

            lax.fori_loop(0, NZ, build, 0, unroll=UNROLL)
            inside(
                lambda z: ([sr[c, 2, z, pl.ds(H, 8), :] for c in range(3)], sr[3, 2, z, pl.ds(H, 8), :]),
                lambda f, dy, dx, z: sr[f, 2 + dx, z, pl.ds(H + dy, 8), :],
                f_ref,
                tile,
                TILTED,
                TILTED_CHUNK,
            )

        return carry

    lax.fori_loop(0, NT, per_tile, 0)


def last_kernel(last, u_ref, v_ref, load_ref, ext_ref, extm_ref, ura_ref, urb_ref, mra_ref, mrb_ref, f_ref, p_ref, q_ref, *refs):
    if last:
        u_hbm, v_hbm, sz, fe, sr, fx, px, qx, nu_ref, nv_ref, sem = refs
    else:
        nu_ref, nv_ref, a_ref, b_ref, sz, fe, sr, fx, px, qx = refs
    even = even_mask("tile")
    even_z = even_mask("seg")
    lane = lax.broadcasted_iota(jnp.int32, (8, LANES), 1)
    zero = jnp.zeros((8, LANES), F32)
    spot = {0: 0, 1: 1, 2: 2, 11: 3, 12: 4, 13: 5}
    for tile in range(NT):
        for z in range(2 * H):
            for half in (0, 8):
                sz[3, z, tile, pl.ds(half, 8), :] = zero
        for f in range(4):
            ra, rb = (ura_ref, urb_ref) if f < 3 else (mra_ref, mrb_ref)
            unpack_z(lambda z: sz.at[f, spot[z], tile], even_z, ra, rb, f * NT + tile)
        base = 4 * NT * ZRUN + tile * FRUN
        for row in (0, 1):
            fe[tile, pl.ds(2 + row, 8), :] = jnp.where(
                even_z, mrb_ref[pl.ds(base + row, 8), :], mra_ref[pl.ds(base + row, 8), :]
            )

    def out_copies(tile):
        out = []
        for index, (src, dst) in enumerate(((nu_ref, u_hbm), (nv_ref, v_hbm))):
            view = (slice(None), slice(None), slice(None), columns(tile))
            out.append(pltpu.make_async_copy(src.at[view], dst.at[view], sem.at[index, tile]))
        return out

    def per_tile(tile, carry):
        after = jnp.minimum(tile + 1, NT - 1)
        more = tile < NT - 1

        def load(c, z, row, side):
            t = tile if side == 0 else after
            if z < 0:
                got = sz[c, H + z, t, pl.ds(row, 8), :]
            elif z >= NZ:
                got = sz[c, z - NZ + H, t, pl.ds(row, 8), :]
            else:
                got = ext_ref[c, z, t, pl.ds(row, 8), :]
            return got if side == 0 else jnp.where(more, got, 0.0)

        def modes_of(c, z):
            level = [x_modes(load(c, z, row, 0), load(c, z, row, 1), lane < 1) for row in (2, 3, 4)]
            return [y_modes(level[1], level[2]), y_modes(level[0], level[1])]

        def close(parts):
            a, b = parts
            return (a[0] - a[2]) + (b[0] + b[2]), (a[1] - a[3]) + (b[1] + b[3])

        def emit(c, z, p, q):
            px[c, 0 if z == 0 else 1, tile] = p
            qx[c, 0 if z == 0 else 1, tile] = q

        def e_low(z, which):
            return fe[tile, pl.ds(H - which, 8), :]

        def e_high(z, which):
            return extm_ref[1, NZ - 1, tile, pl.ds(H - which, 8), :]

        fem_layers(modes_of, e_low, close, -1, 1, emit)
        fem_layers(modes_of, e_high, close, NZ - 1, 1, emit)

        most = zero
        for z in range(2 * H):
            for row in (0, 6):
                got = neighbours(lambda t: sz[3, z, t, pl.ds(row, 8), :], tile)
                most = jnp.maximum(most, reach(lane, *got))
        for z in (0, 1, 2, 5, 6, 7):
            most = jnp.maximum(most, extm_ref[0, z, tile, pl.ds(H, 8), :])
            for c in range(3):
                fx[c, z if z < H else z - 2, tile] = zero

        @pl.when(jnp.max(most) > 0.0)
        def _():
            def build(z, c2):
                for f in range(4):
                    for half in (0, 8):
                        got = neighbours(lambda t: sz[f, z, t, pl.ds(half, 8), :], tile)
                        roll_out(lambda d: sr.at[f, 2 + d, z, pl.ds(half, 8)], f, lane, *got, reach_x=2)
                return c2

            for f in range(4):
                for z in (0, 2 * H - 1):
                    sr[f, 2, z, pl.ds(H, 8), :] = sz[f, z, tile, pl.ds(H, 8), :]
            lax.fori_loop(1, 2 * H - 1, build, 0, unroll=UNROLL)

            def side_loop(side, c2):
                sign = 2 * side - 1
                for k in range(H):
                    z = k + side * (NZ - 1 - 2 * k)
                    center = [ext_ref[c, z, tile, pl.ds(H, 8), :] for c in range(3)]
                    hm = extm_ref[0, z, tile, pl.ds(H, 8), :]
                    acc = [zero] * 3
                    for size in range(k + 1, H + 1):
                        place = (H - (size - k)) + side * (2 * (size - k) - 1)
                        acc = bond_sum(
                            lambda f, dy, dx: sr[f, 2 + dx, place, pl.ds(H + dy, 8), :],
                            center,
                            hm,
                            (sign * size).astype(F32),
                            FLAT[size] + TILTED[size],
                            acc,
                        )
                    for c in range(3):
                        fx[c, k + side * (2 * H - 1 - 2 * k), tile] = acc[c]
                return c2

            lax.fori_loop(0, 2, side_loop, 0)

        before = jnp.maximum(tile - 1, 0)
        for c in range(3):
            for z in range(NZ):
                p, q, f = p_ref[c, z, tile], q_ref[c, z, tile], f_ref[c, z, tile]
                shifted = q_ref[c, z, before]
                if z in (0, NZ - 1):
                    p = p + px[c, 0 if z == 0 else 1, tile]
                    q = q + qx[c, 0 if z == 0 else 1, tile]
                    shifted = shifted + qx[c, 0 if z == 0 else 1, before]
                if z < H or z >= NZ - H:
                    f = f + fx[c, z if z < H else z - 2, tile]
                shifted = jnp.where(tile > 0, shifted, 0.0)
                moved = pltpu.roll(jnp.where(lane == LANES - 1, shifted, q), 1, 1)
                force = f - (p + moved)
                where = (c, z, slice(None), columns(tile))
                v = v_ref[where] + 0.25 * (force + load_ref[where])
                u = u_ref[where] + 0.01 * v
                nv_ref[where] = v
                nu_ref[where] = u
                if not last:
                    row = (tile * 3 + c) * YRUN + z * H
                    up = pltpu.roll(u, H, 0)
                    a_ref[pl.ds(row, 8), :] = jnp.where(even, up, u)
                    b_ref[pl.ds(row, 8), :] = jnp.where(even, u, up)
        if last:
            for copy in out_copies(tile):
                copy.start()
        return carry

    lax.fori_loop(0, NT, per_tile, 0)
    if last:
        for tile in range(NT):
            for copy in out_copies(tile):
                copy.wait()


def shape(*dims):
    return jax.ShapeDtypeStruct(dims, F32)


def swap(axis, a, b):
    count = lax.axis_size(axis)

    def pairs(first):
        out = []
        for i in range(first, count - 1, 2):
            out += [(i, i + 1), (i + 1, i)]
        return out

    got_b = lax.ppermute(b, axis, pairs(1))
    return lax.ppermute(a, axis, pairs(0)), got_b


YROWS = 3 * NT * YRUN + 8
ZROWS = 3 * NT * ZRUN
YROWS5 = 4 * NT * YRUN + NT * NZ + 8
ZROWS5 = 4 * NT * ZRUN + 40


def call(kernel, name, outs, ins, scratch=(), work=1, out_space=vmem, more=()):
    return pl.pallas_call(
        kernel,
        out_shape=tuple(outs),
        in_specs=[anywhere() if kind == "a" else vmem() for kind in ins],
        out_specs=tuple(out_space() for _ in outs),
        scratch_shapes=[pltpu.VMEM(dims, F32) for dims in scratch] + list(more),
        compiler_params=params(),
        cost_estimate=pl.CostEstimate(flops=work * 1000000, bytes_accessed=work * 1000000, transcendentals=0),
        name=name,
    )


def body(displacement, velocity, load, blend, classes, pd_table, fem_table):
    whole = shape(3, NZ, NY, NT * LANES)
    tiles = shape(3, NZ, NT, 8, LANES)
    ext_shape = shape(3, NZ, NT, 16, LANES)
    one = shape(NZ, NT, 8, LANES)
    block = (3, NZ, NY, NT * LANES)
    inputs = [
        pltpu.with_memory_space_constraint(x, pltpu.MemorySpace.HBM)
        for x in (displacement, blend, classes, pd_table, fem_table)
    ]
    u, hm, fem, a, b = pl.pallas_call(
        first_kernel,
        out_shape=(whole, one, one, shape(YROWS5, LANES), shape(YROWS5, LANES)),
        in_specs=[pl.BlockSpec(memory_space=pltpu.MemorySpace.HBM)] * 5,
        out_specs=(vmem(),) * 5,
        scratch_shapes=[
            pltpu.VMEM(block[1:], F32),
            pltpu.VMEM(block[1:], jnp.int32),
            pltpu.SMEM((NCLASS,), F32),
            pltpu.SMEM((NCLASS,), F32),
            pltpu.SemaphoreType.DMA((7,)),
        ],
        compiler_params=params(),
        name="moduli",
    )(*inputs)
    v = velocity
    extm = mra = mrb = None
    for step in range(STEPS):
        last = step == STEPS - 1
        ra, rb = swap("tile", a, b)
        f, p, q = call(
            flat_kernel, f"flat_{step}", (tiles, tiles, tiles), "vvv", [(4, 2 * H + 1, NZ, 8, LANES)], 4
        )(u, hm, fem)
        if step == 0:
            outs = (ext_shape, shape(2, NZ, NT, 16, LANES), shape(ZROWS5, LANES), shape(ZROWS5, LANES))
            ext, extm, a, b = call(functools.partial(spread_kernel, 5), "spread_0", outs, "avvvvv")(f, u, hm, fem, ra, rb)
        else:
            outs = (ext_shape, shape(ZROWS, LANES), shape(ZROWS, LANES))
            ext, a, b = call(functools.partial(spread_kernel, 3), f"spread_{step}", outs, "avvv")(f, u, ra, rb)
        ra, rb = swap("seg", a, b)
        if step == 0:
            mra, mrb = ra, rb
        f, p, q = call(
            tilted_kernel, f"tilted_{step}", (tiles, tiles, tiles), "vvvvv", [(4, 5, NZ, 16, LANES)], 16
        )(ext, extm, f, p, q)
        outs = [whole, whole]
        if not last:
            outs += [shape(YROWS, LANES)] * 2
        scratch = [
            (4, 2 * H, NT, 16, LANES),
            (NT, 16, LANES),
            (4, 5, 2 * H, 16, LANES),
            (3, 2 * H, NT, 8, LANES),
            (3, 2, NT, 8, LANES),
            (3, 2, NT, 8, LANES),
        ]
        more = ()
        if last:
            scratch += [block, block]
            more = (pltpu.SemaphoreType.DMA((2, NT)),)
        space = anywhere if last else vmem
        got = call(functools.partial(last_kernel, last), f"finish_{step}", outs, "v" * 12, scratch, 4, space, more)(
            u, v, load, ext, extm, ra, rb, mra, mrb, f, p, q
        )
        u, v = got[:2]
        if not last:
            a, b = got[2:]
    return u, v


def solution(mesh):
    cells = P(None, "seg", "tile", None)
    plane = P("seg", "tile", None)
    return jax.shard_map(
        body,
        mesh=mesh,
        in_specs=(cells, cells, cells, plane, plane, P(), P()),
        out_specs=(cells, cells),
        check_vma=False,
    )
```

```python
import functools
import math

import jax
import jax.numpy as jnp
from jax import lax
from jax.experimental import pallas as pl
from jax.experimental.pallas import tpu as pltpu
from jax.sharding import PartitionSpec as P

H = 3
STEPS = 2
NCLASS = 4
NZ = 8
NY = 8
NT = 4
LANES = 128
F32 = jnp.float32

YRUN = NZ * H
ZRUN = 32
FRUN = 9
UNROLL = 2
FLAT_CHUNK = 8
TILTED_CHUNK = 4
UNROLL3 = 2


def offsets():
    out = []
    for dz in range(-H, H + 1):
        for dy in range(-H, H + 1):
            for dx in range(-H, H + 1):
                n = dz * dz + dy * dy + dx * dx
                if 0 < n <= H * H:
                    out.append((dz, dy, dx, n))
    return out


OFFSETS = offsets()
FLAT = {dz: [o for o in OFFSETS if o[0] == dz and o[1] == 0] for dz in range(-H, H + 1)}
TILTED = {dz: [o for o in OFFSETS if o[0] == dz and o[1] != 0] for dz in range(-H, H + 1)}


def vmem():
    return pl.BlockSpec(memory_space=pltpu.VMEM)


def anywhere():
    return pl.BlockSpec(memory_space=pl.ANY)


def params():
    return pltpu.CompilerParams(
        vmem_limit_bytes=24 * 1024 * 1024,
    )


def lanes(tile):
    return pl.ds(tile * LANES, LANES)


def even_mask(axis):
    return jnp.full((8, LANES), lax.axis_index(axis) % 2, jnp.int32) == 0


def pack_y(fields, even, a_ref, b_ref):
    for tile in range(NT):
        for index, load in enumerate(fields):
            base = (tile * len(fields) + index) * YRUN
            for z in range(NZ):
                rows = load(z, tile)
                up = pltpu.roll(rows, H, 0)
                a_ref[pl.ds(base + z * H, 8), :] = jnp.where(even, up, rows)
                b_ref[pl.ds(base + z * H, 8), :] = jnp.where(even, rows, up)


def first_kernel(u_hbm, blend_hbm, cls_hbm, pdt_hbm, femt_hbm, u_ref, hm_ref, fem_ref, a_ref, b_ref, blend_ref, cls_ref, pdt_ref, femt_ref, sem):
    copies = [pltpu.make_async_copy(blend_hbm, blend_ref, sem.at[3]), pltpu.make_async_copy(cls_hbm, cls_ref, sem.at[4])]
    copies += [pltpu.make_async_copy(pdt_hbm, pdt_ref, sem.at[5]), pltpu.make_async_copy(femt_hbm, femt_ref, sem.at[6])]
    moves = [pltpu.make_async_copy(u_hbm.at[c], u_ref.at[c], sem.at[c]) for c in range(3)]
    for copy in copies + moves:
        copy.start()
    for copy in copies:
        copy.wait()
    even = even_mask("tile")
    for z in range(NZ):
        for tile in range(NT):
            blend = blend_ref[z, :, lanes(tile)]
            cls = cls_ref[z, :, lanes(tile)]
            pd = jnp.zeros_like(blend)
            fem = jnp.zeros_like(blend)
            for index in range(NCLASS):
                hit = cls == index
                pd = jnp.where(hit, pdt_ref[index], pd)
                fem = jnp.where(hit, femt_ref[index], fem)
            hm_ref[z, tile] = 0.5 * (pd * blend)
            fem_ref[z, tile] = fem * (1.0 - blend)
    for copy in moves:
        copy.wait()
    loaders = [lambda z, t, c=c: u_ref[c, z, :, lanes(t)] for c in range(3)]
    loaders.append(lambda z, t: hm_ref[z, t])
    pack_y(loaders, even, a_ref, b_ref)
    for tile in range(NT):
        base = 4 * NT * YRUN + tile * NZ
        for z in range(NZ):
            up = pltpu.roll(fem_ref[z, tile], 1, 0)
            a_ref[pl.ds(base + z, 8), :] = up
            b_ref[pl.ds(base + z, 8), :] = up


def spread_kernel(nfields, after_ref, *refs):
    if nfields == 5:
        u_ref, hm_ref, fem_ref, ra_ref, rb_ref, ext_ref, extm_ref, a_ref, b_ref = refs
    else:
        u_ref, ra_ref, rb_ref, ext_ref, a_ref, b_ref = refs
    sub = lax.broadcasted_iota(jnp.int32, (8, LANES), 0)
    even = even_mask("tile")
    even_z = even_mask("seg")
    nrun = min(nfields, 4)
    for index in range(nrun):
        for tile in range(NT):
            base = (tile * nrun + index) * YRUN
            for z in range(NZ):
                rows = u_ref[index, z, :, lanes(tile)] if index < 3 else hm_ref[z, tile]
                turned = pltpu.roll(rows, H, 0)
                got_a = ra_ref[pl.ds(base + z * H, 8), :]
                got_b = rb_ref[pl.ds(base + z * H, 8), :]
                lo = jnp.where(even, got_b, got_a)
                hi = pltpu.roll(jnp.where(even, got_a, got_b), H, 0)
                dst = ext_ref.at[index, z, tile] if index < 3 else extm_ref.at[0, z, tile]
                dst[pl.ds(0, 8), :] = jnp.where(sub < H, lo, turned)
                dst[pl.ds(8, 8), :] = jnp.where(sub < H, turned, hi)
    if nfields == 5:
        for tile in range(NT):
            base = 4 * NT * YRUN + tile * NZ
            for z in range(NZ):
                turned = pltpu.roll(fem_ref[z, tile], H, 0)
                lo = jnp.where(even, rb_ref[pl.ds(base + z, 8), :], ra_ref[pl.ds(base + z, 8), :])
                lo = pltpu.roll(lo, H - 1, 0)
                extm_ref[1, z, tile, pl.ds(0, 8), :] = jnp.where(sub < H, lo, turned)
                extm_ref[1, z, tile, pl.ds(8, 8), :] = turned

    def put(row, up, down):
        a_ref[pl.ds(row, 8), :] = jnp.where(even_z, up, down)
        b_ref[pl.ds(row, 8), :] = jnp.where(even_z, down, up)

    for index in range(nrun):
        for tile in range(NT):
            base = (index * NT + tile) * ZRUN
            src = (lambda z: ext_ref.at[index, z, tile]) if index < 3 else (lambda z: extm_ref.at[0, z, tile])
            put(base, src(5)[pl.ds(3, 8), :], src(2)[pl.ds(3, 8), :])
            for place, zu, zd in ((8, 6, 1), (20, 7, 0)):
                put(base + place, src(zu)[pl.ds(1, 8), :], src(zd)[pl.ds(1, 8), :])
                put(base + place + 4, src(zu)[pl.ds(5, 8), :], src(zd)[pl.ds(5, 8), :])
    if nfields == 5:
        for tile in range(NT):
            base = 4 * NT * ZRUN + tile * FRUN
            for row in (0, 1):
                up = extm_ref[1, NZ - 1, tile, pl.ds(2 + row, 8), :]
                put(base + row, up, up)


def unpack_z(dst, even_z, ra_ref, rb_ref, run):
    base = run * ZRUN

    def get(z_lo, z_hi, row, place):
        got_a = ra_ref[pl.ds(base + place, 8), :]
        got_b = rb_ref[pl.ds(base + place, 8), :]
        dst(z_lo)[pl.ds(row, 8), :] = jnp.where(even_z, got_b, got_a)
        dst(z_hi)[pl.ds(row, 8), :] = jnp.where(even_z, got_a, got_b)

    get(0, 13, 3, 0)
    for place, z_lo, z_hi in ((8, 1, 12), (20, 2, 11)):
        get(z_lo, z_hi, 1, place)
        get(z_lo, z_hi, 5, place + 4)


def x_modes(here, after, edge):
    nxt = pltpu.roll(jnp.where(edge, after, here), LANES - 1, 1)
    return here + nxt, nxt - here


def y_modes(low, high):
    return (low[0] + high[0], low[1] + high[1], high[0] - low[0], high[1] - low[1])


def fem_layers(modes_of, e_of, close, first_layer, layers, emit):
    def finish(c, z, low, high):
        parts = []
        for which in range(len(low or high)):
            if low is None:
                parts.append(high[which])
            elif high is None:
                parts.append(low[which])
            else:
                parts.append([low[which][m] + high[which][m] for m in range(4)])
        x_s, x_d = close(parts)
        emit(c, z, x_s - x_d, x_s + x_d)

    for c in range(3):
        before = None
        carried = None
        for z in range(first_layer, first_layer + layers + 1):
            now = modes_of(c, z)
            if before is not None:
                lower, upper = [], []
                for which in range(len(now)):
                    e = e_of(z - 1, which)
                    e1, e2, e3 = e * (1.0 / 16.0), e * (1.0 / 24.0), e * (1.0 / 48.0)
                    lo, hi = before[which], now[which]
                    d_ss = e1 * (hi[0] - lo[0])
                    s_dx, d_dx = e1 * (lo[1] + hi[1]), e2 * (hi[1] - lo[1])
                    s_dy, d_dy = e1 * (lo[2] + hi[2]), e2 * (hi[2] - lo[2])
                    s_dd, d_dd = e2 * (lo[3] + hi[3]), e3 * (hi[3] - lo[3])
                    lower.append((-d_ss, s_dx - d_dx, s_dy - d_dy, s_dd - d_dd))
                    upper.append((d_ss, s_dx + d_dx, s_dy + d_dy, s_dd + d_dd))
                if z - 1 >= 0:
                    finish(c, z - 1, carried, lower)
                carried = upper
            before = now
        last = first_layer + layers
        if last < NZ:
            finish(c, last, carried, None)


def roll_out(dst, field, lane, left, here, right, reach_x=H):
    bake = field == 2
    dst(0)[...] = here
    for d in range(1, reach_x + 1):
        up = pltpu.roll(jnp.where(lane < d, right, here), LANES - d, 1)
        down = pltpu.roll(jnp.where(lane >= LANES - d, left, here), d, 1)
        dst(d)[...] = up + float(d) if bake else up
        dst(-d)[...] = down - float(d) if bake else down


def reach(lane, left, here, right):
    edge = jnp.maximum(jnp.where(lane >= LANES - H, left, 0.0), jnp.where(lane < H, right, 0.0))
    return jnp.maximum(here, edge)


def bond_sum(moved, center, hm, dz, bonds, acc):
    base = {0: center[0] - dz, 2: center[2]}
    mids = {}
    for _, dy, dx, norm in bonds:
        if dy not in mids:
            mids[dy] = center[1] - float(dy) if dy else center[1]
        rel = [moved(0, dy, dx) - base[0], moved(1, dy, dx) - mids[dy], moved(2, dy, dx) - base[2]]
        m = hm + moved(3, dy, dx)
        square = rel[0] * rel[0] + rel[1] * rel[1] + rel[2] * rel[2]
        factor = m * (1.0 / math.sqrt(norm) - lax.rsqrt(square))
        for c in range(3):
            acc[c] = acc[c] + factor * rel[c]
    return acc


def inside(center_of, moved_of, f_ref, tile, bonds, chunk):
    def run(step, size, first, dz, span):
        for k in range(span):
            z = first + k
            center, hm = center_of(z)
            acc = [f_ref[c, z, tile] for c in range(3)]
            acc = bond_sum(lambda f, dy, dx: moved_of(f, dy, dx, z + step), center, hm, dz, bonds[size], acc)
            for c in range(3):
                f_ref[c, z, tile] = acc[c]

    def level(part, carry):
        run(0, 0, part * chunk, 0.0, chunk)
        return carry

    lax.fori_loop(0, NZ // chunk, level, 0)
    for size in range(1, H + 1):
        if not bonds[size]:
            continue

        def both(side, carry, size=size):
            step = size - 2 * size * side
            run(step, size, size * side, step.astype(F32), NZ - size)
            return carry

        lax.fori_loop(0, 2, both, 0)


def neighbours(load, tile):
    here = load(tile)
    left = jnp.where(tile > 0, load(jnp.maximum(tile - 1, 0)), 0.0)
    right = jnp.where(tile < NT - 1, load(jnp.minimum(tile + 1, NT - 1)), 0.0)
    return left, here, right


def columns(tile):
    return pl.ds(pl.multiple_of(tile * LANES, LANES), LANES)


def flat_kernel(u_ref, hm_ref, fem_ref, f_ref, p_ref, q_ref, sr):
    lane = lax.broadcasted_iota(jnp.int32, (8, LANES), 1)
    sub = lax.broadcasted_iota(jnp.int32, (8, LANES), 0)
    zero = jnp.zeros((8, LANES), F32)

    def field(f, z):
        if f < 3:
            return lambda t: u_ref[f, z, :, columns(t)]
        return lambda t: hm_ref[z, t]

    def per_tile(tile, carry):
        after = jnp.minimum(tile + 1, NT - 1)
        more = tile < NT - 1

        def modes_of(c, z):
            low = x_modes(u_ref[c, z, :, columns(tile)], jnp.where(more, u_ref[c, z, :, columns(after)], 0.0), lane < 1)
            high = [pltpu.roll(part, 7, 0) for part in low]
            return [y_modes(low, high)]

        def e_of(z, which):
            return jnp.where(sub < 7, fem_ref[z, tile], 0.0)

        def close(parts):
            (a,) = parts
            return (a[0] - a[2]) + pltpu.roll(a[0] + a[2], 1, 0), (a[1] - a[3]) + pltpu.roll(a[1] + a[3], 1, 0)

        def emit(c, z, p, q):
            p_ref[c, z, tile] = p
            q_ref[c, z, tile] = q

        fem_layers(modes_of, e_of, close, 0, NZ - 1, emit)

        most = zero
        for z in range(NZ):
            most = jnp.maximum(most, reach(lane, *neighbours(field(3, z), tile)))
            for c in range(3):
                f_ref[c, z, tile] = zero

        @pl.when(jnp.max(most) > 0.0)
        def _():
            def build(z, c2):
                for f in range(4):
                    roll_out(lambda d: sr.at[f, H + d, z], f, lane, *neighbours(field(f, z), tile))
                return c2

            lax.fori_loop(0, NZ, build, 0, unroll=UNROLL)
            inside(
                lambda z: ([sr[c, H, z] for c in range(3)], sr[3, H, z]),
                lambda f, dy, dx, z: sr[f, H + dx, z],
                f_ref,
                tile,
                FLAT,
                FLAT_CHUNK,
            )

        return carry

    lax.fori_loop(0, NT, per_tile, 0)


def faces(ext_rows, extm_rows, p_rows, q_rows, lane, sub):
    ending = (lane == LANES - 1) & (sub % NT == NT - 1)

    def rows(ref, item, z, row):
        return ref[pl.ds((item * NZ + z) * NT * 16 + row, 8, stride=16), :]

    def pair(ref, item, z, row):
        if z < NZ - 1:
            return rows(ref, item, z, row)
        return pltpu.roll(rows(ref, item, z - 1, row), 4, 0)

    def packed_x_modes(here):
        nxt = pltpu.roll(jnp.where(lane < 1, pltpu.roll(here, 7, 0), here), LANES - 1, 1)
        nxt = jnp.where(ending, 0.0, nxt)
        return here + nxt, nxt - here

    for near, far, row_e, y in ((3, 2, 2, 0), (10, 11, 10, NY - 1)):
        for c in range(3):
            for z in range(0, NZ, 2):
                lo, hi = [
                    y_modes(packed_x_modes(pair(ext_rows, c, n, far)), packed_x_modes(pair(ext_rows, c, n, near)))
                    for n in (z, z + 1)
                ]
                e = rows(extm_rows, 1, z, row_e)
                if z == NZ - 2:
                    e = jnp.where(sub < 4, e, 0.0)
                e1, e2, e3 = e * (1.0 / 16.0), e * (1.0 / 24.0), e * (1.0 / 48.0)
                d_ss = e1 * (hi[0] - lo[0])
                s_dx, d_dx = e1 * (lo[1] + hi[1]), e2 * (hi[1] - lo[1])
                s_dy, d_dy = e1 * (lo[2] + hi[2]), e2 * (hi[2] - lo[2])
                s_dd, d_dd = e2 * (lo[3] + hi[3]), e3 * (hi[3] - lo[3])
                low = ((s_dy - d_dy) - d_ss, (s_dx - d_dx) + (s_dd - d_dd))
                high = ((s_dy + d_dy) + d_ss, (s_dx + d_dx) + (s_dd + d_dd))
                if z == NZ - 2:
                    high = [pltpu.roll(part, 4, 0) for part in high]
                    low = [low[k] + high[k] for k in range(2)]
                    todo = ((z, low),)
                else:
                    todo = ((z, low), (z + 1, high))
                for n, (x_s, x_d) in todo:
                    where = pl.ds((c * NZ + n) * NT * 8 + y, 8, stride=8)
                    p_rows[where, :] = p_rows[where, :] + (x_s - x_d)
                    q_rows[where, :] = q_rows[where, :] + (x_s + x_d)


def tilted_kernel(ext_ref, extm_ref, ext_rows, extm_rows, fin_ref, pin_rows, qin_rows, f_ref, p_rows, q_rows, sr):
    lane = lax.broadcasted_iota(jnp.int32, (8, LANES), 1)
    sub = lax.broadcasted_iota(jnp.int32, (8, LANES), 0)
    zero = jnp.zeros((8, LANES), F32)

    def field(f, z, row):
        if f < 3:
            return lambda t: ext_ref[f, z, t, pl.ds(row, 8), :]
        return lambda t: extm_ref[0, z, t, pl.ds(row, 8), :]

    faces(ext_rows, extm_rows, p_rows, q_rows, lane, sub)

    def per_tile(tile, carry):
        most = zero
        for z in range(NZ):
            for row in (0, 6):
                most = jnp.maximum(most, reach(lane, *neighbours(field(3, z, row), tile)))

        @pl.when(jnp.max(most) > 0.0)
        def _():
            def build(z, c2):
                for f in range(4):
                    for half in (0, 8):
                        got = neighbours(field(f, z, half), tile)
                        roll_out(lambda d: sr.at[f, 2 + d, z, pl.ds(half, 8)], f, lane, *got, reach_x=2)
                return c2

            lax.fori_loop(0, NZ, build, 0, unroll=UNROLL)
            inside(
                lambda z: ([sr[c, 2, z, pl.ds(H, 8), :] for c in range(3)], sr[3, 2, z, pl.ds(H, 8), :]),
                lambda f, dy, dx, z: sr[f, 2 + dx, z, pl.ds(H + dy, 8), :],
                f_ref,
                tile,
                TILTED,
                TILTED_CHUNK,
            )

        return carry

    lax.fori_loop(0, NT, per_tile, 0)


def last_kernel(last, u_ref, v_ref, load_ref, ext_ref, extm_ref, ura_ref, urb_ref, mra_ref, mrb_ref, f_ref, p_ref, q_ref, *refs):
    if last:
        u_hbm, v_hbm, sz, fe, sr, fx, px, qx, nu_ref, nv_ref, sem = refs
    else:
        nu_ref, nv_ref, a_ref, b_ref, sz, fe, sr, fx, px, qx = refs
    even = even_mask("tile")
    even_z = even_mask("seg")
    lane = lax.broadcasted_iota(jnp.int32, (8, LANES), 1)
    zero = jnp.zeros((8, LANES), F32)
    spot = {0: 0, 1: 1, 2: 2, 11: 3, 12: 4, 13: 5}
    for tile in range(NT):
        for z in range(2 * H):
            for half in (0, 8):
                sz[3, z, tile, pl.ds(half, 8), :] = zero
        for f in range(4):
            ra, rb = (ura_ref, urb_ref) if f < 3 else (mra_ref, mrb_ref)
            unpack_z(lambda z: sz.at[f, spot[z], tile], even_z, ra, rb, f * NT + tile)
        base = 4 * NT * ZRUN + tile * FRUN
        for row in (0, 1):
            fe[tile, pl.ds(2 + row, 8), :] = jnp.where(
                even_z, mrb_ref[pl.ds(base + row, 8), :], mra_ref[pl.ds(base + row, 8), :]
            )

    def out_copies(tile):
        out = []
        for index, (src, dst) in enumerate(((nu_ref, u_hbm), (nv_ref, v_hbm))):
            view = (slice(None), slice(None), slice(None), columns(tile))
            out.append(pltpu.make_async_copy(src.at[view], dst.at[view], sem.at[index, tile]))
        return out

    def per_tile(tile, carry):
        after = jnp.minimum(tile + 1, NT - 1)
        more = tile < NT - 1

        def load(c, z, row, side):
            t = tile if side == 0 else after
            if z < 0:
                got = sz[c, H + z, t, pl.ds(row, 8), :]
            elif z >= NZ:
                got = sz[c, z - NZ + H, t, pl.ds(row, 8), :]
            else:
                got = ext_ref[c, z, t, pl.ds(row, 8), :]
            return got if side == 0 else jnp.where(more, got, 0.0)

        def modes_of(c, z):
            level = [x_modes(load(c, z, row, 0), load(c, z, row, 1), lane < 1) for row in (2, 3, 4)]
            return [y_modes(level[1], level[2]), y_modes(level[0], level[1])]

        def close(parts):
            a, b = parts
            return (a[0] - a[2]) + (b[0] + b[2]), (a[1] - a[3]) + (b[1] + b[3])

        def emit(c, z, p, q):
            px[c, 0 if z == 0 else 1, tile] = p
            qx[c, 0 if z == 0 else 1, tile] = q

        def e_low(z, which):
            return fe[tile, pl.ds(H - which, 8), :]

        def e_high(z, which):
            return extm_ref[1, NZ - 1, tile, pl.ds(H - which, 8), :]

        fem_layers(modes_of, e_low, close, -1, 1, emit)
        fem_layers(modes_of, e_high, close, NZ - 1, 1, emit)

        most = zero
        for z in range(2 * H):
            for row in (0, 6):
                got = neighbours(lambda t: sz[3, z, t, pl.ds(row, 8), :], tile)
                most = jnp.maximum(most, reach(lane, *got))
        for z in (0, 1, 2, 5, 6, 7):
            most = jnp.maximum(most, extm_ref[0, z, tile, pl.ds(H, 8), :])
            for c in range(3):
                fx[c, z if z < H else z - 2, tile] = zero

        @pl.when(jnp.max(most) > 0.0)
        def _():
            def build(z, c2):
                for f in range(4):
                    for half in (0, 8):
                        got = neighbours(lambda t: sz[f, z, t, pl.ds(half, 8), :], tile)
                        roll_out(lambda d: sr.at[f, 2 + d, z, pl.ds(half, 8)], f, lane, *got, reach_x=2)
                return c2

            for f in range(4):
                for z in (0, 2 * H - 1):
                    sr[f, 2, z, pl.ds(H, 8), :] = sz[f, z, tile, pl.ds(H, 8), :]
            lax.fori_loop(1, 2 * H - 1, build, 0, unroll=UNROLL)

            def side_loop(side, c2):
                sign = 2 * side - 1
                for k in range(H):
                    z = k + side * (NZ - 1 - 2 * k)
                    center = [ext_ref[c, z, tile, pl.ds(H, 8), :] for c in range(3)]
                    hm = extm_ref[0, z, tile, pl.ds(H, 8), :]
                    acc = [zero] * 3
                    for size in range(k + 1, H + 1):
                        place = (H - (size - k)) + side * (2 * (size - k) - 1)
                        acc = bond_sum(
                            lambda f, dy, dx: sr[f, 2 + dx, place, pl.ds(H + dy, 8), :],
                            center,
                            hm,
                            (sign * size).astype(F32),
                            FLAT[size] + TILTED[size],
                            acc,
                        )
                    for c in range(3):
                        fx[c, k + side * (2 * H - 1 - 2 * k), tile] = acc[c]
                return c2

            lax.fori_loop(0, 2, side_loop, 0)

        before = jnp.maximum(tile - 1, 0)
        for c in range(3):
            for z in range(NZ):
                p, q, f = p_ref[c, z, tile], q_ref[c, z, tile], f_ref[c, z, tile]
                shifted = q_ref[c, z, before]
                if z in (0, NZ - 1):
                    p = p + px[c, 0 if z == 0 else 1, tile]
                    q = q + qx[c, 0 if z == 0 else 1, tile]
                    shifted = shifted + qx[c, 0 if z == 0 else 1, before]
                if z < H or z >= NZ - H:
                    f = f + fx[c, z if z < H else z - 2, tile]
                shifted = jnp.where(tile > 0, shifted, 0.0)
                moved = pltpu.roll(jnp.where(lane == LANES - 1, shifted, q), 1, 1)
                force = f - (p + moved)
                where = (c, z, slice(None), columns(tile))
                v = v_ref[where] + 0.25 * (force + load_ref[where])
                u = u_ref[where] + 0.01 * v
                nv_ref[where] = v
                nu_ref[where] = u
                if not last:
                    row = (tile * 3 + c) * YRUN + z * H
                    up = pltpu.roll(u, H, 0)
                    a_ref[pl.ds(row, 8), :] = jnp.where(even, up, u)
                    b_ref[pl.ds(row, 8), :] = jnp.where(even, u, up)
        if last:
            for copy in out_copies(tile):
                copy.start()
        return carry

    lax.fori_loop(0, NT, per_tile, 0)
    if last:
        for tile in range(NT):
            for copy in out_copies(tile):
                copy.wait()


def shape(*dims):
    return jax.ShapeDtypeStruct(dims, F32)


def swap(axis, a, b):
    count = lax.axis_size(axis)

    def pairs(first):
        out = []
        for i in range(first, count - 1, 2):
            out += [(i, i + 1), (i + 1, i)]
        return out

    got_b = lax.ppermute(b, axis, pairs(1))
    return lax.ppermute(a, axis, pairs(0)), got_b


YROWS = 3 * NT * YRUN + 8
ZROWS = 3 * NT * ZRUN
YROWS5 = 4 * NT * YRUN + NT * NZ + 8
ZROWS5 = 4 * NT * ZRUN + 40


def call(kernel, name, outs, ins, scratch=(), work=1, out_space=vmem, more=(), aliases=None):
    return pl.pallas_call(
        kernel,
        out_shape=tuple(outs),
        in_specs=[anywhere() if kind == "a" else vmem() for kind in ins],
        out_specs=tuple(out_space() for _ in outs),
        scratch_shapes=[pltpu.VMEM(dims, F32) for dims in scratch] + list(more),
        compiler_params=params(),
        input_output_aliases=aliases or {},
        cost_estimate=pl.CostEstimate(flops=work * 1000000, bytes_accessed=work * 1000000, transcendentals=0),
        name=name,
    )


def body(displacement, velocity, load, blend, classes, pd_table, fem_table):
    whole = shape(3, NZ, NY, NT * LANES)
    tiles = shape(3, NZ, NT, 8, LANES)
    ext_shape = shape(3, NZ, NT, 16, LANES)
    one = shape(NZ, NT, 8, LANES)
    block = (3, NZ, NY, NT * LANES)
    inputs = [
        pltpu.with_memory_space_constraint(x, pltpu.MemorySpace.HBM)
        for x in (displacement, blend, classes, pd_table, fem_table)
    ]
    u, hm, fem, a, b = pl.pallas_call(
        first_kernel,
        out_shape=(whole, one, one, shape(YROWS5, LANES), shape(YROWS5, LANES)),
        in_specs=[pl.BlockSpec(memory_space=pltpu.MemorySpace.HBM)] * 5,
        out_specs=(vmem(),) * 5,
        scratch_shapes=[
            pltpu.VMEM(block[1:], F32),
            pltpu.VMEM(block[1:], jnp.int32),
            pltpu.SMEM((NCLASS,), F32),
            pltpu.SMEM((NCLASS,), F32),
            pltpu.SemaphoreType.DMA((7,)),
        ],
        compiler_params=params(),
        name="moduli",
    )(*inputs)
    v = velocity
    extm = mra = mrb = None
    for step in range(STEPS):
        last = step == STEPS - 1
        ra, rb = swap("tile", a, b)
        f, p, q = call(
            flat_kernel, f"flat_{step}", (tiles, tiles, tiles), "vvv", [(4, 2 * H + 1, NZ, 8, LANES)], 4
        )(u, hm, fem)
        if step == 0:
            outs = (ext_shape, shape(2, NZ, NT, 16, LANES), shape(ZROWS5, LANES), shape(ZROWS5, LANES))
            ext, extm, a, b = call(functools.partial(spread_kernel, 5), "spread_0", outs, "avvvvv")(f, u, hm, fem, ra, rb)
        else:
            outs = (ext_shape, shape(ZROWS, LANES), shape(ZROWS, LANES))
            ext, a, b = call(functools.partial(spread_kernel, 3), f"spread_{step}", outs, "avvv")(f, u, ra, rb)
        ra, rb = swap("seg", a, b)
        if step == 0:
            mra, mrb = ra, rb
        flat_rows = lambda x: x.reshape(-1, LANES)
        rows_shape = shape(3 * NZ * NT * 8, LANES)
        f, p, q = call(
            tilted_kernel,
            f"tilted_{step}",
            (tiles, rows_shape, rows_shape),
            "v" * 7,
            [(4, 5, NZ, 16, LANES)],
            16,
            aliases={4: 0, 5: 1, 6: 2},
        )(ext, extm, flat_rows(ext), flat_rows(extm), f, flat_rows(p), flat_rows(q))
        p, q = p.reshape(tiles.shape), q.reshape(tiles.shape)
        outs = [whole, whole]
        if not last:
            outs += [shape(YROWS, LANES)] * 2
        scratch = [
            (4, 2 * H, NT, 16, LANES),
            (NT, 16, LANES),
            (4, 5, 2 * H, 16, LANES),
            (3, 2 * H, NT, 8, LANES),
            (3, 2, NT, 8, LANES),
            (3, 2, NT, 8, LANES),
        ]
        more = ()
        if last:
            scratch += [block, block]
            more = (pltpu.SemaphoreType.DMA((2, NT)),)
        space = anywhere if last else vmem
        got = call(functools.partial(last_kernel, last), f"finish_{step}", outs, "v" * 12, scratch, 4, space, more)(
            u, v, load, ext, extm, ra, rb, mra, mrb, f, p, q
        )
        u, v = got[:2]
        if not last:
            a, b = got[2:]
    return u, v


def solution(mesh):
    cells = P(None, "seg", "tile", None)
    plane = P("seg", "tile", None)
    return jax.shard_map(
        body,
        mesh=mesh,
        in_specs=(cells, cells, cells, plane, plane, P(), P()),
        out_specs=(cells, cells),
        check_vma=False,
    )
```

```python
import functools
import math

import jax
import jax.numpy as jnp
from jax import lax
from jax.experimental import pallas as pl
from jax.experimental.pallas import tpu as pltpu
from jax.sharding import PartitionSpec as P

H = 3
STEPS = 2
NCLASS = 4
NZ = 8
NY = 8
NT = 4
LANES = 128
F32 = jnp.float32

YRUN = NZ * H
ZRUN = 32
FRUN = 9
UNROLL = 2
FLAT_CHUNK = 8
TILTED_CHUNK = 4
UNROLL3 = 2


def offsets():
    out = []
    for dz in range(-H, H + 1):
        for dy in range(-H, H + 1):
            for dx in range(-H, H + 1):
                n = dz * dz + dy * dy + dx * dx
                if 0 < n <= H * H:
                    out.append((dz, dy, dx, n))
    return out


OFFSETS = offsets()
FLAT = {dz: [o for o in OFFSETS if o[0] == dz and o[1] == 0] for dz in range(-H, H + 1)}
TILTED = {dz: [o for o in OFFSETS if o[0] == dz and o[1] != 0] for dz in range(-H, H + 1)}


def vmem():
    return pl.BlockSpec(memory_space=pltpu.VMEM)


def anywhere():
    return pl.BlockSpec(memory_space=pl.ANY)


def params():
    return pltpu.CompilerParams(
        vmem_limit_bytes=24 * 1024 * 1024,
    )


def lanes(tile):
    return pl.ds(tile * LANES, LANES)


def a_is_up(axis):
    return jnp.full((8, LANES), lax.axis_index(axis) % 2, jnp.int32) == 1


def pack_y(fields, even, a_ref, b_ref):
    for tile in range(NT):
        for index, load in enumerate(fields):
            base = (tile * len(fields) + index) * YRUN
            for z in range(NZ):
                rows = load(z, tile)
                up = pltpu.roll(rows, H, 0)
                a_ref[pl.ds(base + z * H, 8), :] = jnp.where(even, up, rows)
                b_ref[pl.ds(base + z * H, 8), :] = jnp.where(even, rows, up)


def first_kernel(u_hbm, blend_hbm, cls_hbm, pdt_hbm, femt_hbm, u_ref, hm_ref, fem_ref, a_ref, b_ref, blend_ref, cls_ref, pdt_ref, femt_ref, sem):
    copies = [pltpu.make_async_copy(blend_hbm, blend_ref, sem.at[3]), pltpu.make_async_copy(cls_hbm, cls_ref, sem.at[4])]
    copies += [pltpu.make_async_copy(pdt_hbm, pdt_ref, sem.at[5]), pltpu.make_async_copy(femt_hbm, femt_ref, sem.at[6])]
    moves = [pltpu.make_async_copy(u_hbm.at[c], u_ref.at[c], sem.at[c]) for c in range(3)]
    for copy in copies + moves:
        copy.start()
    for copy in copies:
        copy.wait()
    even = a_is_up("tile")
    for z in range(NZ):
        for tile in range(NT):
            blend = blend_ref[z, :, lanes(tile)]
            cls = cls_ref[z, :, lanes(tile)]
            pd = jnp.zeros_like(blend)
            fem = jnp.zeros_like(blend)
            for index in range(NCLASS):
                hit = cls == index
                pd = jnp.where(hit, pdt_ref[index], pd)
                fem = jnp.where(hit, femt_ref[index], fem)
            hm_ref[z, tile] = 0.5 * (pd * blend)
            fem_ref[z, tile] = fem * (1.0 - blend)
    for copy in moves:
        copy.wait()
    loaders = [lambda z, t, c=c: u_ref[c, z, :, lanes(t)] for c in range(3)]
    loaders.append(lambda z, t: hm_ref[z, t])
    pack_y(loaders, even, a_ref, b_ref)
    for tile in range(NT):
        base = 4 * NT * YRUN + tile * NZ
        for z in range(NZ):
            up = pltpu.roll(fem_ref[z, tile], 1, 0)
            a_ref[pl.ds(base + z, 8), :] = up
            b_ref[pl.ds(base + z, 8), :] = up


def spread_kernel(nfields, after_ref, *refs):
    if nfields == 5:
        u_ref, hm_ref, fem_ref, ra_ref, rb_ref, ext_ref, extm_ref, a_ref, b_ref = refs
    else:
        u_ref, ra_ref, rb_ref, ext_ref, a_ref, b_ref = refs
    sub = lax.broadcasted_iota(jnp.int32, (8, LANES), 0)
    even = a_is_up("tile")
    even_z = a_is_up("seg")
    nrun = min(nfields, 4)
    for index in range(nrun):
        for tile in range(NT):
            base = (tile * nrun + index) * YRUN
            for z in range(NZ):
                rows = u_ref[index, z, :, lanes(tile)] if index < 3 else hm_ref[z, tile]
                turned = pltpu.roll(rows, H, 0)
                got_a = ra_ref[pl.ds(base + z * H, 8), :]
                got_b = rb_ref[pl.ds(base + z * H, 8), :]
                lo = jnp.where(even, got_b, got_a)
                hi = pltpu.roll(jnp.where(even, got_a, got_b), H, 0)
                dst = ext_ref.at[index, z, tile] if index < 3 else extm_ref.at[0, z, tile]
                dst[pl.ds(0, 8), :] = jnp.where(sub < H, lo, turned)
                dst[pl.ds(8, 8), :] = jnp.where(sub < H, turned, hi)
    if nfields == 5:
        for tile in range(NT):
            base = 4 * NT * YRUN + tile * NZ
            for z in range(NZ):
                turned = pltpu.roll(fem_ref[z, tile], H, 0)
                lo = jnp.where(even, rb_ref[pl.ds(base + z, 8), :], ra_ref[pl.ds(base + z, 8), :])
                lo = pltpu.roll(lo, H - 1, 0)
                extm_ref[1, z, tile, pl.ds(0, 8), :] = jnp.where(sub < H, lo, turned)
                extm_ref[1, z, tile, pl.ds(8, 8), :] = turned

    def put(row, up, down):
        a_ref[pl.ds(row, 8), :] = jnp.where(even_z, up, down)
        b_ref[pl.ds(row, 8), :] = jnp.where(even_z, down, up)

    for index in range(nrun):
        for tile in range(NT):
            base = (index * NT + tile) * ZRUN
            src = (lambda z: ext_ref.at[index, z, tile]) if index < 3 else (lambda z: extm_ref.at[0, z, tile])
            put(base, src(5)[pl.ds(3, 8), :], src(2)[pl.ds(3, 8), :])
            for place, zu, zd in ((8, 6, 1), (20, 7, 0)):
                put(base + place, src(zu)[pl.ds(1, 8), :], src(zd)[pl.ds(1, 8), :])
                put(base + place + 4, src(zu)[pl.ds(5, 8), :], src(zd)[pl.ds(5, 8), :])
    if nfields == 5:
        for tile in range(NT):
            base = 4 * NT * ZRUN + tile * FRUN
            for row in (0, 1):
                up = extm_ref[1, NZ - 1, tile, pl.ds(2 + row, 8), :]
                put(base + row, up, up)


def unpack_z(dst, even_z, ra_ref, rb_ref, run):
    base = run * ZRUN

    def get(z_lo, z_hi, row, place):
        got_a = ra_ref[pl.ds(base + place, 8), :]
        got_b = rb_ref[pl.ds(base + place, 8), :]
        dst(z_lo)[pl.ds(row, 8), :] = jnp.where(even_z, got_b, got_a)
        dst(z_hi)[pl.ds(row, 8), :] = jnp.where(even_z, got_a, got_b)

    get(0, 13, 3, 0)
    for place, z_lo, z_hi in ((8, 1, 12), (20, 2, 11)):
        get(z_lo, z_hi, 1, place)
        get(z_lo, z_hi, 5, place + 4)


def x_modes(here, after, edge):
    nxt = pltpu.roll(jnp.where(edge, after, here), LANES - 1, 1)
    return here + nxt, nxt - here


def y_modes(low, high):
    return (low[0] + high[0], low[1] + high[1], high[0] - low[0], high[1] - low[1])


def fem_layers(modes_of, e_of, close, first_layer, layers, emit):
    def finish(c, z, low, high):
        parts = []
        for which in range(len(low or high)):
            if low is None:
                parts.append(high[which])
            elif high is None:
                parts.append(low[which])
            else:
                parts.append([low[which][m] + high[which][m] for m in range(4)])
        x_s, x_d = close(parts)
        emit(c, z, x_s - x_d, x_s + x_d)

    for c in range(3):
        before = None
        carried = None
        for z in range(first_layer, first_layer + layers + 1):
            now = modes_of(c, z)
            if before is not None:
                lower, upper = [], []
                for which in range(len(now)):
                    e = e_of(z - 1, which)
                    e1, e2, e3 = e * (1.0 / 16.0), e * (1.0 / 24.0), e * (1.0 / 48.0)
                    lo, hi = before[which], now[which]
                    d_ss = e1 * (hi[0] - lo[0])
                    s_dx, d_dx = e1 * (lo[1] + hi[1]), e2 * (hi[1] - lo[1])
                    s_dy, d_dy = e1 * (lo[2] + hi[2]), e2 * (hi[2] - lo[2])
                    s_dd, d_dd = e2 * (lo[3] + hi[3]), e3 * (hi[3] - lo[3])
                    lower.append((-d_ss, s_dx - d_dx, s_dy - d_dy, s_dd - d_dd))
                    upper.append((d_ss, s_dx + d_dx, s_dy + d_dy, s_dd + d_dd))
                if z - 1 >= 0:
                    finish(c, z - 1, carried, lower)
                carried = upper
            before = now
        last = first_layer + layers
        if last < NZ:
            finish(c, last, carried, None)


def roll_out(dst, field, lane, left, here, right, reach_x=H):
    bake = field == 2
    dst(0)[...] = here
    for d in range(1, reach_x + 1):
        up = pltpu.roll(jnp.where(lane < d, right, here), LANES - d, 1)
        down = pltpu.roll(jnp.where(lane >= LANES - d, left, here), d, 1)
        dst(d)[...] = up + float(d) if bake else up
        dst(-d)[...] = down - float(d) if bake else down


def reach(lane, left, here, right):
    edge = jnp.maximum(jnp.where(lane >= LANES - H, left, 0.0), jnp.where(lane < H, right, 0.0))
    return jnp.maximum(here, edge)


def bond_sum(moved, center, hm, dz, bonds, acc):
    base = {0: center[0] - dz, 2: center[2]}
    mids = {}
    for _, dy, dx, norm in bonds:
        if dy not in mids:
            mids[dy] = center[1] - float(dy) if dy else center[1]
        rel = [moved(0, dy, dx) - base[0], moved(1, dy, dx) - mids[dy], moved(2, dy, dx) - base[2]]
        m = hm + moved(3, dy, dx)
        square = rel[0] * rel[0] + rel[1] * rel[1] + rel[2] * rel[2]
        factor = m * (1.0 / math.sqrt(norm) - lax.rsqrt(square))
        for c in range(3):
            acc[c] = acc[c] + factor * rel[c]
    return acc


def inside(center_of, moved_of, f_ref, tile, bonds, chunk):
    def run(step, size, first, dz, span):
        for k in range(span):
            z = first + k
            center, hm = center_of(z)
            acc = [f_ref[c, z, tile] for c in range(3)]
            acc = bond_sum(lambda f, dy, dx: moved_of(f, dy, dx, z + step), center, hm, dz, bonds[size], acc)
            for c in range(3):
                f_ref[c, z, tile] = acc[c]

    def level(part, carry):
        run(0, 0, part * chunk, 0.0, chunk)
        return carry

    lax.fori_loop(0, NZ // chunk, level, 0)
    for size in range(1, H + 1):
        if not bonds[size]:
            continue

        def both(side, carry, size=size):
            step = size - 2 * size * side
            run(step, size, size * side, step.astype(F32), NZ - size)
            return carry

        lax.fori_loop(0, 2, both, 0)


def neighbours(load, tile):
    here = load(tile)
    left = jnp.where(tile > 0, load(jnp.maximum(tile - 1, 0)), 0.0)
    right = jnp.where(tile < NT - 1, load(jnp.minimum(tile + 1, NT - 1)), 0.0)
    return left, here, right


def columns(tile):
    return pl.ds(pl.multiple_of(tile * LANES, LANES), LANES)


def flat_kernel(u_ref, hm_ref, fem_ref, f_ref, p_ref, q_ref, sr):
    lane = lax.broadcasted_iota(jnp.int32, (8, LANES), 1)
    sub = lax.broadcasted_iota(jnp.int32, (8, LANES), 0)
    zero = jnp.zeros((8, LANES), F32)

    def field(f, z):
        if f < 3:
            return lambda t: u_ref[f, z, :, columns(t)]
        return lambda t: hm_ref[z, t]

    def per_tile(tile, carry):
        after = jnp.minimum(tile + 1, NT - 1)
        more = tile < NT - 1

        def modes_of(c, z):
            low = x_modes(u_ref[c, z, :, columns(tile)], jnp.where(more, u_ref[c, z, :, columns(after)], 0.0), lane < 1)
            high = [pltpu.roll(part, 7, 0) for part in low]
            return [y_modes(low, high)]

        def e_of(z, which):
            return jnp.where(sub < 7, fem_ref[z, tile], 0.0)

        def close(parts):
            (a,) = parts
            return (a[0] - a[2]) + pltpu.roll(a[0] + a[2], 1, 0), (a[1] - a[3]) + pltpu.roll(a[1] + a[3], 1, 0)

        def emit(c, z, p, q):
            p_ref[c, z, tile] = p
            q_ref[c, z, tile] = q

        fem_layers(modes_of, e_of, close, 0, NZ - 1, emit)

        most = zero
        for z in range(NZ):
            most = jnp.maximum(most, reach(lane, *neighbours(field(3, z), tile)))
            for c in range(3):
                f_ref[c, z, tile] = zero

        @pl.when(jnp.max(most) > 0.0)
        def _():
            def build(z, c2):
                for f in range(4):
                    roll_out(lambda d: sr.at[f, H + d, z], f, lane, *neighbours(field(f, z), tile))
                return c2

            lax.fori_loop(0, NZ, build, 0, unroll=UNROLL)
            inside(
                lambda z: ([sr[c, H, z] for c in range(3)], sr[3, H, z]),
                lambda f, dy, dx, z: sr[f, H + dx, z],
                f_ref,
                tile,
                FLAT,
                FLAT_CHUNK,
            )

        return carry

    lax.fori_loop(0, NT, per_tile, 0)


def faces(ext_rows, extm_rows, p_rows, q_rows, lane, sub):
    ending = (lane == LANES - 1) & (sub % NT == NT - 1)

    def rows(ref, item, z, row):
        return ref[pl.ds((item * NZ + z) * NT * 16 + row, 8, stride=16), :]

    def pair(ref, item, z, row):
        if z < NZ - 1:
            return rows(ref, item, z, row)
        return pltpu.roll(rows(ref, item, z - 1, row), 4, 0)

    def packed_x_modes(here):
        nxt = pltpu.roll(jnp.where(lane < 1, pltpu.roll(here, 7, 0), here), LANES - 1, 1)
        nxt = jnp.where(ending, 0.0, nxt)
        return here + nxt, nxt - here

    for near, far, row_e, y in ((3, 2, 2, 0), (10, 11, 10, NY - 1)):
        for c in range(3):
            for z in range(0, NZ, 2):
                lo, hi = [
                    y_modes(packed_x_modes(pair(ext_rows, c, n, far)), packed_x_modes(pair(ext_rows, c, n, near)))
                    for n in (z, z + 1)
                ]
                e = rows(extm_rows, 1, z, row_e)
                if z == NZ - 2:
                    e = jnp.where(sub < 4, e, 0.0)
                e1, e2, e3 = e * (1.0 / 16.0), e * (1.0 / 24.0), e * (1.0 / 48.0)
                d_ss = e1 * (hi[0] - lo[0])
                s_dx, d_dx = e1 * (lo[1] + hi[1]), e2 * (hi[1] - lo[1])
                s_dy, d_dy = e1 * (lo[2] + hi[2]), e2 * (hi[2] - lo[2])
                s_dd, d_dd = e2 * (lo[3] + hi[3]), e3 * (hi[3] - lo[3])
                low = ((s_dy - d_dy) - d_ss, (s_dx - d_dx) + (s_dd - d_dd))
                high = ((s_dy + d_dy) + d_ss, (s_dx + d_dx) + (s_dd + d_dd))
                if z == NZ - 2:
                    high = [pltpu.roll(part, 4, 0) for part in high]
                    low = [low[k] + high[k] for k in range(2)]
                    todo = ((z, low),)
                else:
                    todo = ((z, low), (z + 1, high))
                for n, (x_s, x_d) in todo:
                    where = pl.ds((c * NZ + n) * NT * 8 + y, 8, stride=8)
                    p_rows[where, :] = p_rows[where, :] + (x_s - x_d)
                    q_rows[where, :] = q_rows[where, :] + (x_s + x_d)


def tilted_kernel(ext_ref, extm_ref, ext_rows, extm_rows, fin_ref, pin_rows, qin_rows, f_ref, p_rows, q_rows, sr):
    lane = lax.broadcasted_iota(jnp.int32, (8, LANES), 1)
    sub = lax.broadcasted_iota(jnp.int32, (8, LANES), 0)
    zero = jnp.zeros((8, LANES), F32)

    def field(f, z, row):
        if f < 3:
            return lambda t: ext_ref[f, z, t, pl.ds(row, 8), :]
        return lambda t: extm_ref[0, z, t, pl.ds(row, 8), :]

    faces(ext_rows, extm_rows, p_rows, q_rows, lane, sub)

    def per_tile(tile, carry):
        most = zero
        for z in range(NZ):
            for row in (0, 6):
                most = jnp.maximum(most, reach(lane, *neighbours(field(3, z, row), tile)))

        @pl.when(jnp.max(most) > 0.0)
        def _():
            def build(z, c2):
                for f in range(4):
                    for half in (0, 8):
                        got = neighbours(field(f, z, half), tile)
                        roll_out(lambda d: sr.at[f, 2 + d, z, pl.ds(half, 8)], f, lane, *got, reach_x=2)
                return c2

            lax.fori_loop(0, NZ, build, 0, unroll=UNROLL)
            inside(
                lambda z: ([sr[c, 2, z, pl.ds(H, 8), :] for c in range(3)], sr[3, 2, z, pl.ds(H, 8), :]),
                lambda f, dy, dx, z: sr[f, 2 + dx, z, pl.ds(H + dy, 8), :],
                f_ref,
                tile,
                TILTED,
                TILTED_CHUNK,
            )

        return carry

    lax.fori_loop(0, NT, per_tile, 0)


def last_kernel(last, u_ref, v_ref, load_ref, ext_ref, extm_ref, ura_ref, urb_ref, mra_ref, mrb_ref, f_ref, p_ref, q_ref, *refs):
    if last:
        u_hbm, v_hbm, sz, fe, sr, fx, px, qx, nu_ref, nv_ref, sem = refs
    else:
        nu_ref, nv_ref, a_ref, b_ref, sz, fe, sr, fx, px, qx = refs
    even = a_is_up("tile")
    even_z = a_is_up("seg")
    lane = lax.broadcasted_iota(jnp.int32, (8, LANES), 1)
    zero = jnp.zeros((8, LANES), F32)
    spot = {0: 0, 1: 1, 2: 2, 11: 3, 12: 4, 13: 5}
    for tile in range(NT):
        for z in range(2 * H):
            for half in (0, 8):
                sz[3, z, tile, pl.ds(half, 8), :] = zero
        for f in range(4):
            ra, rb = (ura_ref, urb_ref) if f < 3 else (mra_ref, mrb_ref)
            unpack_z(lambda z: sz.at[f, spot[z], tile], even_z, ra, rb, f * NT + tile)
        base = 4 * NT * ZRUN + tile * FRUN
        for row in (0, 1):
            fe[tile, pl.ds(2 + row, 8), :] = jnp.where(
                even_z, mrb_ref[pl.ds(base + row, 8), :], mra_ref[pl.ds(base + row, 8), :]
            )

    def out_copies(tile):
        out = []
        for index, (src, dst) in enumerate(((nu_ref, u_hbm), (nv_ref, v_hbm))):
            view = (slice(None), slice(None), slice(None), columns(tile))
            out.append(pltpu.make_async_copy(src.at[view], dst.at[view], sem.at[index, tile]))
        return out

    def per_tile(tile, carry):
        after = jnp.minimum(tile + 1, NT - 1)
        more = tile < NT - 1

        def load(c, z, row, side):
            t = tile if side == 0 else after
            if z < 0:
                got = sz[c, H + z, t, pl.ds(row, 8), :]
            elif z >= NZ:
                got = sz[c, z - NZ + H, t, pl.ds(row, 8), :]
            else:
                got = ext_ref[c, z, t, pl.ds(row, 8), :]
            return got if side == 0 else jnp.where(more, got, 0.0)

        def modes_of(c, z):
            level = [x_modes(load(c, z, row, 0), load(c, z, row, 1), lane < 1) for row in (2, 3, 4)]
            return [y_modes(level[1], level[2]), y_modes(level[0], level[1])]

        def close(parts):
            a, b = parts
            return (a[0] - a[2]) + (b[0] + b[2]), (a[1] - a[3]) + (b[1] + b[3])

        def emit(c, z, p, q):
            px[c, 0 if z == 0 else 1, tile] = p
            qx[c, 0 if z == 0 else 1, tile] = q

        def e_low(z, which):
            return fe[tile, pl.ds(H - which, 8), :]

        def e_high(z, which):
            return extm_ref[1, NZ - 1, tile, pl.ds(H - which, 8), :]

        fem_layers(modes_of, e_low, close, -1, 1, emit)
        fem_layers(modes_of, e_high, close, NZ - 1, 1, emit)

        most = zero
        for z in range(2 * H):
            for row in (0, 6):
                got = neighbours(lambda t: sz[3, z, t, pl.ds(row, 8), :], tile)
                most = jnp.maximum(most, reach(lane, *got))
        for z in (0, 1, 2, 5, 6, 7):
            most = jnp.maximum(most, extm_ref[0, z, tile, pl.ds(H, 8), :])
            for c in range(3):
                fx[c, z if z < H else z - 2, tile] = zero

        @pl.when(jnp.max(most) > 0.0)
        def _():
            def build(z, c2):
                for f in range(4):
                    for half in (0, 8):
                        got = neighbours(lambda t: sz[f, z, t, pl.ds(half, 8), :], tile)
                        roll_out(lambda d: sr.at[f, 2 + d, z, pl.ds(half, 8)], f, lane, *got, reach_x=2)
                return c2

            for f in range(4):
                for z in (0, 2 * H - 1):
                    sr[f, 2, z, pl.ds(H, 8), :] = sz[f, z, tile, pl.ds(H, 8), :]
            lax.fori_loop(1, 2 * H - 1, build, 0, unroll=UNROLL)

            def side_loop(side, c2):
                sign = 2 * side - 1
                for k in range(H):
                    z = k + side * (NZ - 1 - 2 * k)
                    center = [ext_ref[c, z, tile, pl.ds(H, 8), :] for c in range(3)]
                    hm = extm_ref[0, z, tile, pl.ds(H, 8), :]
                    acc = [zero] * 3
                    for size in range(k + 1, H + 1):
                        place = (H - (size - k)) + side * (2 * (size - k) - 1)
                        acc = bond_sum(
                            lambda f, dy, dx: sr[f, 2 + dx, place, pl.ds(H + dy, 8), :],
                            center,
                            hm,
                            (sign * size).astype(F32),
                            FLAT[size] + TILTED[size],
                            acc,
                        )
                    for c in range(3):
                        fx[c, k + side * (2 * H - 1 - 2 * k), tile] = acc[c]
                return c2

            lax.fori_loop(0, 2, side_loop, 0)

        before = jnp.maximum(tile - 1, 0)
        for c in range(3):
            for z in range(NZ):
                p, q, f = p_ref[c, z, tile], q_ref[c, z, tile], f_ref[c, z, tile]
                shifted = q_ref[c, z, before]
                if z in (0, NZ - 1):
                    p = p + px[c, 0 if z == 0 else 1, tile]
                    q = q + qx[c, 0 if z == 0 else 1, tile]
                    shifted = shifted + qx[c, 0 if z == 0 else 1, before]
                if z < H or z >= NZ - H:
                    f = f + fx[c, z if z < H else z - 2, tile]
                shifted = jnp.where(tile > 0, shifted, 0.0)
                moved = pltpu.roll(jnp.where(lane == LANES - 1, shifted, q), 1, 1)
                force = f - (p + moved)
                where = (c, z, slice(None), columns(tile))
                v = v_ref[where] + 0.25 * (force + load_ref[where])
                u = u_ref[where] + 0.01 * v
                nv_ref[where] = v
                nu_ref[where] = u
                if not last:
                    row = (tile * 3 + c) * YRUN + z * H
                    up = pltpu.roll(u, H, 0)
                    a_ref[pl.ds(row, 8), :] = jnp.where(even, up, u)
                    b_ref[pl.ds(row, 8), :] = jnp.where(even, u, up)
        if last:
            for copy in out_copies(tile):
                copy.start()
        return carry

    lax.fori_loop(0, NT, per_tile, 0)
    if last:
        for tile in range(NT):
            for copy in out_copies(tile):
                copy.wait()


def shape(*dims):
    return jax.ShapeDtypeStruct(dims, F32)


def swap(axis, a, b):
    count = lax.axis_size(axis)

    def pairs(first):
        out = []
        for i in range(first, count - 1, 2):
            out += [(i, i + 1), (i + 1, i)]
        return out

    return lax.ppermute(a, axis, pairs(1)), lax.ppermute(b, axis, pairs(0))


YROWS = 3 * NT * YRUN + 8
ZROWS = 3 * NT * ZRUN
YROWS5 = 4 * NT * YRUN + NT * NZ + 8
ZROWS5 = 4 * NT * ZRUN + 40


def call(kernel, name, outs, ins, scratch=(), work=1, out_space=vmem, more=(), aliases=None):
    return pl.pallas_call(
        kernel,
        out_shape=tuple(outs),
        in_specs=[anywhere() if kind == "a" else vmem() for kind in ins],
        out_specs=tuple(out_space() for _ in outs),
        scratch_shapes=[pltpu.VMEM(dims, F32) for dims in scratch] + list(more),
        compiler_params=params(),
        input_output_aliases=aliases or {},
        cost_estimate=pl.CostEstimate(flops=work * 1000000, bytes_accessed=work * 1000000, transcendentals=0),
        name=name,
    )


def body(displacement, velocity, load, blend, classes, pd_table, fem_table):
    whole = shape(3, NZ, NY, NT * LANES)
    tiles = shape(3, NZ, NT, 8, LANES)
    ext_shape = shape(3, NZ, NT, 16, LANES)
    one = shape(NZ, NT, 8, LANES)
    block = (3, NZ, NY, NT * LANES)
    inputs = [
        pltpu.with_memory_space_constraint(x, pltpu.MemorySpace.HBM)
        for x in (displacement, blend, classes, pd_table, fem_table)
    ]
    u, hm, fem, a, b = pl.pallas_call(
        first_kernel,
        out_shape=(whole, one, one, shape(YROWS5, LANES), shape(YROWS5, LANES)),
        in_specs=[pl.BlockSpec(memory_space=pltpu.MemorySpace.HBM)] * 5,
        out_specs=(vmem(),) * 5,
        scratch_shapes=[
            pltpu.VMEM(block[1:], F32),
            pltpu.VMEM(block[1:], jnp.int32),
            pltpu.SMEM((NCLASS,), F32),
            pltpu.SMEM((NCLASS,), F32),
            pltpu.SemaphoreType.DMA((7,)),
        ],
        compiler_params=params(),
        name="moduli",
    )(*inputs)
    v = velocity
    extm = mra = mrb = None
    for step in range(STEPS):
        last = step == STEPS - 1
        ra, rb = swap("tile", a, b)
        f, p, q = call(
            flat_kernel, f"flat_{step}", (tiles, tiles, tiles), "vvv", [(4, 2 * H + 1, NZ, 8, LANES)], 4
        )(u, hm, fem)
        if step == 0:
            outs = (ext_shape, shape(2, NZ, NT, 16, LANES), shape(ZROWS5, LANES), shape(ZROWS5, LANES))
            ext, extm, a, b = call(functools.partial(spread_kernel, 5), "spread_0", outs, "avvvvv")(f, u, hm, fem, ra, rb)
        else:
            outs = (ext_shape, shape(ZROWS, LANES), shape(ZROWS, LANES))
            ext, a, b = call(functools.partial(spread_kernel, 3), f"spread_{step}", outs, "avvv")(f, u, ra, rb)
        ra, rb = swap("seg", a, b)
        if step == 0:
            mra, mrb = ra, rb
        flat_rows = lambda x: x.reshape(-1, LANES)
        rows_shape = shape(3 * NZ * NT * 8, LANES)
        f, p, q = call(
            tilted_kernel,
            f"tilted_{step}",
            (tiles, rows_shape, rows_shape),
            "v" * 7,
            [(4, 5, NZ, 16, LANES)],
            16,
            aliases={4: 0, 5: 1, 6: 2},
        )(ext, extm, flat_rows(ext), flat_rows(extm), f, flat_rows(p), flat_rows(q))
        p, q = p.reshape(tiles.shape), q.reshape(tiles.shape)
        outs = [whole, whole]
        if not last:
            outs += [shape(YROWS, LANES)] * 2
        scratch = [
            (4, 2 * H, NT, 16, LANES),
            (NT, 16, LANES),
            (4, 5, 2 * H, 16, LANES),
            (3, 2 * H, NT, 8, LANES),
            (3, 2, NT, 8, LANES),
            (3, 2, NT, 8, LANES),
        ]
        more = ()
        if last:
            scratch += [block, block]
            more = (pltpu.SemaphoreType.DMA((2, NT)),)
        space = anywhere if last else vmem
        got = call(functools.partial(last_kernel, last), f"finish_{step}", outs, "v" * 12, scratch, 4, space, more)(
            u, v, load, ext, extm, ra, rb, mra, mrb, f, p, q
        )
        u, v = got[:2]
        if not last:
            a, b = got[2:]
    return u, v


def solution(mesh):
    cells = P(None, "seg", "tile", None)
    plane = P("seg", "tile", None)
    return jax.shard_map(
        body,
        mesh=mesh,
        in_specs=(cells, cells, cells, plane, plane, P(), P()),
        out_specs=(cells, cells),
        check_vma=False,
    )
```

```python
import functools
import math

import jax
import jax.numpy as jnp
from jax import lax
from jax.experimental import pallas as pl
from jax.experimental.pallas import tpu as pltpu
from jax.sharding import PartitionSpec as P

H = 3
STEPS = 2
NCLASS = 4
NZ = 8
NY = 8
NT = 4
LANES = 128
F32 = jnp.float32

YRUN = NZ * H
ZRUN = 32
FRUN = 9
UNROLL = 2
FLAT_CHUNK = 8
TILTED_CHUNK = 4
UNROLL3 = 2


def offsets():
    out = []
    for dz in range(-H, H + 1):
        for dy in range(-H, H + 1):
            for dx in range(-H, H + 1):
                n = dz * dz + dy * dy + dx * dx
                if 0 < n <= H * H:
                    out.append((dz, dy, dx, n))
    return out


OFFSETS = offsets()
FLAT = {dz: [o for o in OFFSETS if o[0] == dz and o[1] == 0] for dz in range(-H, H + 1)}
TILTED = {dz: [o for o in OFFSETS if o[0] == dz and o[1] != 0] for dz in range(-H, H + 1)}


FLAGS = pltpu.SMEM((NT,), jnp.int32)


def vmem():
    return pl.BlockSpec(memory_space=pltpu.VMEM)


def anywhere():
    return pl.BlockSpec(memory_space=pl.ANY)


def params():
    return pltpu.CompilerParams(
        vmem_limit_bytes=24 * 1024 * 1024,
    )


def lanes(tile):
    return pl.ds(tile * LANES, LANES)


def even_mask(axis):
    return jnp.full((8, LANES), lax.axis_index(axis) % 2, jnp.int32) == 0


def pack_y(fields, even, a_ref, b_ref):
    for tile in range(NT):
        for index, load in enumerate(fields):
            base = (tile * len(fields) + index) * YRUN
            for z in range(NZ):
                rows = load(z, tile)
                up = pltpu.roll(rows, H, 0)
                a_ref[pl.ds(base + z * H, 8), :] = jnp.where(even, up, rows)
                b_ref[pl.ds(base + z * H, 8), :] = jnp.where(even, rows, up)


def first_kernel(u_hbm, blend_hbm, cls_hbm, pdt_hbm, femt_hbm, u_ref, hm_ref, fem_ref, a_ref, b_ref, blend_ref, cls_ref, pdt_ref, femt_ref, sem):
    copies = [pltpu.make_async_copy(blend_hbm, blend_ref, sem.at[3]), pltpu.make_async_copy(cls_hbm, cls_ref, sem.at[4])]
    copies += [pltpu.make_async_copy(pdt_hbm, pdt_ref, sem.at[5]), pltpu.make_async_copy(femt_hbm, femt_ref, sem.at[6])]
    moves = [pltpu.make_async_copy(u_hbm.at[c], u_ref.at[c], sem.at[c]) for c in range(3)]
    for copy in copies + moves:
        copy.start()
    for copy in copies:
        copy.wait()
    even = even_mask("tile")
    for z in range(NZ):
        for tile in range(NT):
            blend = blend_ref[z, :, lanes(tile)]
            cls = cls_ref[z, :, lanes(tile)]
            pd = jnp.zeros_like(blend)
            fem = jnp.zeros_like(blend)
            for index in range(NCLASS):
                hit = cls == index
                pd = jnp.where(hit, pdt_ref[index], pd)
                fem = jnp.where(hit, femt_ref[index], fem)
            hm_ref[z, tile] = 0.5 * (pd * blend)
            fem_ref[z, tile] = fem * (1.0 - blend)
    for copy in moves:
        copy.wait()
    loaders = [lambda z, t, c=c: u_ref[c, z, :, lanes(t)] for c in range(3)]
    loaders.append(lambda z, t: hm_ref[z, t])
    pack_y(loaders, even, a_ref, b_ref)
    for tile in range(NT):
        base = 4 * NT * YRUN + tile * NZ
        for z in range(NZ):
            up = pltpu.roll(fem_ref[z, tile], 1, 0)
            a_ref[pl.ds(base + z, 8), :] = up
            b_ref[pl.ds(base + z, 8), :] = up


def spread_kernel(nfields, after_ref, *refs):
    if nfields == 5:
        u_ref, hm_ref, fem_ref, ra_ref, rb_ref, ext_ref, extm_ref, a_ref, b_ref = refs
    else:
        u_ref, ra_ref, rb_ref, ext_ref, a_ref, b_ref = refs
    sub = lax.broadcasted_iota(jnp.int32, (8, LANES), 0)
    even = even_mask("tile")
    even_z = even_mask("seg")
    nrun = min(nfields, 4)
    for index in range(nrun):
        for tile in range(NT):
            base = (tile * nrun + index) * YRUN
            for z in range(NZ):
                rows = u_ref[index, z, :, lanes(tile)] if index < 3 else hm_ref[z, tile]
                turned = pltpu.roll(rows, H, 0)
                got_a = ra_ref[pl.ds(base + z * H, 8), :]
                got_b = rb_ref[pl.ds(base + z * H, 8), :]
                lo = jnp.where(even, got_b, got_a)
                hi = pltpu.roll(jnp.where(even, got_a, got_b), H, 0)
                dst = ext_ref.at[index, z, tile] if index < 3 else extm_ref.at[0, z, tile]
                dst[pl.ds(0, 8), :] = jnp.where(sub < H, lo, turned)
                dst[pl.ds(8, 8), :] = jnp.where(sub < H, turned, hi)
    if nfields == 5:
        for tile in range(NT):
            base = 4 * NT * YRUN + tile * NZ
            for z in range(NZ):
                turned = pltpu.roll(fem_ref[z, tile], H, 0)
                lo = jnp.where(even, rb_ref[pl.ds(base + z, 8), :], ra_ref[pl.ds(base + z, 8), :])
                lo = pltpu.roll(lo, H - 1, 0)
                extm_ref[1, z, tile, pl.ds(0, 8), :] = jnp.where(sub < H, lo, turned)
                extm_ref[1, z, tile, pl.ds(8, 8), :] = turned

    def put(row, up, down):
        a_ref[pl.ds(row, 8), :] = jnp.where(even_z, up, down)
        b_ref[pl.ds(row, 8), :] = jnp.where(even_z, down, up)

    for index in range(nrun):
        for tile in range(NT):
            base = (index * NT + tile) * ZRUN
            src = (lambda z: ext_ref.at[index, z, tile]) if index < 3 else (lambda z: extm_ref.at[0, z, tile])
            put(base, src(5)[pl.ds(3, 8), :], src(2)[pl.ds(3, 8), :])
            for place, zu, zd in ((8, 6, 1), (20, 7, 0)):
                put(base + place, src(zu)[pl.ds(1, 8), :], src(zd)[pl.ds(1, 8), :])
                put(base + place + 4, src(zu)[pl.ds(5, 8), :], src(zd)[pl.ds(5, 8), :])
    if nfields == 5:
        for tile in range(NT):
            base = 4 * NT * ZRUN + tile * FRUN
            for row in (0, 1):
                up = extm_ref[1, NZ - 1, tile, pl.ds(2 + row, 8), :]
                put(base + row, up, up)


def unpack_z(dst, even_z, ra_ref, rb_ref, run):
    base = run * ZRUN

    def get(z_lo, z_hi, row, place):
        got_a = ra_ref[pl.ds(base + place, 8), :]
        got_b = rb_ref[pl.ds(base + place, 8), :]
        dst(z_lo)[pl.ds(row, 8), :] = jnp.where(even_z, got_b, got_a)
        dst(z_hi)[pl.ds(row, 8), :] = jnp.where(even_z, got_a, got_b)

    get(0, 13, 3, 0)
    for place, z_lo, z_hi in ((8, 1, 12), (20, 2, 11)):
        get(z_lo, z_hi, 1, place)
        get(z_lo, z_hi, 5, place + 4)


def x_modes(here, after, edge):
    nxt = pltpu.roll(jnp.where(edge, after, here), LANES - 1, 1)
    return here + nxt, nxt - here


def y_modes(low, high):
    return (low[0] + high[0], low[1] + high[1], high[0] - low[0], high[1] - low[1])


def fem_layers(modes_of, e_of, close, first_layer, layers, emit):
    def finish(c, z, low, high):
        parts = []
        for which in range(len(low or high)):
            if low is None:
                parts.append(high[which])
            elif high is None:
                parts.append(low[which])
            else:
                parts.append([low[which][m] + high[which][m] for m in range(4)])
        x_s, x_d = close(parts)
        emit(c, z, x_s - x_d, x_s + x_d)

    for c in range(3):
        before = None
        carried = None
        for z in range(first_layer, first_layer + layers + 1):
            now = modes_of(c, z)
            if before is not None:
                lower, upper = [], []
                for which in range(len(now)):
                    e = e_of(z - 1, which)
                    e1, e2, e3 = e * (1.0 / 16.0), e * (1.0 / 24.0), e * (1.0 / 48.0)
                    lo, hi = before[which], now[which]
                    d_ss = e1 * (hi[0] - lo[0])
                    s_dx, d_dx = e1 * (lo[1] + hi[1]), e2 * (hi[1] - lo[1])
                    s_dy, d_dy = e1 * (lo[2] + hi[2]), e2 * (hi[2] - lo[2])
                    s_dd, d_dd = e2 * (lo[3] + hi[3]), e3 * (hi[3] - lo[3])
                    lower.append((-d_ss, s_dx - d_dx, s_dy - d_dy, s_dd - d_dd))
                    upper.append((d_ss, s_dx + d_dx, s_dy + d_dy, s_dd + d_dd))
                if z - 1 >= 0:
                    finish(c, z - 1, carried, lower)
                carried = upper
            before = now
        last = first_layer + layers
        if last < NZ:
            finish(c, last, carried, None)


def roll_out(dst, field, lane, left, here, right, reach_x=H):
    bake = field == 2
    dst(0)[...] = here
    for d in range(1, reach_x + 1):
        up = pltpu.roll(jnp.where(lane < d, right, here), LANES - d, 1)
        down = pltpu.roll(jnp.where(lane >= LANES - d, left, here), d, 1)
        dst(d)[...] = up + float(d) if bake else up
        dst(-d)[...] = down - float(d) if bake else down


def reach(lane, left, here, right):
    edge = jnp.maximum(jnp.where(lane >= LANES - H, left, 0.0), jnp.where(lane < H, right, 0.0))
    return jnp.maximum(here, edge)


def bond_sum(moved, center, hm, dz, bonds, acc):
    base = {0: center[0] - dz, 2: center[2]}
    mids = {}
    for _, dy, dx, norm in bonds:
        if dy not in mids:
            mids[dy] = center[1] - float(dy) if dy else center[1]
        rel = [moved(0, dy, dx) - base[0], moved(1, dy, dx) - mids[dy], moved(2, dy, dx) - base[2]]
        m = hm + moved(3, dy, dx)
        square = rel[0] * rel[0] + rel[1] * rel[1] + rel[2] * rel[2]
        factor = m * (1.0 / math.sqrt(norm) - lax.rsqrt(square))
        for c in range(3):
            acc[c] = acc[c] + factor * rel[c]
    return acc


def inside(center_of, moved_of, f_ref, tile, bonds, chunk):
    def run(step, size, first, dz, span):
        for k in range(span):
            z = first + k
            center, hm = center_of(z)
            acc = [f_ref[c, z, tile] for c in range(3)]
            acc = bond_sum(lambda f, dy, dx: moved_of(f, dy, dx, z + step), center, hm, dz, bonds[size], acc)
            for c in range(3):
                f_ref[c, z, tile] = acc[c]

    def level(part, carry):
        run(0, 0, part * chunk, 0.0, chunk)
        return carry

    lax.fori_loop(0, NZ // chunk, level, 0)
    for size in range(1, H + 1):
        if not bonds[size]:
            continue

        def both(side, carry, size=size):
            step = size - 2 * size * side
            run(step, size, size * side, step.astype(F32), NZ - size)
            return carry

        lax.fori_loop(0, 2, both, 0)


def set_flags(flags, lane, most):
    zero = jnp.zeros((8, LANES), F32)
    for tile in range(NT):
        left = most[tile - 1] if tile else zero
        right = most[tile + 1] if tile < NT - 1 else zero
        flags[tile] = (jnp.max(reach(lane, left, most[tile], right)) > 0.0).astype(jnp.int32)


def largest(parts):
    most = parts[0]
    for part in parts[1:]:
        most = jnp.maximum(most, part)
    return most


def neighbours(load, tile):
    here = load(tile)
    left = jnp.where(tile > 0, load(jnp.maximum(tile - 1, 0)), 0.0)
    right = jnp.where(tile < NT - 1, load(jnp.minimum(tile + 1, NT - 1)), 0.0)
    return left, here, right


def columns(tile):
    return pl.ds(pl.multiple_of(tile * LANES, LANES), LANES)


def flat_kernel(u_ref, hm_ref, fem_ref, f_ref, p_ref, q_ref, sr, flags):
    lane = lax.broadcasted_iota(jnp.int32, (8, LANES), 1)
    sub = lax.broadcasted_iota(jnp.int32, (8, LANES), 0)
    zero = jnp.zeros((8, LANES), F32)

    def field(f, z):
        if f < 3:
            return lambda t: u_ref[f, z, :, columns(t)]
        return lambda t: hm_ref[z, t]

    set_flags(flags, lane, [largest([hm_ref[z, t] for z in range(NZ)]) for t in range(NT)])

    def per_tile(tile, carry):
        after = jnp.minimum(tile + 1, NT - 1)
        more = tile < NT - 1

        def modes_of(c, z):
            low = x_modes(u_ref[c, z, :, columns(tile)], jnp.where(more, u_ref[c, z, :, columns(after)], 0.0), lane < 1)
            high = [pltpu.roll(part, 7, 0) for part in low]
            return [y_modes(low, high)]

        def e_of(z, which):
            return jnp.where(sub < 7, fem_ref[z, tile], 0.0)

        def close(parts):
            (a,) = parts
            return (a[0] - a[2]) + pltpu.roll(a[0] + a[2], 1, 0), (a[1] - a[3]) + pltpu.roll(a[1] + a[3], 1, 0)

        def emit(c, z, p, q):
            p_ref[c, z, tile] = p
            q_ref[c, z, tile] = q

        fem_layers(modes_of, e_of, close, 0, NZ - 1, emit)

        for z in range(NZ):
            for c in range(3):
                f_ref[c, z, tile] = zero

        @pl.when(flags[tile] > 0)
        def _():
            def build(z, c2):
                for f in range(4):
                    roll_out(lambda d: sr.at[f, H + d, z], f, lane, *neighbours(field(f, z), tile))
                return c2

            lax.fori_loop(0, NZ, build, 0, unroll=UNROLL)
            inside(
                lambda z: ([sr[c, H, z] for c in range(3)], sr[3, H, z]),
                lambda f, dy, dx, z: sr[f, H + dx, z],
                f_ref,
                tile,
                FLAT,
                FLAT_CHUNK,
            )

        return carry

    lax.fori_loop(0, NT, per_tile, 0)


def faces(ext_rows, extm_rows, p_rows, q_rows, lane, sub):
    ending = (lane == LANES - 1) & (sub % NT == NT - 1)

    def rows(ref, item, z, row):
        return ref[pl.ds((item * NZ + z) * NT * 16 + row, 8, stride=16), :]

    def pair(ref, item, z, row):
        if z < NZ - 1:
            return rows(ref, item, z, row)
        return pltpu.roll(rows(ref, item, z - 1, row), 4, 0)

    def packed_x_modes(here):
        nxt = pltpu.roll(jnp.where(lane < 1, pltpu.roll(here, 7, 0), here), LANES - 1, 1)
        nxt = jnp.where(ending, 0.0, nxt)
        return here + nxt, nxt - here

    for near, far, row_e, y in ((3, 2, 2, 0), (10, 11, 10, NY - 1)):
        for c in range(3):
            for z in range(0, NZ, 2):
                lo, hi = [
                    y_modes(packed_x_modes(pair(ext_rows, c, n, far)), packed_x_modes(pair(ext_rows, c, n, near)))
                    for n in (z, z + 1)
                ]
                e = rows(extm_rows, 1, z, row_e)
                if z == NZ - 2:
                    e = jnp.where(sub < 4, e, 0.0)
                e1, e2, e3 = e * (1.0 / 16.0), e * (1.0 / 24.0), e * (1.0 / 48.0)
                d_ss = e1 * (hi[0] - lo[0])
                s_dx, d_dx = e1 * (lo[1] + hi[1]), e2 * (hi[1] - lo[1])
                s_dy, d_dy = e1 * (lo[2] + hi[2]), e2 * (hi[2] - lo[2])
                s_dd, d_dd = e2 * (lo[3] + hi[3]), e3 * (hi[3] - lo[3])
                low = ((s_dy - d_dy) - d_ss, (s_dx - d_dx) + (s_dd - d_dd))
                high = ((s_dy + d_dy) + d_ss, (s_dx + d_dx) + (s_dd + d_dd))
                if z == NZ - 2:
                    high = [pltpu.roll(part, 4, 0) for part in high]
                    low = [low[k] + high[k] for k in range(2)]
                    todo = ((z, low),)
                else:
                    todo = ((z, low), (z + 1, high))
                for n, (x_s, x_d) in todo:
                    where = pl.ds((c * NZ + n) * NT * 8 + y, 8, stride=8)
                    p_rows[where, :] = p_rows[where, :] + (x_s - x_d)
                    q_rows[where, :] = q_rows[where, :] + (x_s + x_d)


def tilted_kernel(ext_ref, extm_ref, ext_rows, extm_rows, fin_ref, pin_rows, qin_rows, f_ref, p_rows, q_rows, sr, flags):
    lane = lax.broadcasted_iota(jnp.int32, (8, LANES), 1)
    sub = lax.broadcasted_iota(jnp.int32, (8, LANES), 0)
    zero = jnp.zeros((8, LANES), F32)

    def field(f, z, row):
        if f < 3:
            return lambda t: ext_ref[f, z, t, pl.ds(row, 8), :]
        return lambda t: extm_ref[0, z, t, pl.ds(row, 8), :]

    most = [largest([field(3, z, row)(t) for z in range(NZ) for row in (0, 6)]) for t in range(NT)]
    set_flags(flags, lane, most)
    faces(ext_rows, extm_rows, p_rows, q_rows, lane, sub)

    def per_tile(tile, carry):
        @pl.when(flags[tile] > 0)
        def _():
            def build(z, c2):
                for f in range(4):
                    for half in (0, 8):
                        got = neighbours(field(f, z, half), tile)
                        roll_out(lambda d: sr.at[f, 2 + d, z, pl.ds(half, 8)], f, lane, *got, reach_x=2)
                return c2

            lax.fori_loop(0, NZ, build, 0, unroll=UNROLL)
            inside(
                lambda z: ([sr[c, 2, z, pl.ds(H, 8), :] for c in range(3)], sr[3, 2, z, pl.ds(H, 8), :]),
                lambda f, dy, dx, z: sr[f, 2 + dx, z, pl.ds(H + dy, 8), :],
                f_ref,
                tile,
                TILTED,
                TILTED_CHUNK,
            )

        return carry

    lax.fori_loop(0, NT, per_tile, 0)


def last_kernel(last, u_ref, v_ref, load_ref, ext_ref, extm_ref, ura_ref, urb_ref, mra_ref, mrb_ref, f_ref, p_ref, q_ref, *refs):
    if last:
        u_hbm, v_hbm, sz, fe, sr, fx, px, qx, nu_ref, nv_ref, flags, sem = refs
    else:
        nu_ref, nv_ref, a_ref, b_ref, sz, fe, sr, fx, px, qx, flags = refs
    even = even_mask("tile")
    even_z = even_mask("seg")
    lane = lax.broadcasted_iota(jnp.int32, (8, LANES), 1)
    zero = jnp.zeros((8, LANES), F32)
    spot = {0: 0, 1: 1, 2: 2, 11: 3, 12: 4, 13: 5}
    for tile in range(NT):
        for z in range(2 * H):
            for half in (0, 8):
                sz[3, z, tile, pl.ds(half, 8), :] = zero
        for f in range(4):
            ra, rb = (ura_ref, urb_ref) if f < 3 else (mra_ref, mrb_ref)
            unpack_z(lambda z: sz.at[f, spot[z], tile], even_z, ra, rb, f * NT + tile)
        base = 4 * NT * ZRUN + tile * FRUN
        for row in (0, 1):
            fe[tile, pl.ds(2 + row, 8), :] = jnp.where(
                even_z, mrb_ref[pl.ds(base + row, 8), :], mra_ref[pl.ds(base + row, 8), :]
            )

    most = []
    for tile in range(NT):
        parts = [sz[3, z, tile, pl.ds(row, 8), :] for z in range(2 * H) for row in (0, 6)]
        parts += [extm_ref[0, z, tile, pl.ds(H, 8), :] for z in (0, 1, 2, 5, 6, 7)]
        most.append(largest(parts))
    set_flags(flags, lane, most)

    def out_copies(tile):
        out = []
        for index, (src, dst) in enumerate(((nu_ref, u_hbm), (nv_ref, v_hbm))):
            view = (slice(None), slice(None), slice(None), columns(tile))
            out.append(pltpu.make_async_copy(src.at[view], dst.at[view], sem.at[index, tile]))
        return out

    def per_tile(tile, carry):
        after = jnp.minimum(tile + 1, NT - 1)
        more = tile < NT - 1

        def load(c, z, row, side):
            t = tile if side == 0 else after
            if z < 0:
                got = sz[c, H + z, t, pl.ds(row, 8), :]
            elif z >= NZ:
                got = sz[c, z - NZ + H, t, pl.ds(row, 8), :]
            else:
                got = ext_ref[c, z, t, pl.ds(row, 8), :]
            return got if side == 0 else jnp.where(more, got, 0.0)

        def modes_of(c, z):
            level = [x_modes(load(c, z, row, 0), load(c, z, row, 1), lane < 1) for row in (2, 3, 4)]
            return [y_modes(level[1], level[2]), y_modes(level[0], level[1])]

        def close(parts):
            a, b = parts
            return (a[0] - a[2]) + (b[0] + b[2]), (a[1] - a[3]) + (b[1] + b[3])

        def emit(c, z, p, q):
            px[c, 0 if z == 0 else 1, tile] = p
            qx[c, 0 if z == 0 else 1, tile] = q

        def e_low(z, which):
            return fe[tile, pl.ds(H - which, 8), :]

        def e_high(z, which):
            return extm_ref[1, NZ - 1, tile, pl.ds(H - which, 8), :]

        fem_layers(modes_of, e_low, close, -1, 1, emit)
        fem_layers(modes_of, e_high, close, NZ - 1, 1, emit)

        for z in range(2 * H):
            for c in range(3):
                fx[c, z, tile] = zero

        @pl.when(flags[tile] > 0)
        def _():
            def build(z, c2):
                for f in range(4):
                    for half in (0, 8):
                        got = neighbours(lambda t: sz[f, z, t, pl.ds(half, 8), :], tile)
                        roll_out(lambda d: sr.at[f, 2 + d, z, pl.ds(half, 8)], f, lane, *got, reach_x=2)
                return c2

            for f in range(4):
                for z in (0, 2 * H - 1):
                    sr[f, 2, z, pl.ds(H, 8), :] = sz[f, z, tile, pl.ds(H, 8), :]
            lax.fori_loop(1, 2 * H - 1, build, 0, unroll=UNROLL)

            def side_loop(side, c2):
                sign = 2 * side - 1
                for k in range(H):
                    z = k + side * (NZ - 1 - 2 * k)
                    center = [ext_ref[c, z, tile, pl.ds(H, 8), :] for c in range(3)]
                    hm = extm_ref[0, z, tile, pl.ds(H, 8), :]
                    acc = [zero] * 3
                    for size in range(k + 1, H + 1):
                        place = (H - (size - k)) + side * (2 * (size - k) - 1)
                        acc = bond_sum(
                            lambda f, dy, dx: sr[f, 2 + dx, place, pl.ds(H + dy, 8), :],
                            center,
                            hm,
                            (sign * size).astype(F32),
                            FLAT[size] + TILTED[size],
                            acc,
                        )
                    for c in range(3):
                        fx[c, k + side * (2 * H - 1 - 2 * k), tile] = acc[c]
                return c2

            lax.fori_loop(0, 2, side_loop, 0)

        before = jnp.maximum(tile - 1, 0)
        for c in range(3):
            for z in range(NZ):
                p, q, f = p_ref[c, z, tile], q_ref[c, z, tile], f_ref[c, z, tile]
                shifted = q_ref[c, z, before]
                if z in (0, NZ - 1):
                    p = p + px[c, 0 if z == 0 else 1, tile]
                    q = q + qx[c, 0 if z == 0 else 1, tile]
                    shifted = shifted + qx[c, 0 if z == 0 else 1, before]
                if z < H or z >= NZ - H:
                    f = f + fx[c, z if z < H else z - 2, tile]
                shifted = jnp.where(tile > 0, shifted, 0.0)
                moved = pltpu.roll(jnp.where(lane == LANES - 1, shifted, q), 1, 1)
                force = f - (p + moved)
                where = (c, z, slice(None), columns(tile))
                v = v_ref[where] + 0.25 * (force + load_ref[where])
                u = u_ref[where] + 0.01 * v
                nv_ref[where] = v
                nu_ref[where] = u
                if not last:
                    row = (tile * 3 + c) * YRUN + z * H
                    up = pltpu.roll(u, H, 0)
                    a_ref[pl.ds(row, 8), :] = jnp.where(even, up, u)
                    b_ref[pl.ds(row, 8), :] = jnp.where(even, u, up)
        if last:
            for copy in out_copies(tile):
                copy.start()
        return carry

    lax.fori_loop(0, NT, per_tile, 0)
    if last:
        for tile in range(NT):
            for copy in out_copies(tile):
                copy.wait()


def shape(*dims):
    return jax.ShapeDtypeStruct(dims, F32)


def swap(axis, a, b):
    count = lax.axis_size(axis)

    def pairs(first):
        out = []
        for i in range(first, count - 1, 2):
            out += [(i, i + 1), (i + 1, i)]
        return out

    got_b = lax.ppermute(b, axis, pairs(1))
    return lax.ppermute(a, axis, pairs(0)), got_b


YROWS = 3 * NT * YRUN + 8
ZROWS = 3 * NT * ZRUN
YROWS5 = 4 * NT * YRUN + NT * NZ + 8
ZROWS5 = 4 * NT * ZRUN + 40


def call(kernel, name, outs, ins, scratch=(), work=1, out_space=vmem, more=(), aliases=None):
    return pl.pallas_call(
        kernel,
        out_shape=tuple(outs),
        in_specs=[anywhere() if kind == "a" else vmem() for kind in ins],
        out_specs=tuple(out_space() for _ in outs),
        scratch_shapes=[pltpu.VMEM(dims, F32) for dims in scratch] + list(more),
        compiler_params=params(),
        input_output_aliases=aliases or {},
        cost_estimate=pl.CostEstimate(flops=work * 1000000, bytes_accessed=work * 1000000, transcendentals=0),
        name=name,
    )


def body(displacement, velocity, load, blend, classes, pd_table, fem_table):
    whole = shape(3, NZ, NY, NT * LANES)
    tiles = shape(3, NZ, NT, 8, LANES)
    ext_shape = shape(3, NZ, NT, 16, LANES)
    one = shape(NZ, NT, 8, LANES)
    block = (3, NZ, NY, NT * LANES)
    inputs = [
        pltpu.with_memory_space_constraint(x, pltpu.MemorySpace.HBM)
        for x in (displacement, blend, classes, pd_table, fem_table)
    ]
    u, hm, fem, a, b = pl.pallas_call(
        first_kernel,
        out_shape=(whole, one, one, shape(YROWS5, LANES), shape(YROWS5, LANES)),
        in_specs=[pl.BlockSpec(memory_space=pltpu.MemorySpace.HBM)] * 5,
        out_specs=(vmem(),) * 5,
        scratch_shapes=[
            pltpu.VMEM(block[1:], F32),
            pltpu.VMEM(block[1:], jnp.int32),
            pltpu.SMEM((NCLASS,), F32),
            pltpu.SMEM((NCLASS,), F32),
            pltpu.SemaphoreType.DMA((7,)),
        ],
        compiler_params=params(),
        name="moduli",
    )(*inputs)
    v = velocity
    extm = mra = mrb = None
    for step in range(STEPS):
        last = step == STEPS - 1
        ra, rb = swap("tile", a, b)
        f, p, q = call(
            flat_kernel, f"flat_{step}", (tiles, tiles, tiles), "vvv", [(4, 2 * H + 1, NZ, 8, LANES)], 4, more=(FLAGS,)
        )(u, hm, fem)
        if step == 0:
            outs = (ext_shape, shape(2, NZ, NT, 16, LANES), shape(ZROWS5, LANES), shape(ZROWS5, LANES))
            ext, extm, a, b = call(functools.partial(spread_kernel, 5), "spread_0", outs, "avvvvv")(f, u, hm, fem, ra, rb)
        else:
            outs = (ext_shape, shape(ZROWS, LANES), shape(ZROWS, LANES))
            ext, a, b = call(functools.partial(spread_kernel, 3), f"spread_{step}", outs, "avvv")(f, u, ra, rb)
        ra, rb = swap("seg", a, b)
        if step == 0:
            mra, mrb = ra, rb
        flat_rows = lambda x: x.reshape(-1, LANES)
        rows_shape = shape(3 * NZ * NT * 8, LANES)
        f, p, q = call(
            tilted_kernel,
            f"tilted_{step}",
            (tiles, rows_shape, rows_shape),
            "v" * 7,
            [(4, 5, NZ, 16, LANES)],
            16,
            more=(FLAGS,),
            aliases={4: 0, 5: 1, 6: 2},
        )(ext, extm, flat_rows(ext), flat_rows(extm), f, flat_rows(p), flat_rows(q))
        p, q = p.reshape(tiles.shape), q.reshape(tiles.shape)
        outs = [whole, whole]
        if not last:
            outs += [shape(YROWS, LANES)] * 2
        scratch = [
            (4, 2 * H, NT, 16, LANES),
            (NT, 16, LANES),
            (4, 5, 2 * H, 16, LANES),
            (3, 2 * H, NT, 8, LANES),
            (3, 2, NT, 8, LANES),
            (3, 2, NT, 8, LANES),
        ]
        more = (FLAGS,)
        if last:
            scratch += [block, block]
            more += (pltpu.SemaphoreType.DMA((2, NT)),)
        space = anywhere if last else vmem
        got = call(functools.partial(last_kernel, last), f"finish_{step}", outs, "v" * 12, scratch, 4, space, more)(
            u, v, load, ext, extm, ra, rb, mra, mrb, f, p, q
        )
        u, v = got[:2]
        if not last:
            a, b = got[2:]
    return u, v


def solution(mesh):
    cells = P(None, "seg", "tile", None)
    plane = P("seg", "tile", None)
    return jax.shard_map(
        body,
        mesh=mesh,
        in_specs=(cells, cells, cells, plane, plane, P(), P()),
        out_specs=(cells, cells),
        check_vma=False,
    )
```
